32 devices in a mesh: dp: 4 (over y, x), seq: 4 (over z), tensor: 2 (over core).
Axes of the slice: x: 2, y: 2, z: 4, core: 2. Of those that a mesh axis runs over, the one named last changes fastest.
Arguments:
- tokens: bfloat16 [16, 1024, 768], P('dp', 'seq'), may hold values from -6 to 6
- cotangent: bfloat16 [16, 1024, 768], P('dp', 'seq'), may hold values from -6 to 6
- masked_pos: int32 [16, 153], P('dp'), may hold values from 0 to 1023
- rand_blocks: int32 [16, 16, 3], P('dp'), may hold values from 0 to 15, as said below
- ln1_gain: bfloat16 [768], replicated, may hold values from 0.25 to 1.75
- ln1_bias: bfloat16 [768], replicated, may hold values from -1.75 to 1.75
- w_query: bfloat16 [768, 768], P(None, 'tensor'), may hold values from -0.3125 to 0.3125
- b_query: bfloat16 [768], P('tensor'), may hold values from -1.75 to 1.75
- w_key: bfloat16 [768, 768], P(None, 'tensor'), may hold values from -0.3125 to 0.3125
- w_value: bfloat16 [768, 768], P(None, 'tensor'), may hold values from -0.21875 to 0.21875
- b_value: bfloat16 [768], P('tensor'), may hold values from -1.25 to 1.25
- w_out: bfloat16 [768, 768], P('tensor'), may hold values from -0.875 to 0.875
- b_out: bfloat16 [768], replicated, may hold values from -1.75 to 1.75
- ln2_gain: bfloat16 [768], replicated, may hold values from 0.25 to 1.75
- ln2_bias: bfloat16 [768], replicated, may hold values from -1.75 to 1.75
- w_inner: bfloat16 [768, 3072], P(None, 'tensor'), may hold values from -0.21875 to 0.21875
- b_inner: bfloat16 [3072], P('tensor'), may hold values from -3 to 3
- w_outer: bfloat16 [3072, 768], P('tensor'), may hold values from -0.109375 to 0.109375
- b_outer: bfloat16 [768], replicated, may hold values from -1.75 to 1.75
Outputs:
- out: bfloat16 [16, 1024, 768], P('dp', 'seq')
- grad_tokens: bfloat16 [16, 1024, 768], P('dp', 'seq')
- grad_ln1_gain: float32 [768], replicated
- grad_ln1_bias: float32 [768], replicated
- grad_w_query: float32 [768, 768], P(None, 'tensor')
- grad_b_query: float32 [768], P('tensor')
- grad_w_key: float32 [768, 768], P(None, 'tensor')
- grad_w_value: float32 [768, 768], P(None, 'tensor')
- grad_b_value: float32 [768], P('tensor')
- grad_w_out: float32 [768, 768], P('tensor')
- grad_b_out: float32 [768], replicated
- grad_ln2_gain: float32 [768], replicated
- grad_ln2_bias: float32 [768], replicated
- grad_w_inner: float32 [768, 3072], P(None, 'tensor')
- grad_b_inner: float32 [3072], P('tensor')
- grad_w_outer: float32 [3072, 768], P('tensor')
- grad_b_outer: float32 [768], replicated
The draws below stay inside these ranges and needn't reach their ends.
Inputs may be any that keep to these rules, and one draw needn't show every extreme that they name: `rand_blocks`: each window names three distinct random key blocks for each query block. For each aligned group of 2 windows on one index of dp and each device's query blocks j * 4 to (j + 1) * 4 - 1, at most 6 of the named 3 * 2 * 4 blocks lie in any one device's blocks k * 4 to (k + 1) * 4 - 1, and exactly 6 in some. Named blocks may coincide with sliding or global blocks, and different query blocks may name the same block. `masked_pos`: A position may appear more than once.
All inputs are finite; a program needn't handle non-finite values.
Results may differ from the reference program's by a relative error of at most 0.018.
Values may be sent and summed in bfloat16 or wider, within the bound.
No kernel may reach another device: no remote copies, remote signals or barrier semaphores. Data moves between devices by JAX's collectives and lax.ppermute only.
A program may use at most 192 MiB of HBM per device.

```python
import jax
import jax.numpy as jnp
from jax import lax

D = 768
HEADS = 12
HD = 64
FF = 3072
BS = 64
WIN_MB = 2
BLK_DEV = 4
NB = 16
SEQ = 1024
WINDOWS = 16
NMASK = 153
CAP = 6


def draw_rand_blocks(key, part):
    owner_count = NB // BLK_DEV
    group_items = 3 * WIN_MB * BLK_DEV
    list_count = WIN_MB * BLK_DEV
    group_count = WINDOWS // WIN_MB * owner_count
    order_key, local_key = jax.random.split(jax.random.fold_in(key, 7))
    order_keys = jax.random.split(order_key, group_count)
    orders = jax.vmap(lambda single: jax.random.permutation(single, owner_count * CAP))(order_keys)
    owner_ids = (orders[:, :group_items] % owner_count).reshape(group_count, list_count, 3)
    local_ids = jax.random.randint(local_key, (group_count, list_count, 3), 0, BLK_DEV)
    owner_a, owner_b, owner_c = (owner_ids[..., 0], owner_ids[..., 1], owner_ids[..., 2])
    local_a = local_ids[..., 0]
    local_b = local_ids[..., 1]
    clash_b = (owner_b == owner_a) & (local_b == local_a)
    local_b = jnp.where(clash_b, (local_b + 1) % BLK_DEV, local_b)
    local_c = local_ids[..., 2]
    for attempt in range(2):
        clash_c = (owner_c == owner_a) & (local_c == local_a) | (owner_c == owner_b) & (local_c == local_b)
        local_c = jnp.where(clash_c, (local_c + 1) % BLK_DEV, local_c)
    locals_fixed = jnp.stack([local_a, local_b, local_c], axis=-1)
    blocks = owner_ids * BLK_DEV + locals_fixed
    blocks = blocks.reshape(WINDOWS // WIN_MB, owner_count, WIN_MB, BLK_DEV, 3)
    blocks = jnp.transpose(blocks, (0, 2, 1, 3, 4)).reshape(WINDOWS, NB, 3)
    return blocks.astype(jnp.int32)


def set_ends(drawn, rng, smallest, top_value):
    longest = drawn.shape.index(max(drawn.shape))
    spots = []
    for shift in (0, 1):
        where = [jax.random.randint(jax.random.fold_in(rng, axis), (), 0, length) for axis, length in enumerate(drawn.shape)]
        where[longest] = (where[longest] + shift) % drawn.shape[longest]
        spots.append(tuple(where))
    return drawn.at[spots[0]].set(smallest).at[spots[1]].set(top_value)


def shard_levels(rng, extent, shards, low, top_value):
    level = 1.0
    for axis_at, blocks in shards:
        steps = jax.random.uniform(jax.random.fold_in(jax.random.fold_in(rng, 6), axis_at), (blocks,), jnp.float32, low / len(shards), top_value / len(shards))
        level = level * jnp.repeat(jnp.exp(steps), extent[axis_at] // blocks).reshape((-1,) + (1,) * (len(extent) - 1 - axis_at))
    return level


def bell_draw(stream_key, extent, deviation, most, cuts=(), kind=jnp.bfloat16):
    values = deviation * jax.random.normal(stream_key, extent, jnp.float32)
    if cuts:
        values = values * shard_levels(stream_key, extent, cuts, -0.22, 0.18)
    return jnp.clip(values, -most, most).astype(kind)


def setup_inputs(seed: int = 0) -> dict:
    arg_keys = jax.random.split(jax.random.key(seed), 20)
    return {
        "tokens": bell_draw(arg_keys[0], (WINDOWS, SEQ, D), 1.0, 6.0, ((0, 4), (1, 4))),
        "cotangent": bell_draw(arg_keys[1], (WINDOWS, SEQ, D), 1.0, 6.0, ((0, 4), (1, 4))),
        "masked_pos": set_ends(jax.random.randint(arg_keys[2], (WINDOWS, NMASK), 0, SEQ), jax.random.fold_in(arg_keys[2], 1), 0, SEQ - 1).astype(jnp.int32),
        "rand_blocks": draw_rand_blocks(jax.random.fold_in(arg_keys[19], 71), 0),
        "ln1_gain": jnp.clip(1.0 + 0.15 * jax.random.normal(arg_keys[4], (D,), jnp.float32), 0.25, 1.75).astype(jnp.bfloat16),
        "ln1_bias": bell_draw(arg_keys[5], (D,), 0.3, 1.75),
        "w_query": bell_draw(arg_keys[6], (D, D), (D // 2) ** -0.5, 0.3125, ((1, 2),)),
        "b_query": bell_draw(arg_keys[7], (D,), 0.3, 1.75, ((0, 2),)),
        "w_key": bell_draw(arg_keys[8], (D, D), (D // 2) ** -0.5, 0.3125, ((1, 2),)),
        "w_value": bell_draw(arg_keys[9], (D, D), D ** -0.5, 0.21875, ((1, 2),)),
        "b_value": bell_draw(arg_keys[10], (D,), 0.2, 1.25, ((0, 2),)),
        "w_out": bell_draw(arg_keys[11], (D, D), (D // 16) ** -0.5, 0.875, ((0, 2),)),
        "b_out": bell_draw(arg_keys[12], (D,), 0.3, 1.75),
        "ln2_gain": jnp.clip(1.0 + 0.15 * jax.random.normal(arg_keys[13], (D,), jnp.float32), 0.25, 1.75).astype(jnp.bfloat16),
        "ln2_bias": bell_draw(arg_keys[14], (D,), 0.3, 1.75),
        "w_inner": bell_draw(arg_keys[15], (D, FF), D ** -0.5, 0.21875, ((1, 2),)),
        "b_inner": bell_draw(arg_keys[16], (FF,), 0.5, 3.0, ((0, 2),)),
        "w_outer": bell_draw(arg_keys[17], (FF, D), FF ** -0.5, 0.109375, ((0, 2),)),
        "b_outer": bell_draw(arg_keys[18], (D,), 0.3, 1.75),
    }


@jax.custom_vjp
def low(v):
    return lax.optimization_barrier(v.astype(jnp.bfloat16)).astype(jnp.float32)

@jax.custom_vjp
def low_back(v):
    return v

def low_keep(v):
    return (low(v), None)

def low_pass(kept, grad):
    return (grad,)

def back_keep(v):
    return (v, None)

def back_low(kept, grad):
    return (low(grad),)
low.defvjp(low_keep, low_pass)
low_back.defvjp(back_keep, back_low)
eps_norm = 1e-05
highest = lax.Precision.HIGHEST

def norm_rows(values, gain, shift):
    center = values - lax.optimization_barrier(jnp.mean(values, axis=-1, keepdims=True))
    scaled = lax.rsqrt(lax.optimization_barrier(jnp.mean(center * center, axis=-1, keepdims=True)) + eps_norm)
    return center * scaled * gain + shift

def block_lists(rand_window, block_count):
    query_ids = jnp.arange(block_count, dtype=jnp.int32)
    offsets = jnp.arange(3, dtype=jnp.int32) - 1
    sliding = query_ids[:, None] + offsets[None, :]
    slide_ok = (sliding >= 0) & (sliding <= block_count - 1)
    end_ids = jnp.stack([jnp.zeros_like(query_ids), jnp.full_like(query_ids, block_count - 1)], axis=1)
    end_ok = jnp.abs(end_ids - query_ids[:, None]) > 1
    rand_ok = (jnp.abs(rand_window - query_ids[:, None]) > 1) & (rand_window != 0) & (rand_window != block_count - 1)
    index_list = jnp.concatenate([jnp.clip(sliding, 0, block_count - 1), end_ids, rand_window.astype(jnp.int32)], axis=1).astype(jnp.int32)
    present = jnp.concatenate([slide_ok, end_ok, rand_ok], axis=1)
    return (index_list, present)

def attend(query, keyset, values, rand_window):
    block_count = SEQ // BS
    index_list, present = block_lists(rand_window, block_count)
    group_size = min(block_count, 512 // BS)
    group_count = block_count // group_size
    query_groups = query.reshape(group_count, group_size, BS, HEADS, HD)
    key_blocks = keyset.reshape(block_count, BS, HEADS, HD)
    value_blocks = values.reshape(block_count, BS, HEADS, HD)
    index_groups = index_list.reshape(group_count, group_size, 8)
    present_groups = present.reshape(group_count, group_size, 8)

    def one_group(inputs):
        query_part, index_part, present_part = inputs
        key_part = key_blocks[index_part].reshape(group_size, 8 * BS, HEADS, HD)
        value_part = value_blocks[index_part].reshape(group_size, 8 * BS, HEADS, HD)
        scores = jnp.einsum('gqhd,gkhd->ghqk', query_part, key_part, precision=highest) * HD ** (-0.5)
        scores = low_back(scores)
        allowed = jnp.repeat(present_part, BS, axis=1)[:, None, None, :]
        scores = jnp.where(allowed, scores, -1e+30)
        top_score = lax.optimization_barrier(jnp.max(scores, axis=-1, keepdims=True))
        log_total = top_score + jnp.log(lax.optimization_barrier(jnp.sum(jnp.exp(scores - top_score), axis=-1, keepdims=True)))
        weights = low(jnp.exp(scores - log_total))
        return jnp.einsum('ghqk,gkhd->gqhd', weights, value_part, precision=highest)
    mixed = lax.map(jax.checkpoint(one_group), (query_groups, index_groups, present_groups))
    return mixed.reshape(SEQ, D)

def window_forward(tokens_window, rand_window, params):
    ln1_gain, ln1_bias, w_query, b_query, w_key, w_value, b_value, w_out, b_out, ln2_gain, ln2_bias, w_inner, b_inner, w_outer, b_outer = params
    hidden = low(norm_rows(tokens_window, ln1_gain, ln1_bias))
    query = low_back(low(jnp.dot(hidden, w_query, precision=highest) + b_query))
    keyset = low_back(low(jnp.dot(hidden, w_key, precision=highest)))
    values = low_back(low(jnp.dot(hidden, w_value, precision=highest) + b_value))
    mixed = low_back(low(attend(query, keyset, values, rand_window)))
    attn_out = low_back(jnp.dot(mixed, w_out, precision=highest) + b_out)
    middle = tokens_window + attn_out
    hidden_two = low(norm_rows(middle, ln2_gain, ln2_bias))
    inner_pre = low_back(jnp.dot(hidden_two, w_inner, precision=highest) + b_inner)
    active = low(jax.nn.gelu(inner_pre, approximate=False))
    return middle + jnp.dot(active, w_outer, precision=highest) + b_outer

def reference(tokens, cotangent, masked_pos, rand_blocks, ln1_gain, ln1_bias, w_query, b_query, w_key, w_value, b_value, w_out, b_out, ln2_gain, ln2_bias, w_inner, b_inner, w_outer, b_outer):
    params = tuple((member.astype(jnp.float32) for member in (ln1_gain, ln1_bias, w_query, b_query, w_key, w_value, b_value, w_out, b_out, ln2_gain, ln2_bias, w_inner, b_inner, w_outer, b_outer)))
    seq_ids = jnp.arange(SEQ, dtype=jnp.int32)

    def one_window(carry, inputs):
        tokens_window, cot_window, masked_window, rand_window = inputs
        chosen = jnp.any(seq_ids[:, None] == masked_window[None, :], axis=1)
        cot_masked = cot_window.astype(jnp.float32) * chosen[:, None].astype(jnp.float32)
        result, pullback = jax.vjp(lambda xin, pin: window_forward(xin, rand_window, pin), tokens_window.astype(jnp.float32), params)
        grad_input, grad_params = pullback(cot_masked)
        carry = jax.tree.map(jnp.add, carry, grad_params)
        return (carry, (result.astype(jnp.bfloat16), grad_input.astype(jnp.bfloat16)))
    zeros_params = jax.tree.map(jnp.zeros_like, params)
    sums, stacked = lax.scan(one_window, zeros_params, (tokens, cotangent, masked_pos, rand_blocks))
    return (stacked[0], stacked[1], sums[0], sums[1], sums[2], sums[3], sums[4], sums[5], sums[6], sums[7], sums[8], sums[9], sums[10], sums[11], sums[12], sums[13], sums[14])
```

```python
import functools

import jax
import jax.numpy as jnp
from jax import lax
from jax.experimental import pallas as pl
from jax.experimental.pallas import tpu as pltpu
from jax.sharding import PartitionSpec as P

HD = 64
BS = 64
MB = 2
WIN_MB = 2


eps_norm = 1e-05
inv_root_two = 0.7071067811865476
inv_root_two_pi = 0.3989422804014327


LANES = 128
NEG = -1e30
VMEM_LIMIT = 60 * 1024 * 1024


def dot_nn(left, right):
    return lax.dot_general(left, right, (((1,), (0,)), ((), ())), preferred_element_type=jnp.float32)


def dot_nt(left, right):
    return lax.dot_general(left, right, (((1,), (1,)), ((), ())), preferred_element_type=jnp.float32)


def dot_tn(left, right):
    return lax.dot_general(left, right, (((0,), (0,)), ((), ())), preferred_element_type=jnp.float32)


def norm_parts(values):
    center = values - jnp.mean(values, axis=-1, keepdims=True)
    scaled = lax.rsqrt(jnp.mean(center * center, axis=-1, keepdims=True) + eps_norm)
    return center * scaled, scaled


def pick_rows(positions, total):
    ids = lax.broadcasted_iota(jnp.int32, (positions.shape[0], total), 1)
    return jnp.where(ids == positions, 1.0, 0.0).astype(jnp.bfloat16)


def row_lists(blocks, allow):
    ids = lax.broadcasted_iota(jnp.int32, (blocks.shape[0], allow.shape[0]), 1)
    return dot_nn(jnp.where(ids == blocks, 1.0, 0.0).astype(jnp.bfloat16), allow)


def head_half(half):
    lane = lax.broadcasted_iota(jnp.int32, (1, LANES), 1)
    return (lane < HD) if half == 0 else (lane >= HD)


def one_head(slab, half):
    return jnp.where(head_half(half), slab, jnp.zeros_like(slab))


def call(kernel, name, outs, args, flops, scratch=(), smem=0, exps=0):
    moved = sum(a.size * a.dtype.itemsize for a in args) + sum(
        o.size * o.dtype.itemsize for o in outs
    )
    spec = pl.BlockSpec(memory_space=pltpu.VMEM)
    return pl.pallas_call(
        kernel,
        name=name,
        out_shape=outs,
        in_specs=[pl.BlockSpec(memory_space=pltpu.SMEM)] * smem + [spec] * (len(args) - smem),
        out_specs=[spec] * len(outs),
        scratch_shapes=list(scratch),
        compiler_params=pltpu.CompilerParams(vmem_limit_bytes=VMEM_LIMIT),
        cost_estimate=pl.CostEstimate(
            flops=int(flops), bytes_accessed=int(moved), transcendentals=int(exps)
        ),
    )(*args)


def shape(dims, dtype=jnp.bfloat16):
    return jax.ShapeDtypeStruct(dims, dtype)


def front_kernel(
    tok, pos, allow, g1, b1, wq, bq, wk, wv, bv, wo, h, q, k, v, xm, hm, qm, om, lse, part
):
    total = tok.shape[0]
    tile = min(total, 256)
    for start in range(0, total, tile):
        rows = pl.ds(start, tile)
        normed, _ = norm_parts(tok[rows, :].astype(jnp.float32))
        low = (normed * g1[...] + b1[...]).astype(jnp.bfloat16)
        h[rows, :] = low
        q[rows, :] = (dot_nn(low, wq[...]) + bq[...]).astype(jnp.bfloat16)
        k[rows, :] = dot_nn(low, wk[...]).astype(jnp.bfloat16)
        v[rows, :] = (dot_nn(low, wv[...]) + bv[...]).astype(jnp.bfloat16)
    pick = pick_rows(pos[...], total)
    xm[...] = dot_nn(pick, tok[...]).astype(jnp.bfloat16)
    hm[...] = dot_nn(pick, h[...]).astype(jnp.bfloat16)
    qm[...] = dot_nn(pick, q[...]).astype(jnp.bfloat16)
    listed = row_lists(pos[...] >> 6, allow[...]) > 0.5
    lane = lax.broadcasted_iota(jnp.int32, (pos.shape[0], LANES), 1)
    sums = jnp.zeros((pos.shape[0], LANES), jnp.float32)
    for slab in range(q.shape[1] // LANES):
        cols = pl.ds(slab * LANES, LANES)
        query = (qm[:, cols].astype(jnp.float32) * HD ** (-0.5)).astype(jnp.bfloat16)
        mixed = None
        for half in range(2):
            scores = jnp.where(listed, dot_nt(one_head(query, half), k[:, cols]), NEG)
            top = jnp.max(scores, axis=-1, keepdims=True)
            weight = jnp.exp(scores - top)
            total_weight = jnp.sum(weight, axis=-1, keepdims=True)
            sums = jnp.where(lane == 2 * slab + half, top + jnp.log(total_weight), sums)
            found = dot_nn((weight * (1.0 / total_weight)).astype(jnp.bfloat16), v[:, cols])
            mixed = found if half == 0 else jnp.where(head_half(0), mixed, found)
        om[:, cols] = mixed.astype(jnp.bfloat16)
    lse[...] = sums
    part[...] = dot_nn(om[...], wo[...]).astype(jnp.bfloat16)


def gelu_parts(z):
    cdf = 0.5 * (1.0 + lax.erf(z * inv_root_two))
    return z * cdf, cdf + z * (jnp.exp(-0.5 * z * z) * inv_root_two_pi)


def middle_of(xm, part, other, bo):
    both = part[...].astype(jnp.float32) + other[...].astype(jnp.float32)
    return xm[...].astype(jnp.float32) + (both + bo[...])


def hidden_kernel(
    bits, xm, part, other, g, bo, g2, b2, wi, bi, wf,
    dwf_a, dwf_as, dwf_b, dwf_bs, dwi_a, dwi_as, dwi_b, dwi_bs, dh2, dbi, dbf,
    u_all, h2_all, dz_all,
):
    width, hidden = wi.shape
    normed, _ = norm_parts(middle_of(xm, part, other, bo))
    h2_all[...] = (normed * g2[...] + b2[...]).astype(jnp.bfloat16)
    h2 = h2_all[...]
    step = hidden // 3
    for start in range(0, hidden, step):
        cols = pl.ds(start, step)
        z = dot_nn(h2, wi[:, cols]) + bi[:, cols]
        act, slope = gelu_parts(z)
        u_all[:, cols] = act.astype(jnp.bfloat16)
        dz = (dot_nt(g[...], wf[cols, :]) * slope).astype(jnp.bfloat16)
        dz_all[:, cols] = dz
        dbi[:, cols] = jnp.sum(dz.astype(jnp.float32), axis=0, keepdims=True)
    dbf[...] = jnp.sum(g[...].astype(jnp.float32), axis=0, keepdims=True)
    half = hidden // 2
    count = half // 2
    for order, keep, send in ((0, dwf_a, dwf_as), (1, dwf_b, dwf_bs)):
        for out, bit in ((keep, bits[order]), (send, 1 - bits[order])):
            at = pl.multiple_of(order * half + bit * count, LANES)
            out[...] = dot_tn(u_all[:, pl.ds(at, count)], g[...]).astype(jnp.bfloat16)
    count = width // 2
    for order, keep, send in ((0, dwi_a, dwi_as), (1, dwi_b, dwi_bs)):
        for out, bit in ((keep, bits[order]), (send, 1 - bits[order])):
            at = pl.multiple_of(bit * count, LANES)
            out[...] = dot_tn(
                h2_all[:, pl.ds(at, count)], dz_all[:, pl.ds(order * half, half)]
            ).astype(jnp.bfloat16)
    dh2[...] = dot_nt(dz_all[...], wi[...]).astype(jnp.bfloat16)


def attend_back_kernel(
    bits, xm, part, other, g, dh2, dh2_other, bo, g2, wo, pos, allow, qm, om, hm, lse, h, k, v,
    da_a, da_as, da_b, da_bs, dx1, dq, dk, dv, dg2, db2, dbo, dbq, dbv, da_all, do_all,
):
    width = g.shape[1]
    normed, scaled = norm_parts(middle_of(xm, part, other, bo))
    up = dh2[...].astype(jnp.float32) + dh2_other[...].astype(jnp.float32)
    dg2[...] = jnp.sum(up * normed, axis=0, keepdims=True)
    db2[...] = jnp.sum(up, axis=0, keepdims=True)
    weighted = up * g2[...]
    centered = weighted - jnp.mean(weighted, axis=-1, keepdims=True)
    slope = jnp.mean(weighted * normed, axis=-1, keepdims=True)
    grad = g[...].astype(jnp.float32) + scaled * (centered - normed * slope)
    dx1[...] = grad
    low = grad.astype(jnp.bfloat16)
    da_all[...] = low
    dbo[...] = jnp.sum(low.astype(jnp.float32), axis=0, keepdims=True)
    do_all[...] = dot_nt(low, wo[...]).astype(jnp.bfloat16)
    listed = row_lists(pos[...] >> 6, allow[...]) > 0.5
    for slab in range(qm.shape[1] // LANES):
        cols = pl.ds(slab * LANES, LANES)
        query = (qm[:, cols].astype(jnp.float32) * HD ** (-0.5)).astype(jnp.bfloat16)
        grad_q, grad_k, grad_v = None, None, None
        for half in range(2):
            at = 2 * slab + half
            own = one_head(query, half)
            own_do = one_head(do_all[:, cols], half)
            scores = jnp.where(listed, dot_nt(own, k[:, cols]), NEG)
            prob = jnp.exp(scores - lse[:, at : at + 1])
            grad_p = dot_nt(own_do, v[:, cols])
            delta = jnp.sum(prob * grad_p, axis=-1, keepdims=True)
            ds = (prob * (grad_p - delta)).astype(jnp.bfloat16)
            found_q = dot_nn(ds, k[:, cols])
            found_k = dot_tn(ds, own)
            found_v = dot_tn(prob.astype(jnp.bfloat16), own_do)
            grad_q = found_q if half == 0 else jnp.where(head_half(0), grad_q, found_q)
            grad_k = found_k if half == 0 else grad_k + found_k
            grad_v = found_v if half == 0 else grad_v + found_v
        dq[:, cols] = (grad_q * HD ** (-0.5)).astype(jnp.bfloat16)
        dk[:, cols] = grad_k.astype(jnp.bfloat16)
        dv[:, cols] = grad_v.astype(jnp.bfloat16)
    dbq[...] = jnp.sum(dq[...].astype(jnp.float32), axis=0, keepdims=True)
    dbv[...] = jnp.sum(dv[...].astype(jnp.float32), axis=0, keepdims=True)
    local = qm.shape[1]
    count = width // 2
    for keep, bit in ((da_a, bits[0]), (da_as, 1 - bits[0])):
        cols = pl.ds(pl.multiple_of(bit * count, LANES), count)
        keep[:, :local] = dot_tn(hm[:, cols], dq[...]).astype(jnp.bfloat16)
        keep[:, local:] = dot_tn(h[:, cols], dk[...]).astype(jnp.bfloat16)
    for keep, bit in ((da_b, bits[1]), (da_bs, 1 - bits[1])):
        cols = pl.ds(pl.multiple_of(bit * count, LANES), count)
        keep[:, :local] = dot_tn(h[:, cols], dv[...]).astype(jnp.bfloat16)
        keep[:, local:] = dot_tn(om[...], da_all[:, cols]).astype(jnp.bfloat16)


def input_kernel(bits, pos, dq, dk, dv, wq, wk, wv, keep, send, dq_all):
    total = dk.shape[0]
    dq_all[...] = dot_tn(pick_rows(pos[...], total), dq[...]).astype(jnp.bfloat16)
    run = BS * 2
    for at in range(0, total // (2 * run)):
        for out, bit in ((keep, bits[2]), (send, 1 - bits[2])):
            rows = pl.ds(pl.multiple_of(at * 2 * run + bit * run, run), run)
            out[pl.ds(at * run, run), :] = (
                dot_nt(dq_all[rows, :], wq[...])
                + dot_nt(dk[rows, :], wk[...])
                + dot_nt(dv[rows, :], wv[...])
            ).astype(jnp.bfloat16)


def first_norm_kernel(pos_half, tok, own, other, dx1, g1, grad, dg1, db1):
    count = tok.shape[0]
    normed, scaled = norm_parts(tok[...].astype(jnp.float32))
    up = own[...].astype(jnp.float32) + other[...].astype(jnp.float32)
    dg1[...] = jnp.sum(up * normed, axis=0, keepdims=True)
    db1[...] = jnp.sum(up, axis=0, keepdims=True)
    weighted = up * g1[...]
    centered = weighted - jnp.mean(weighted, axis=-1, keepdims=True)
    slope = jnp.mean(weighted * normed, axis=-1, keepdims=True)
    pick = pick_rows(pos_half[...], count)
    high = dx1[...].astype(jnp.bfloat16)
    rest = (dx1[...] - high.astype(jnp.float32)).astype(jnp.bfloat16)
    through = dot_tn(pick, high) + dot_tn(pick, rest)
    grad[...] = (through + scaled * (centered - normed * slope)).astype(jnp.bfloat16)


def attend_kernel(q, k, v, allow, wo, part, mixed_all):
    tile = q.shape[0]
    first = pl.program_id(0) * (tile // BS)
    ids = lax.broadcasted_iota(jnp.int32, (tile, 1), 0)
    listed = row_lists(first + (ids >> 6), allow[...]) > 0.5
    for slab in range(q.shape[1] // LANES):
        cols = pl.ds(slab * LANES, LANES)
        query = (q[:, cols].astype(jnp.float32) * HD ** (-0.5)).astype(jnp.bfloat16)
        mixed = None
        for half in range(2):
            scores = jnp.where(listed, dot_nt(one_head(query, half), k[:, cols]), NEG)
            top = jnp.max(scores, axis=-1, keepdims=True)
            weight = jnp.exp(scores - top)
            total_weight = jnp.sum(weight, axis=-1, keepdims=True)
            found = dot_nn((weight * (1.0 / total_weight)).astype(jnp.bfloat16), v[:, cols])
            mixed = found if half == 0 else jnp.where(head_half(0), mixed, found)
        mixed_all[:, cols] = mixed.astype(jnp.bfloat16)
    part[...] = dot_nn(mixed_all[...], wo[...]).astype(jnp.bfloat16)


def feed_kernel(tok, part, other, bo, g2, b2, wi, bi, wf, out):
    normed, _ = norm_parts(middle_of(tok, part, other, bo))
    h2 = (normed * g2[...] + b2[...]).astype(jnp.bfloat16)
    hidden = wi.shape[1]
    step = hidden // 3
    total = None
    for start in range(0, hidden, step):
        cols = pl.ds(start, step)
        z = dot_nn(h2, wi[:, cols]) + bi[:, cols]
        act = z * (0.5 * (1.0 + lax.erf(z * inv_root_two)))
        found = dot_nn(act.astype(jnp.bfloat16), wf[cols, :])
        total = found if total is None else total + found
    out[...] = total.astype(jnp.bfloat16)


def tiled_call(kernel, name, tiles, rows, split, args, outs, flops, scratch=(), exps=0):
    moved = sum(a.size * a.dtype.itemsize for a in args)
    in_specs = [
        pl.BlockSpec((rows, a.shape[1]), lambda i: (i, 0))
        if cut
        else pl.BlockSpec(a.shape, lambda i: (0, 0))
        for a, cut in zip(args, split)
    ]
    return pl.pallas_call(
        kernel,
        name=name,
        grid=(tiles,),
        out_shape=outs,
        in_specs=in_specs,
        out_specs=pl.BlockSpec((rows, outs.shape[1]), lambda i: (i, 0)),
        scratch_shapes=list(scratch),
        compiler_params=pltpu.CompilerParams(vmem_limit_bytes=VMEM_LIMIT),
        cost_estimate=pl.CostEstimate(
            flops=int(flops), bytes_accessed=int(moved), transcendentals=int(exps)
        ),
    )(*args)


def flip(value, axis, bit):
    return lax.ppermute(value, axis, [(i, i ^ bit) for i in range(lax.axis_size(axis))])


def bit_of(axis, bit):
    return jnp.where((lax.axis_index(axis) & bit) != 0, 1, 0).astype(jnp.int32)


def halves(value, bit):
    count = value.shape[0] // 2
    keep = lax.dynamic_slice_in_dim(value, bit * count, count, 0)
    send = lax.dynamic_slice_in_dim(value, (1 - bit) * count, count, 0)
    return keep, send


def joined(own, other, bit):
    return jnp.where(
        bit == 0, jnp.concatenate([own, other], axis=0), jnp.concatenate([other, own], axis=0)
    )


def add_low(left, right):
    return (left.astype(jnp.float32) + right.astype(jnp.float32)).astype(jnp.bfloat16)


def stages_of(order):
    dp_bits = [("dp", 1 << i) for i in range(lax.axis_size("dp").bit_length() - 1)]
    seq_bits = [("seq", 1 << i) for i in range(lax.axis_size("seq").bit_length() - 1)]
    return (dp_bits if order == 0 else dp_bits[::-1]) + seq_bits


def sum_over_devices(keep, send, order):
    steps = stages_of(order)
    for at, (axis, bit) in enumerate(steps):
        total = add_low(keep, flip(send, axis, bit))
        if at + 1 < len(steps):
            keep, send = halves(total, bit_of(*steps[at + 1]))
    for axis, bit in steps[::-1]:
        total = joined(total, flip(total, axis, bit), bit_of(axis, bit))
    return total.astype(jnp.float32)


def sum_small(value):
    for axis, bit in stages_of(0):
        value = value + flip(value, axis, bit)
    return value


def to_windows(rows):
    return lax.all_to_all(rows, "seq", split_axis=0, concat_axis=0, tiled=True)


def window_body(
    tokens, cotangent, masked_pos, rand_blocks, ln1_gain, ln1_bias, w_query, b_query, w_key,
    w_value, b_value, w_out, b_out, ln2_gain, ln2_bias, w_inner, b_inner, w_outer, b_outer,
):
    windows, rows, width = tokens.shape
    local = w_query.shape[1]
    hidden = w_inner.shape[1]
    total = windows * rows
    blocks = total // BS
    wide = hidden // 2
    place = lax.axis_index("seq")
    core = lax.axis_index("tensor")
    bits = jnp.stack([bit_of(*stages_of(0)[0]), bit_of(*stages_of(1)[0]), core.astype(jnp.int32), 0])

    def line(vector):
        return vector.astype(jnp.float32)[None, :]

    run = rows // 2
    cut = tokens.reshape(windows, 2, run, width)
    own_rows = to_windows(lax.dynamic_index_in_dim(cut, core, 1, keepdims=False))
    other_rows = flip(own_rows, "tensor", 1)
    pair = jnp.where(
        core == 0,
        jnp.stack([own_rows, other_rows], axis=1),
        jnp.stack([other_rows, own_rows], axis=1),
    )
    tok = pair.reshape(total, width)
    tok_half = own_rows.reshape(total // 2, width)

    named = masked_pos.shape[1]
    count = -(-named // 16) * 16
    spots = jnp.concatenate(
        [masked_pos, jnp.full((windows, count - named), -1, jnp.int32)], axis=1
    )
    slot = jnp.arange(count, dtype=jnp.int32)
    again = jnp.any(
        (spots[:, :, None] == spots[:, None, :]) & (slot[None, :] < slot[:, None])[None], axis=2
    )
    spots = jnp.where(again, -1, spots)
    pos = lax.dynamic_index_in_dim(spots, place, 0, keepdims=True).reshape(count, 1)

    here = spots - place * rows
    pick = (here[:, :, None] == jnp.arange(rows, dtype=jnp.int32)[None, None, :]).astype(
        jnp.bfloat16
    )
    cot_cut = lax.dynamic_slice_in_dim(cotangent, core * (width // 2), width // 2, 2)
    found = jnp.einsum("wmr,wrd->wmd", pick, cot_cut, preferred_element_type=jnp.float32)
    found, tok_half = lax.optimization_barrier((found.astype(jnp.bfloat16), tok_half))
    g_half = jnp.sum(to_windows(found).astype(jnp.float32), axis=0).astype(jnp.bfloat16)
    g_other = flip(g_half, "tensor", 1)
    g = jnp.where(
        core == 0,
        jnp.concatenate([g_half, g_other], axis=1),
        jnp.concatenate([g_other, g_half], axis=1),
    )

    rand = lax.dynamic_index_in_dim(rand_blocks, place, 0, keepdims=False)
    ids = jnp.arange(blocks, dtype=jnp.int32)
    listed = (
        (jnp.abs(ids[:, None] - ids[None, :]) <= 1)
        | (ids == 0)[None, :]
        | (ids == blocks - 1)[None, :]
        | jnp.any(rand[:, :, None] == ids[None, None, :], axis=1)
    )
    allow = jnp.repeat(listed.astype(jnp.bfloat16), BS, axis=1)

    bo, g1, b1, g2, b2 = (line(x) for x in (b_out, ln1_gain, ln1_bias, ln2_gain, ln2_bias))
    bq, bv, bi = (line(x) for x in (b_query, b_value, b_inner))
    square = 2 * total * width * local
    pairs = count * total * local * 2
    h, q, k, v, xm, hm, qm, om, lse, part = call(
        front_kernel,
        "front",
        [shape((total, width))]
        + [shape((total, local))] * 3
        + [shape((count, width))] * 2
        + [shape((count, local))] * 2
        + [shape((count, LANES), jnp.float32), shape((count, width))],
        (tok, pos, allow, g1, b1, w_query, bq, w_key, w_value, bv, w_out),
        3 * square + 4 * pairs,
        exps=count * total * local // HD,
    )
    other = flip(part, "tensor", 1)
    low_piece = [shape((wide // 2, width))] * 4 + [shape((width // 2, wide))] * 4
    outs = call(
        hidden_kernel,
        "hidden",
        low_piece
        + [
            shape((count, width)),
            shape((1, hidden), jnp.float32),
            shape((1, width), jnp.float32),
        ],
        (bits, xm, part, other, g, bo, g2, b2, w_inner, bi, w_outer),
        10 * count * width * hidden,
        scratch=[
            pltpu.VMEM((count, hidden), jnp.bfloat16),
            pltpu.VMEM((count, width), jnp.bfloat16),
            pltpu.VMEM((count, hidden), jnp.bfloat16),
        ],
        smem=1,
    )
    dwf_a, dwf_as, dwf_b, dwf_bs, dwi_a, dwi_as, dwi_b, dwi_bs, dh2, dbi, dbf = outs
    grad_wf = [sum_over_devices(dwf_a, dwf_as, 0), sum_over_devices(dwf_b, dwf_bs, 1)]
    grad_wi = [sum_over_devices(dwi_a, dwi_as, 0), sum_over_devices(dwi_b, dwi_bs, 1)]
    dh2_other = flip(dh2, "tensor", 1)
    one = shape((1, width), jnp.float32)
    few = shape((1, local), jnp.float32)
    outs = call(
        attend_back_kernel,
        "attend_back",
        [shape((width // 2, 2 * local))] * 2
        + [shape((width // 2, local + width // 2))] * 2
        + [shape((count, width), jnp.float32), shape((count, local))]
        + [shape((total, local))] * 2
        + [one, one, one, few, few],
        (bits, xm, part, other, g, dh2, dh2_other, bo, g2, w_out, pos, allow)
        + (qm, om, hm, lse, h, k, v),
        2 * square + 8 * pairs,
        scratch=[
            pltpu.VMEM((count, width), jnp.bfloat16),
            pltpu.VMEM((count, local), jnp.bfloat16),
        ],
        smem=1,
        exps=count * total * local // HD,
    )
    da_a, da_as, da_b, da_bs, dx1, dq, dk, dv, dg2, db2, dbo, dbq, dbv = outs
    grad_qk = sum_over_devices(da_a, da_as, 0)
    grad_vo = sum_over_devices(da_b, da_bs, 1)

    dh_own, dh_send = call(
        input_kernel,
        "input_grad",
        [shape((total // 2, width))] * 2,
        (bits, pos, dq, dk, dv, w_query, w_key, w_value),
        3 * square,
        scratch=[pltpu.VMEM((total, local), jnp.bfloat16)],
        smem=1,
    )
    dh_other = flip(dh_send, "tensor", 1)
    shard, inside = pos // rows, pos % rows
    mine = (pos >= 0) & (inside // run == core)
    pos_half = jnp.where(mine, shard * run + inside % run, -1)
    grad_half, dg1, db1 = call(
        first_norm_kernel,
        "first_norm",
        [shape((total // 2, width)), one, one],
        (pos_half, tok_half, dh_own, dh_other, dx1, g1),
        4 * count * total * width,
    )

    def to_shards(half):
        back = to_windows(half.reshape(windows, run, width))
        over = flip(back, "tensor", 1)
        both = jnp.where(
            core == 0, jnp.stack([back, over], axis=1), jnp.stack([over, back], axis=1)
        )
        return both.reshape(windows, rows, width)

    grad_tokens = to_shards(grad_half)

    tile = min(total, 256)
    tiles = total // tile
    part_all = tiled_call(
        attend_kernel,
        "attend",
        tiles,
        tile,
        (True, False, False, False, False),
        (q, k, v, allow, w_out),
        shape((total, width)),
        square + 4 * total * total * local,
        scratch=[pltpu.VMEM((tile, local), jnp.bfloat16)],
        exps=total * total * local // HD,
    )
    other_all = flip(part_all, "tensor", 1)
    feed_all = tiled_call(
        feed_kernel,
        "feed",
        tiles,
        tile,
        (True, True, True) + (False,) * 6,
        (tok, part_all, other_all, bo, g2, b2, w_inner, bi, w_outer),
        shape((total, width)),
        4 * total * width * hidden,
        exps=total * hidden,
    )

    def by_core(value):
        value = value.reshape(windows, 2, run, width)
        own = lax.dynamic_index_in_dim(value, core, 1, keepdims=False)
        sent = lax.dynamic_index_in_dim(value, 1 - core, 1, keepdims=False)
        return own, sent

    feed_own, feed_send = by_core(feed_all)
    feed_other = flip(feed_send, "tensor", 1)
    base = own_rows.astype(jnp.float32) + (
        by_core(part_all)[0].astype(jnp.float32)
        + by_core(other_all)[0].astype(jnp.float32)
        + b_out.astype(jnp.float32)
    )
    out_half = base + (
        feed_own.astype(jnp.float32) + feed_other.astype(jnp.float32) + b_outer.astype(jnp.float32)
    )
    out = to_shards(out_half.astype(jnp.bfloat16).reshape(total // 2, width))

    first = jnp.concatenate([dg1, db1], axis=0)
    first = first + flip(first, "tensor", 1)
    small = jnp.concatenate(
        [jnp.concatenate([x.reshape(-1) for x in (first, dg2, db2, dbo, dbf, dbi, dbq, dbv)])]
    )
    pad = -small.shape[0] % (8 * LANES)
    small = jnp.concatenate([small, jnp.zeros((pad,), jnp.float32)]).reshape(-1, LANES)
    small = sum_small(small).reshape(-1)
    cursor = 0
    smalls = []
    for extent in (width, width, width, width, width, width, hidden, local, local):
        smalls.append(small[cursor : cursor + extent])
        cursor += extent
    s_g1, s_b1, s_g2, s_b2, s_bo, s_bf, s_bi, s_bq, s_bv = smalls
    vo = grad_vo[:, local:]
    return (
        out,
        grad_tokens,
        s_g1,
        s_b1,
        grad_qk[:, :local],
        s_bq,
        grad_qk[:, local:],
        grad_vo[:, :local],
        s_bv,
        jnp.concatenate([vo[: width // 2], vo[width // 2 :]], axis=1),
        s_bo,
        s_g2,
        s_b2,
        jnp.concatenate(grad_wi, axis=1),
        s_bi,
        jnp.concatenate(grad_wf, axis=0),
        s_bf,
    )


def with_halo(block, sides, width):
    for axis, dim in sides:
        count = lax.axis_size(axis)
        forward = [(i, i + 1) for i in range(count - 1)]
        backward = [(target, source) for source, target in forward]
        low = lax.ppermute(
            lax.slice_in_dim(block, block.shape[dim] - width, None, axis=dim), axis, forward
        )
        high = lax.ppermute(lax.slice_in_dim(block, 0, width, axis=dim), axis, backward)
        block = jnp.concatenate([low, block, high], axis=dim)
    return block


def broadcast(value, axis, root):
    mine = lax.axis_index(axis) == root
    return lax.psum(jnp.where(mine, value, jnp.zeros_like(value)), axis)


def norm_forward(values, gain, shift):
    center = values - jnp.mean(values, axis=-1, keepdims=True)
    scaled = lax.rsqrt(jnp.mean(center * center, axis=-1, keepdims=True) + eps_norm)
    normed = center * scaled
    return (normed * gain + shift, normed, scaled)


def norm_backward(upstream, gain, normed, scaled):
    weighted = upstream * gain
    centered = weighted - jnp.mean(weighted, axis=-1, keepdims=True)
    return scaled * (centered - normed * jnp.mean(weighted * normed, axis=-1, keepdims=True))


def row_dot(left, right):
    return lax.dot_general(
        left, right, (((left.ndim - 1,), (0,)), ((), ())), preferred_element_type=jnp.float32
    )


def back_dot(left, right):
    return lax.dot_general(
        left, right, (((left.ndim - 1,), (1,)), ((), ())), preferred_element_type=jnp.float32
    )


def outer_sum(left, right):
    return lax.dot_general(
        left, right, (((0, 1), (0, 1)), ((), ())), preferred_element_type=jnp.float32
    )


def column_sum(values):
    return jnp.sum(values, axis=(0, 1), dtype=jnp.float32)


def list_masks(rand_local, first_block, block_count):
    window_count, local_count = (rand_local.shape[0], rand_local.shape[1])
    query_ids = first_block + jnp.arange(local_count, dtype=jnp.int32)
    slide_ok = jnp.stack(
        [query_ids - 1 >= 0, query_ids >= 0, query_ids + 1 <= block_count - 1], axis=1
    )
    end_ok = jnp.stack([jnp.abs(query_ids) > 1, jnp.abs(block_count - 1 - query_ids) > 1], axis=1)
    rand_ok = (
        (jnp.abs(rand_local - query_ids[None, :, None]) > 1)
        & (rand_local != 0)
        & (rand_local != block_count - 1)
    )
    fixed_ok = jnp.broadcast_to(
        jnp.concatenate([slide_ok, end_ok], axis=1)[None], (window_count, local_count, 5)
    )
    return jnp.concatenate([fixed_ok, rand_ok], axis=-1)


def build_routing(rand_batch, position, devices, local_count, capacity):
    window_count = rand_batch.shape[0]
    item_count = window_count * local_count * 3

    def arrange(grid_values):
        grid_values = grid_values.reshape(window_count, devices, local_count, 3)
        return jnp.transpose(grid_values, (1, 0, 2, 3)).reshape(devices, item_count)

    window_grid = jnp.broadcast_to(
        jnp.arange(window_count, dtype=jnp.int32)[:, None, None], rand_batch.shape
    )
    owner_table = arrange(rand_batch // local_count)
    source_table = arrange(window_grid * local_count + rand_batch % local_count)
    device_ids = jnp.arange(devices, dtype=jnp.int32)
    matches = (owner_table[:, :, None] == device_ids[None, None, :]).astype(jnp.int32)
    earlier = jnp.cumsum(matches, axis=1) - matches
    slot_table = jnp.sum(earlier * matches, axis=2)
    owned_here = (owner_table == position).astype(jnp.int32)
    slot_ids = jnp.arange(capacity, dtype=jnp.int32)
    slot_matches = (slot_table[:, :, None] == slot_ids[None, None, :]).astype(
        jnp.int32
    ) * owned_here[:, :, None]
    send_rows = jnp.sum(slot_matches * source_table[:, :, None], axis=1).reshape(devices * capacity)
    send_live = jnp.sum(slot_matches, axis=1).reshape(devices * capacity)
    my_owner = lax.dynamic_index_in_dim(owner_table, position, 0, keepdims=False)
    my_slot = lax.dynamic_index_in_dim(slot_table, position, 0, keepdims=False)
    take_rows = my_owner * capacity + my_slot
    return (send_rows, send_live, take_rows)


def fetch_blocks(packed, routing, block_rows):
    window_count, local_rows, kv_width = packed.shape
    local_count = local_rows // block_rows
    devices = lax.axis_size("seq")
    padded = with_halo(packed, (("seq", 1),), block_rows)
    padded = padded.reshape(window_count, local_count + 2, block_rows, kv_width)
    sliding = jnp.stack([padded[:, offset : offset + local_count] for offset in range(3)], axis=2)
    first_part = broadcast(packed[:, :block_rows], "seq", 0)
    last_part = broadcast(packed[:, local_rows - block_rows :], "seq", devices - 1)
    end_blocks = jnp.stack([first_part, last_part], axis=1)
    end_blocks = jnp.broadcast_to(
        end_blocks[:, None], (window_count, local_count, 2, block_rows, kv_width)
    )
    send_rows, send_live, take_rows = routing
    sources = packed.reshape(window_count * local_count, block_rows, kv_width)
    outgoing = jnp.take(sources, send_rows, axis=0).reshape(devices, -1, block_rows, kv_width)
    incoming = lax.all_to_all(outgoing, "seq", split_axis=0, concat_axis=0, tiled=True).reshape(
        -1, block_rows, kv_width
    )
    fetched = jnp.take(incoming, take_rows, axis=0).reshape(
        window_count, local_count, 3, block_rows, kv_width
    )
    return jnp.concatenate([sliding, end_blocks, fetched], axis=2)


def return_blocks(kv_grads, routing, block_rows):
    window_count, local_count = (kv_grads.shape[0], kv_grads.shape[1])
    kv_width = kv_grads.shape[-1]
    local_rows = local_count * block_rows
    devices = lax.axis_size("seq")
    position = lax.axis_index("seq")
    padded_grad = jnp.zeros((window_count, local_count + 2, block_rows, kv_width), jnp.float32)
    for offset in range(3):
        padded_grad = padded_grad.at[:, offset : offset + local_count].add(kv_grads[:, :, offset])
    rim_rows = jnp.concatenate([padded_grad[:, 0], padded_grad[:, local_count + 1]], axis=1)
    rim_back = with_halo(rim_rows.astype(jnp.bfloat16), (("seq", 1),), block_rows).astype(
        rim_rows.dtype
    )
    end_grads = lax.psum(jnp.sum(kv_grads[:, :, 3:5], axis=1).astype(jnp.bfloat16), "seq").astype(
        jnp.float32
    )
    zeros_block = jnp.zeros((window_count, block_rows, kv_width), jnp.float32)
    first_add = rim_back[:, :block_rows] + jnp.where(position == 0, end_grads[:, 0], zeros_block)
    last_add = rim_back[:, 3 * block_rows :] + jnp.where(
        position == devices - 1, end_grads[:, 1], zeros_block
    )
    send_rows, send_live, take_rows = routing
    rand_items = kv_grads[:, :, 5:8].reshape(-1, block_rows, kv_width)
    capacity_rows = send_rows.shape[0]
    outgoing = (
        jnp.zeros((capacity_rows, block_rows, kv_width), jnp.float32).at[take_rows].set(rand_items)
    )
    incoming = lax.all_to_all(
        outgoing.reshape(devices, -1, block_rows, kv_width).astype(jnp.bfloat16),
        "seq",
        split_axis=0,
        concat_axis=0,
        tiled=True,
    ).astype(jnp.float32)
    incoming = (
        incoming.reshape(capacity_rows, block_rows, kv_width)
        * send_live.astype(jnp.float32)[:, None, None]
    )
    from_owners = (
        jnp.zeros((window_count * local_count, block_rows, kv_width), jnp.float32)
        .at[send_rows]
        .add(incoming)
    )
    summed = padded_grad[:, 1 : local_count + 1].reshape(window_count, local_rows, kv_width)
    summed = summed + from_owners.reshape(window_count, local_rows, kv_width)
    summed = summed.at[:, :block_rows].add(first_add)
    summed = summed.at[:, local_rows - block_rows :].add(last_add)
    return summed


def split_scores(query_low, keyset, key_valid):
    window_count, local_rows, local_width = query_low.shape
    local_count = keyset.shape[1]
    head_count = local_width // HD
    key_rows = keyset.shape[2] * BS
    query_split = query_low.reshape(window_count, local_count, BS, head_count, HD)
    paired = keyset.reshape(window_count, local_count, key_rows, 2, head_count, HD)
    key_part = paired[:, :, :, 0]
    value_part = paired[:, :, :, 1]
    scores = jnp.einsum(
        "wbqhd,wbkhd->wbhqk", query_split, key_part, preferred_element_type=jnp.float32
    ) * HD ** (-0.5)
    allowed = jnp.repeat(key_valid, BS, axis=2)[:, :, None, None, :]
    scores = jnp.where(allowed, scores, -1e30)
    return (scores, query_split, key_part, value_part)


def attend_forward(query_low, keyset, key_valid):
    scores, query_split, key_part, value_part = split_scores(query_low, keyset, key_valid)
    top_score = jnp.max(scores, axis=-1, keepdims=True)
    log_total = top_score + jnp.log(jnp.sum(jnp.exp(scores - top_score), axis=-1, keepdims=True))
    weights = jnp.exp(scores - log_total).astype(jnp.bfloat16)
    mixed = jnp.einsum(
        "wbhqk,wbkhd->wbqhd", weights, value_part, preferred_element_type=jnp.float32
    )
    return (mixed.reshape(query_low.shape).astype(jnp.bfloat16), log_total)


def attend_backward(query_low, keyset, key_valid, log_total, grad_mixed):
    scores, query_split, key_part, value_part = split_scores(query_low, keyset, key_valid)
    window_count, local_count = (keyset.shape[0], keyset.shape[1])
    local_width = query_low.shape[2]
    weights = jnp.exp(scores - log_total)
    grad_split = grad_mixed.reshape(query_split.shape)
    grad_weights = jnp.einsum(
        "wbqhd,wbkhd->wbhqk", grad_split, value_part, preferred_element_type=jnp.float32
    )
    delta_sum = jnp.sum(weights * grad_weights, axis=-1, keepdims=True)
    grad_scores = (weights * (grad_weights - delta_sum)).astype(jnp.bfloat16)
    grad_query = jnp.einsum(
        "wbhqk,wbkhd->wbqhd", grad_scores, key_part, preferred_element_type=jnp.float32
    ) * HD ** (-0.5)
    grad_key = jnp.einsum(
        "wbhqk,wbqhd->wbkhd", grad_scores, query_split, preferred_element_type=jnp.float32
    ) * HD ** (-0.5)
    grad_value = jnp.einsum(
        "wbhqk,wbqhd->wbkhd",
        weights.astype(jnp.bfloat16),
        grad_split,
        preferred_element_type=jnp.float32,
    )
    list_shape = (window_count, local_count, keyset.shape[2], BS, local_width)
    kv_grads = jnp.concatenate(
        [grad_key.reshape(list_shape), grad_value.reshape(list_shape)], axis=-1
    )
    return (grad_query.reshape(query_low.shape), kv_grads)


def flatten_all(members):
    return jnp.concatenate([member.reshape(-1) for member in members])


def share_sum(vector):
    return lax.psum_scatter(vector, ("dp", "seq"), scatter_dimension=0, tiled=True)


def spread_body(
    tokens,
    cotangent,
    masked_pos,
    rand_blocks,
    ln1_gain,
    ln1_bias,
    w_query,
    b_query,
    w_key,
    w_value,
    b_value,
    w_out,
    b_out,
    ln2_gain,
    ln2_bias,
    w_inner,
    b_inner,
    w_outer,
    b_outer,
):
    local_rows = tokens.shape[1]
    devices = lax.axis_size("seq")
    position = lax.axis_index("seq")
    block_count = rand_blocks.shape[1]
    local_count = block_count // devices
    capacity = (3 * WIN_MB * local_count + devices - 1) // devices
    gain_one = ln1_gain.astype(jnp.float32)
    bias_one = ln1_bias.astype(jnp.float32)
    gain_two = ln2_gain.astype(jnp.float32)
    bias_two = ln2_bias.astype(jnp.float32)
    row_ids = position * local_rows + jnp.arange(local_rows, dtype=jnp.int32)
    first_block = position * local_count
    outputs = []
    input_grads = []
    totals = None
    for batch_index in range(MB):
        batch_start = batch_index * WIN_MB
        batch_stop = batch_start + WIN_MB
        tokens_now = tokens[batch_start:batch_stop].astype(jnp.float32)
        rand_now = rand_blocks[batch_start:batch_stop]
        routing = build_routing(rand_now, position, devices, local_count, capacity)
        rand_local = lax.dynamic_slice_in_dim(rand_now, first_block, local_count, 1)
        key_valid = list_masks(rand_local, first_block, block_count)
        hidden_one, normed_one, scaled_one = norm_forward(tokens_now, gain_one, bias_one)
        hidden_low = hidden_one.astype(jnp.bfloat16)
        query_low = (row_dot(hidden_low, w_query) + b_query.astype(jnp.float32)).astype(
            jnp.bfloat16
        )
        key_low = row_dot(hidden_low, w_key).astype(jnp.bfloat16)
        value_low = (row_dot(hidden_low, w_value) + b_value.astype(jnp.float32)).astype(
            jnp.bfloat16
        )
        packed = jnp.concatenate([key_low, value_low], axis=2)
        keyset = fetch_blocks(packed, routing, BS)
        mixed_low, log_total = attend_forward(query_low, keyset, key_valid)
        attn_out = lax.psum(row_dot(mixed_low, w_out).astype(jnp.bfloat16), "tensor").astype(
            jnp.float32
        ) + b_out.astype(jnp.float32)
        middle = tokens_now + attn_out
        hidden_two, normed_two, scaled_two = norm_forward(middle, gain_two, bias_two)
        hidden_two_low = hidden_two.astype(jnp.bfloat16)
        inner_pre = row_dot(hidden_two_low, w_inner) + b_inner.astype(jnp.float32)
        active = jax.nn.gelu(inner_pre, approximate=False).astype(jnp.bfloat16)
        ffn_out = lax.psum(row_dot(active, w_outer).astype(jnp.bfloat16), "tensor").astype(
            jnp.float32
        ) + b_outer.astype(jnp.float32)
        outputs.append((middle + ffn_out).astype(jnp.bfloat16))
        masked_now = masked_pos[batch_start:batch_stop]
        chosen = jnp.any(row_ids[None, :, None] == masked_now[:, None, :], axis=2)
        cot_now = cotangent[batch_start:batch_stop]
        grad_top = jnp.where(chosen[:, :, None], cot_now, jnp.zeros_like(cot_now))
        grad_active = back_dot(grad_top, w_outer)
        normal_cdf = 0.5 * (1.0 + lax.erf(inner_pre * inv_root_two))
        density = jnp.exp(-0.5 * inner_pre * inner_pre) * inv_root_two_pi
        grad_inner = (grad_active * (normal_cdf + inner_pre * density)).astype(jnp.bfloat16)
        grad_hidden_two = lax.psum(
            back_dot(grad_inner, w_inner).astype(jnp.bfloat16), "tensor"
        ).astype(jnp.float32)
        grad_middle = grad_top.astype(jnp.float32) + norm_backward(
            grad_hidden_two, gain_two, normed_two, scaled_two
        )
        grad_attn = grad_middle.astype(jnp.bfloat16)
        grad_mixed = back_dot(grad_attn, w_out).astype(jnp.bfloat16)
        keyset_back = fetch_blocks(packed, routing, BS)
        grad_query, kv_grads = attend_backward(
            query_low, keyset_back, key_valid, log_total, grad_mixed
        )
        grad_query = grad_query.astype(jnp.bfloat16)
        grad_packed = return_blocks(kv_grads, routing, BS)
        local_width = query_low.shape[2]
        grad_key = grad_packed[:, :, :local_width].astype(jnp.bfloat16)
        grad_value = grad_packed[:, :, local_width:].astype(jnp.bfloat16)
        grad_partial = (
            back_dot(grad_query, w_query)
            + back_dot(grad_key, w_key)
            + back_dot(grad_value, w_value)
        )
        grad_hidden_one = lax.psum(grad_partial.astype(jnp.bfloat16), "tensor").astype(jnp.float32)
        grad_tokens_now = grad_middle + norm_backward(
            grad_hidden_one, gain_one, normed_one, scaled_one
        )
        input_grads.append(grad_tokens_now.astype(jnp.bfloat16))
        batch_grads = (
            jnp.sum(grad_hidden_one * normed_one, axis=(0, 1)),
            jnp.sum(grad_hidden_one, axis=(0, 1)),
            outer_sum(hidden_low, grad_query),
            column_sum(grad_query),
            outer_sum(hidden_low, grad_key),
            outer_sum(hidden_low, grad_value),
            column_sum(grad_value),
            outer_sum(mixed_low, grad_attn),
            column_sum(grad_attn),
            jnp.sum(grad_hidden_two * normed_two, axis=(0, 1)),
            jnp.sum(grad_hidden_two, axis=(0, 1)),
            outer_sum(hidden_two_low, grad_inner),
            column_sum(grad_inner),
            outer_sum(active, grad_top),
            column_sum(grad_top),
        )
        totals = batch_grads if totals is None else jax.tree.map(jnp.add, totals, batch_grads)
    final_share = share_sum(flatten_all(totals))
    gathered = lax.all_gather(
        final_share.astype(jnp.bfloat16), ("dp", "seq"), axis=0, tiled=True
    ).astype(final_share.dtype)
    param_shapes = [
        member.shape
        for member in (
            ln1_gain,
            ln1_bias,
            w_query,
            b_query,
            w_key,
            w_value,
            b_value,
            w_out,
            b_out,
            ln2_gain,
            ln2_bias,
            w_inner,
            b_inner,
            w_outer,
            b_outer,
        )
    ]
    results = []
    cursor = 0
    for shape_now in param_shapes:
        length = 1
        for extent in shape_now:
            length = length * extent
        results.append(gathered[cursor : cursor + length].reshape(shape_now))
        cursor = cursor + length
    out_all = jnp.concatenate(outputs, axis=0)
    grad_all = jnp.concatenate(input_grads, axis=0)
    return (
        out_all,
        grad_all,
        results[0],
        results[1],
        results[2],
        results[3],
        results[4],
        results[5],
        results[6],
        results[7],
        results[8],
        results[9],
        results[10],
        results[11],
        results[12],
        results[13],
        results[14],
    )


def power_of_two(number):
    return number & (number - 1) == 0


def body(tokens, *rest):
    dp, seq, tensor = (lax.axis_size(axis) for axis in ("dp", "seq", "tensor"))
    fits = seq == tokens.shape[0] and tensor == 2 and dp > 1 and power_of_two(dp * seq)
    return (window_body if fits else spread_body)(tokens, *rest)


def solution(mesh):
    in_specs = (
        P("dp", "seq", None),
        P("dp", "seq", None),
        P("dp", None),
        P("dp", None, None),
        P(),
        P(),
        P(None, "tensor"),
        P("tensor"),
        P(None, "tensor"),
        P(None, "tensor"),
        P("tensor"),
        P("tensor", None),
        P(),
        P(),
        P(),
        P(None, "tensor"),
        P("tensor"),
        P("tensor", None),
        P(),
    )
    out_specs = (
        P("dp", "seq", None),
        P("dp", "seq", None),
        P(),
        P(),
        P(None, "tensor"),
        P("tensor"),
        P(None, "tensor"),
        P(None, "tensor"),
        P("tensor"),
        P("tensor", None),
        P(),
        P(),
        P(),
        P(None, "tensor"),
        P("tensor"),
        P("tensor", None),
        P(),
    )
    return jax.shard_map(body, mesh=mesh, in_specs=in_specs, out_specs=out_specs, check_vma=False)
```

```python
import functools

import jax
import jax.numpy as jnp
from jax import lax
from jax.experimental import pallas as pl
from jax.experimental.pallas import tpu as pltpu
from jax.sharding import PartitionSpec as P

HD = 64
BS = 64
MB = 2
WIN_MB = 2


eps_norm = 1e-05
inv_root_two = 0.7071067811865476
inv_root_two_pi = 0.3989422804014327


LANES = 128
NEG = -1e30
VMEM_LIMIT = 16 * 1024 * 1024


def dot_nn(left, right):
    return lax.dot_general(left, right, (((1,), (0,)), ((), ())), preferred_element_type=jnp.float32)


def dot_nt(left, right):
    return lax.dot_general(left, right, (((1,), (1,)), ((), ())), preferred_element_type=jnp.float32)


def dot_tn(left, right):
    return lax.dot_general(left, right, (((0,), (0,)), ((), ())), preferred_element_type=jnp.float32)


def norm_parts(values):
    center = values - jnp.mean(values, axis=-1, keepdims=True)
    scaled = lax.rsqrt(jnp.mean(center * center, axis=-1, keepdims=True) + eps_norm)
    return center * scaled, scaled


def pick_rows(positions, total):
    ids = lax.broadcasted_iota(jnp.int32, (positions.shape[0], total), 1)
    return jnp.where(ids == positions, 1.0, 0.0).astype(jnp.bfloat16)


def row_lists(blocks, allow):
    ids = lax.broadcasted_iota(jnp.int32, (blocks.shape[0], allow.shape[0]), 1)
    return dot_nn(jnp.where(ids == blocks, 1.0, 0.0).astype(jnp.bfloat16), allow)


def head_half(half):
    lane = lax.broadcasted_iota(jnp.int32, (1, LANES), 1)
    return (lane < HD) if half == 0 else (lane >= HD)


def one_head(slab, half):
    return jnp.where(head_half(half), slab, jnp.zeros_like(slab))


class Order:
    def __init__(self):
        self.last = None

    def call(self, kernel, name, outs, args, smem=1, scratch=(), aliases=None):
        first = args[0]
        if self.last is not None:
            first = after(first, self.last)
        spec = pl.BlockSpec(memory_space=pltpu.VMEM)
        found = pl.pallas_call(
            kernel,
            name=name,
            out_shape=outs,
            in_specs=[pl.BlockSpec(memory_space=pltpu.SMEM)] * smem + [spec] * (len(args) - smem),
            out_specs=[spec] * len(outs),
            scratch_shapes=list(scratch),
            input_output_aliases=aliases or {},
            compiler_params=pltpu.CompilerParams(vmem_limit_bytes=VMEM_LIMIT),
            cost_estimate=pl.CostEstimate(flops=1, bytes_accessed=1, transcendentals=0),
        )(first, *args[1:])
        self.last = min(found, key=lambda a: a.size)
        return found


def after(value, *others):
    return lax.optimization_barrier((value, others))[0]


def shape(dims, dtype=jnp.bfloat16):
    return jax.ShapeDtypeStruct(dims, dtype)


def shard_kernel(at, bits, own, other, vec, wq, wk, wv, *rest):
    tok, h, q, k, v = rest[-5:]
    run = own.shape[0]
    local = wq.shape[1]
    first = bits[2] == 0
    tok[pl.ds(2 * at * run, run), :] = jnp.where(first, own[...], other[...])
    tok[pl.ds((2 * at + 1) * run, run), :] = jnp.where(first, other[...], own[...])
    rows = pl.ds(2 * at * run, 2 * run)
    normed, _ = norm_parts(tok[rows, :].astype(jnp.float32))
    low = (normed * vec[0:1, :] + vec[1:2, :]).astype(jnp.bfloat16)
    h[rows, :] = low
    q[rows, :] = (dot_nn(low, wq[...]) + vec[6:7, :local]).astype(jnp.bfloat16)
    k[rows, :] = dot_nn(low, wk[...]).astype(jnp.bfloat16)
    v[rows, :] = (dot_nn(low, wv[...]) + vec[6:7, local:]).astype(jnp.bfloat16)


def sum_rows_kernel(bits, *refs):
    total = None
    for piece in refs[:-1]:
        value = piece[...].astype(jnp.float32)
        total = value if total is None else total + value
    refs[-1][...] = total.astype(jnp.bfloat16)


def front_kernel(bits, pos, allow, wo, tok, h, q, k, v, xm, hm, qm, om, lse, part):
    total, local = q.shape
    pick = pick_rows(pos[...], total)
    xm[...] = dot_nn(pick, tok[...]).astype(jnp.bfloat16)
    hm[...] = dot_nn(pick, h[...]).astype(jnp.bfloat16)
    qm[...] = dot_nn(pick, q[...]).astype(jnp.bfloat16)
    listed = row_lists(pos[...] >> 6, allow[...]) > 0.5
    lane = lax.broadcasted_iota(jnp.int32, (pos.shape[0], LANES), 1)

    def one_slab(slab, sums):
        cols = pl.ds(pl.multiple_of(slab * LANES, LANES), LANES)
        query = (qm[:, cols].astype(jnp.float32) * HD ** (-0.5)).astype(jnp.bfloat16)
        mixed = None
        for half in range(2):
            scores = jnp.where(listed, dot_nt(one_head(query, half), k[:, cols]), NEG)
            top = jnp.max(scores, axis=-1, keepdims=True)
            weight = jnp.exp(scores - top)
            total_weight = jnp.sum(weight, axis=-1, keepdims=True)
            sums = jnp.where(lane == 2 * slab + half, top + jnp.log(total_weight), sums)
            found = dot_nn(weight.astype(jnp.bfloat16), v[:, cols]) * (1.0 / total_weight)
            mixed = found if half == 0 else jnp.where(head_half(0), mixed, found)
        om[:, cols] = mixed.astype(jnp.bfloat16)
        return sums

    none = jnp.zeros((pos.shape[0], LANES), jnp.float32)
    sums = lax.fori_loop(0, local // LANES, one_slab, none)
    lse[...] = sums
    part[...] = dot_nn(om[...], wo[...]).astype(jnp.bfloat16)


def gelu_parts(z):
    cdf = 0.5 * (1.0 + lax.erf(z * inv_root_two))
    return z * cdf, cdf + z * (jnp.exp(-0.5 * z * z) * inv_root_two_pi)


def middle_of(xm, part, other, vec):
    both = part[...].astype(jnp.float32) + other[...].astype(jnp.float32)
    return xm[...].astype(jnp.float32) + (both + vec[2:3, :])


def hidden_kernel(
    bits, xm, part, other, g_own, g_other, vec, wi, wf,
    dwf_a, dwf_as, dwf_b, dwf_bs, dwi_a, dwi_as, dwi_b, dwi_bs, dh2, few, g,
    u_all, h2_all, dz_all,
):
    width, hidden = wi.shape
    split = width // 2
    first = bits[2] == 0
    g[:, :split] = jnp.where(first, g_own[...], g_other[...])
    g[:, split:] = jnp.where(first, g_other[...], g_own[...])
    normed, _ = norm_parts(middle_of(xm, part, other, vec))
    h2_all[...] = (normed * vec[3:4, :] + vec[4:5, :]).astype(jnp.bfloat16)
    h2 = h2_all[...]
    for at in range(hidden // width):
        cols = pl.ds(at * width, width)
        z = dot_nn(h2, wi[:, cols]) + vec[7 + at : 8 + at, :]
        act, slope = gelu_parts(z)
        u_all[:, cols] = act.astype(jnp.bfloat16)
        dz = (dot_nt(g[...], wf[cols, :]) * slope).astype(jnp.bfloat16)
        dz_all[:, cols] = dz
        few[1 + at : 2 + at, :] = jnp.sum(dz.astype(jnp.float32), axis=0, keepdims=True)
    few[0:1, :] = jnp.sum(g[...].astype(jnp.float32), axis=0, keepdims=True)
    half = hidden // 2
    count = half // 2
    for order, keep, send in ((0, dwf_a, dwf_as), (1, dwf_b, dwf_bs)):
        for out, bit in ((keep, bits[order]), (send, 1 - bits[order])):
            at = pl.multiple_of(order * half + bit * count, LANES)
            out[...] = dot_tn(u_all[:, pl.ds(at, count)], g[...]).astype(jnp.bfloat16)
    count = width // 2
    for order, keep, send in ((0, dwi_a, dwi_as), (1, dwi_b, dwi_bs)):
        for out, bit in ((keep, bits[order]), (send, 1 - bits[order])):
            at = pl.multiple_of(bit * count, LANES)
            out[...] = dot_tn(
                h2_all[:, pl.ds(at, count)], dz_all[:, pl.ds(order * half, half)]
            ).astype(jnp.bfloat16)
    dh2[...] = dot_nt(dz_all[...], wi[...]).astype(jnp.bfloat16)


def attend_back_kernel(
    bits, xm, part, other, g, dh2, dh2_other, vec, wo, pos, allow, qm, om, hm, lse, h, k, v,
    da_a, da_as, da_b, da_bs, dx1, dq, dk, dv, few, da_all, do_all,
):
    width = g.shape[1]
    normed, scaled = norm_parts(middle_of(xm, part, other, vec))
    up = dh2[...].astype(jnp.float32) + dh2_other[...].astype(jnp.float32)
    few[0:1, :] = jnp.sum(up * normed, axis=0, keepdims=True)
    few[1:2, :] = jnp.sum(up, axis=0, keepdims=True)
    weighted = up * vec[3:4, :]
    centered = weighted - jnp.mean(weighted, axis=-1, keepdims=True)
    slope = jnp.mean(weighted * normed, axis=-1, keepdims=True)
    grad = g[...].astype(jnp.float32) + scaled * (centered - normed * slope)
    dx1[...] = grad
    low = grad.astype(jnp.bfloat16)
    da_all[...] = low
    few[2:3, :] = jnp.sum(low.astype(jnp.float32), axis=0, keepdims=True)
    do_all[...] = dot_nt(low, wo[...]).astype(jnp.bfloat16)
    listed = row_lists(pos[...] >> 6, allow[...]) > 0.5
    for slab in range(qm.shape[1] // LANES):
        cols = pl.ds(slab * LANES, LANES)
        query = (qm[:, cols].astype(jnp.float32) * HD ** (-0.5)).astype(jnp.bfloat16)
        grad_q, grad_k, grad_v = None, None, None
        for half in range(2):
            at = 2 * slab + half
            own = one_head(query, half)
            own_do = one_head(do_all[:, cols], half)
            scores = jnp.where(listed, dot_nt(own, k[:, cols]), NEG)
            prob = jnp.exp(scores - lse[:, at : at + 1])
            grad_p = dot_nt(own_do, v[:, cols])
            delta = jnp.sum(prob * grad_p, axis=-1, keepdims=True)
            ds = (prob * (grad_p - delta)).astype(jnp.bfloat16)
            found_q = dot_nn(ds, k[:, cols])
            found_k = dot_tn(ds, own)
            found_v = dot_tn(prob.astype(jnp.bfloat16), own_do)
            grad_q = found_q if half == 0 else jnp.where(head_half(0), grad_q, found_q)
            grad_k = found_k if half == 0 else grad_k + found_k
            grad_v = found_v if half == 0 else grad_v + found_v
        dq[:, cols] = (grad_q * HD ** (-0.5)).astype(jnp.bfloat16)
        dk[:, cols] = grad_k.astype(jnp.bfloat16)
        dv[:, cols] = grad_v.astype(jnp.bfloat16)
    local = qm.shape[1]
    few[3:4, :local] = jnp.sum(dq[...].astype(jnp.float32), axis=0, keepdims=True)
    few[3:4, local:] = jnp.sum(dv[...].astype(jnp.float32), axis=0, keepdims=True)
    count = width // 2
    for keep, bit in ((da_a, bits[0]), (da_as, 1 - bits[0])):
        cols = pl.ds(pl.multiple_of(bit * count, LANES), count)
        keep[:, :local] = dot_tn(hm[:, cols], dq[...]).astype(jnp.bfloat16)
        keep[:, local:] = dot_tn(h[:, cols], dk[...]).astype(jnp.bfloat16)
    for keep, bit in ((da_b, bits[1]), (da_bs, 1 - bits[1])):
        cols = pl.ds(pl.multiple_of(bit * count, LANES), count)
        keep[:, :local] = dot_tn(h[:, cols], dv[...]).astype(jnp.bfloat16)
        keep[:, local:] = dot_tn(om[...], da_all[:, cols]).astype(jnp.bfloat16)


def input_kernel(bits, pos, dq, dk, dv, wq, wk, wv, keep, *rest):
    sends, dq_all = rest[:-1], rest[-1]
    total = dk.shape[0]
    dq_all[...] = dot_tn(pick_rows(pos[...], total), dq[...]).astype(jnp.bfloat16)
    run = BS * 2
    for at in range(0, total // (2 * run)):
        own = keep.at[pl.ds(at * run, run), :]
        sent = sends[at // 2].at[pl.ds(at % 2 * run, run), :]
        for out, bit in ((own, bits[2]), (sent, 1 - bits[2])):
            rows = pl.ds(pl.multiple_of(at * 2 * run + bit * run, run), run)
            out[...] = (
                dot_nt(dq_all[rows, :], wq[...])
                + dot_nt(dk[rows, :], wk[...])
                + dot_nt(dv[rows, :], wv[...])
            ).astype(jnp.bfloat16)


def first_norm_kernel(count, bits, pos_half, own, dx1, vec, *rest):
    toks, others, grads = rest[:count], rest[count : -3 - count], rest[-3 - count : -3]
    few, tok, other = rest[-3:]
    run = others[0].shape[0]
    for at, piece in enumerate(others):
        other[pl.ds(at * run, run), :] = piece[...]
    run = toks[0].shape[0]
    for at, piece in enumerate(toks):
        tok[pl.ds(at * run, run), :] = piece[...]
    normed, scaled = norm_parts(tok[...].astype(jnp.float32))
    up = own[...].astype(jnp.float32) + other[...].astype(jnp.float32)
    few[0:1, :] = jnp.sum(up * normed, axis=0, keepdims=True)
    few[1:2, :] = jnp.sum(up, axis=0, keepdims=True)
    weighted = up * vec[0:1, :]
    centered = weighted - jnp.mean(weighted, axis=-1, keepdims=True)
    slope = jnp.mean(weighted * normed, axis=-1, keepdims=True)
    pick = pick_rows(pos_half[...], tok.shape[0])
    high = dx1[...].astype(jnp.bfloat16)
    rest = (dx1[...] - high.astype(jnp.float32)).astype(jnp.bfloat16)
    through = dot_tn(pick, high) + dot_tn(pick, rest)
    grad = (through + scaled * (centered - normed * slope)).astype(jnp.bfloat16)
    for at, piece in enumerate(grads):
        piece[...] = grad[at * run : (at + 1) * run, :]


def attend_kernel(at, q, k, v, allow, wo, part_low, part_high, mixed_all):
    tile = mixed_all.shape[0]
    rows = pl.ds(pl.multiple_of(at[0] * tile, tile), tile)
    ids = lax.broadcasted_iota(jnp.int32, (tile, 1), 0)
    bias = (row_lists(at[0] * (tile // BS) + (ids >> 6), allow[...]) - 1.0) * -NEG

    def one_slab(slab, carry):
        cols = pl.ds(pl.multiple_of(slab * LANES, LANES), LANES)
        query = (q[rows, cols].astype(jnp.float32) * HD ** (-0.5)).astype(jnp.bfloat16)
        mixed = None
        for half in range(2):
            scores = dot_nt(one_head(query, half), k[:, cols]) + bias
            weight = jnp.exp(scores - jnp.max(scores, axis=-1, keepdims=True))
            total_weight = jnp.sum(weight, axis=-1, keepdims=True)
            found = dot_nn(weight.astype(jnp.bfloat16), v[:, cols]) * (1.0 / total_weight)
            mixed = found if half == 0 else jnp.where(head_half(0), mixed, found)
        mixed_all[:, cols] = mixed.astype(jnp.bfloat16)
        return carry

    lax.fori_loop(0, q.shape[1] // LANES, one_slab, 0)
    half = tile // 2
    part_low[...] = dot_nn(mixed_all[:half, :], wo[...]).astype(jnp.bfloat16)
    part_high[...] = dot_nn(mixed_all[half:, :], wo[...]).astype(jnp.bfloat16)


def feed_kernel(
    at, bits, tok, low, high, low_other, high_other, vec, wi, wf, keep, send, total_all, mid_all
):
    width, hidden = wi.shape
    tile = total_all.shape[0]
    half = tile // 2
    for which, (own, other) in enumerate(((low, low_other), (high, high_other))):
        rows = pl.ds(pl.multiple_of(at[0] * tile + which * half, half), half)
        mid_all[pl.ds(which * half, half), :] = middle_of(tok.at[rows, :], own, other, vec)
    middle = mid_all[...]
    normed, _ = norm_parts(middle)
    h2 = (normed * vec[3:4, :] + vec[4:5, :]).astype(jnp.bfloat16)
    total = None
    for part_at in range(hidden // width):
        cols = pl.ds(part_at * width, width)
        z = dot_nn(h2, wi[:, cols]) + vec[7 + part_at : 8 + part_at, :]
        act = z * (0.5 * (1.0 + lax.erf(z * inv_root_two)))
        found = dot_nn(act.astype(jnp.bfloat16), wf[cols, :])
        total = found if total is None else total + found
    run = tile // 2
    total_all[...] = total
    send[...] = total_all[pl.ds(pl.multiple_of((1 - bits[2]) * run, run), run), :].astype(
        jnp.bfloat16
    )
    total_all[...] += middle + vec[5:6, :]
    keep[...] = total_all[pl.ds(pl.multiple_of(bits[2] * run, run), run), :]


def gather_small_kernel(bits, first, first_other, attend, hidden, out):
    out[0:2, :] = first[...] + first_other[...]
    out[2:6, :] = attend[...]
    out[6:, :] = hidden[...]


def add_small_kernel(bits, own, other, out):
    out[...] = own[...] + other[...]


def finish_kernel(count, bits, *refs):
    for at in range(count):
        keep, other = refs[at][...], refs[count + at][...].astype(jnp.float32)
        refs[2 * count + at][...] = (keep + other).astype(jnp.bfloat16)


def interleave_kernel(bits, *refs):
    out = refs[-1]
    count = out.shape[0]
    run = refs[0].shape[0]
    for at in range(count):
        window = bits[5] ^ at
        out[window, pl.ds(pl.multiple_of(bits[2] * run, run), run), :] = refs[at][...]
        out[window, pl.ds(pl.multiple_of((1 - bits[2]) * run, run), run), :] = refs[count + at][...]


def add_low(left, right):
    return (left.astype(jnp.float32) + right.astype(jnp.float32)).astype(jnp.bfloat16)


def part_rows(bit, count):
    return pl.ds(pl.multiple_of(bit * count, 16), count)


def halve_plane_kernel(at, bits, ka, ra, kb, rb, keep_a, send_a, keep_b, send_b):
    count = keep_a.shape[0]
    groups = ((ka, ra, keep_a, send_a, bits[at[0]]), (kb, rb, keep_b, send_b, bits[at[1]]))
    for k, r, keep, send, bit in groups:
        for out, side in ((keep, bit), (send, 1 - bit)):
            rows = part_rows(side, count)
            out[...] = add_low(k[rows, :], r[rows, :])


def halve_join_kernel(at, bits, ka, ra, kb, rb, keep, send):
    count = keep.shape[1]
    for out, side in ((keep, bits[at]), (send, 1 - bits[at])):
        rows = part_rows(side, count)
        out[0] = add_low(ka[rows, :], ra[rows, :])
        out[1] = add_low(kb[rows, :], rb[rows, :])


def halve_line_kernel(at, bits, k, r, keep, send):
    count = keep.shape[1]
    for out, side in ((keep, bits[at]), (send, 1 - bits[at])):
        rows = part_rows(side, count)
        out[...] = add_low(k[:, rows, :], r[:, rows, :])


def last_line_kernel(bits, k, r, out):
    out[...] = add_low(k[...], r[...])


def double_line_kernel(at, bits, own, other, out):
    count = own.shape[1]
    out[:, part_rows(bits[at], count), :] = own[...]
    out[:, part_rows(1 - bits[at], count), :] = other[...]


def double_split_kernel(at, bits, own, other, out_a, out_b):
    count = own.shape[1]
    for which, out in ((0, out_a), (1, out_b)):
        out[part_rows(bits[at], count), :] = own[which]
        out[part_rows(1 - bits[at], count), :] = other[which]


def double_plane_kernel(at, bits, own_a, other_a, own_b, other_b, out_a, out_b):
    groups = ((own_a, other_a, out_a, bits[at[0]]), (own_b, other_b, out_b, bits[at[1]]))
    for own, other, out, bit in groups:
        count = own.shape[0]
        out[part_rows(bit, count), :] = own[...]
        out[part_rows(1 - bit, count), :] = other[...]


def last_rows_kernel(at, bits, own_a, other_a, own_b, other_b, out):
    count = own_a.shape[0]
    groups = ((own_a, other_a, bits[at[0]]), (own_b, other_b, bits[at[1]]))
    for which, (own, other, bit) in enumerate(groups):
        for value, side in ((own, bit), (other, 1 - bit)):
            out[part_rows(2 * which + side, count), :] = value[...].astype(jnp.float32)


def last_columns_kernel(at, bits, own_a, other_a, own_b, other_b, out):
    count, width = own_a.shape
    groups = ((own_a, other_a, bits[at[0]]), (own_b, other_b, bits[at[1]]))
    for which, (own, other, bit) in enumerate(groups):
        for value, side in ((own, bit), (other, 1 - bit)):
            out[part_rows(side, count), pl.ds(which * width, width)] = value[...].astype(
                jnp.float32
            )


def last_attend_kernel(
    at, bits, own_a, other_a, own_b, other_b, grad_q, grad_k, grad_v, grad_o
):
    count = own_a.shape[0]
    local = grad_q.shape[1]
    for value, side in ((own_a, bits[at[0]]), (other_a, 1 - bits[at[0]])):
        grad_q[part_rows(side, count), :] = value[:, :local].astype(jnp.float32)
        grad_k[part_rows(side, count), :] = value[:, local:].astype(jnp.float32)
    for value, side in ((own_b, bits[at[1]]), (other_b, 1 - bits[at[1]])):
        grad_v[part_rows(side, count), :] = value[:, :local].astype(jnp.float32)
        cols = pl.ds(pl.multiple_of(side * count, LANES), count)
        grad_o[:, cols] = value[:, local:].astype(jnp.float32)


def flip(value, axis, bit):
    return lax.ppermute(value, axis, [(i, i ^ bit) for i in range(lax.axis_size(axis))])


def bit_of(axis, bit):
    return jnp.where((lax.axis_index(axis) & bit) != 0, 1, 0).astype(jnp.int32)


def stages_of(order):
    dp_bits = [("dp", 1 << i) for i in range(lax.axis_size("dp").bit_length() - 1)]
    seq_bits = [("seq", 1 << i) for i in range(lax.axis_size("seq").bit_length() - 1)]
    return (dp_bits if order == 0 else dp_bits[::-1]) + seq_bits


class Summing:
    def __init__(self, order, bits, keep, send):
        self.order, self.bits = order, bits
        self.keep, self.send = list(keep), list(send)
        self.plane = [stages_of(which)[:2] for which in range(2)]
        self.line = stages_of(0)[2:]

    def hold(self, *others):
        self.send = [after(value, *others) for value in self.send]

    def exchange(self, at):
        return [flip(s, *self.plane[which][at]) for which, s in enumerate(self.send)]

    def halve_first(self):
        other = self.exchange(0)
        rows, width = self.keep[0].shape
        ka, sa, kb, sb = self.order.call(
            functools.partial(halve_plane_kernel, (1, 0)),
            "halve_plane",
            [shape((rows // 2, width))] * 4,
            (self.bits, self.keep[0], other[0], self.keep[1], other[1]),
        )
        self.keep, self.send = [ka, kb], [sa, sb]

    def halve_second(self):
        other = self.exchange(1)
        rows, width = self.keep[0].shape
        self.keep, self.send = self.order.call(
            functools.partial(halve_join_kernel, 3),
            "halve_join",
            [shape((2, rows // 2, width))] * 2,
            (self.bits, self.keep[0], other[0], self.keep[1], other[1]),
        )

    def halve_line(self, at):
        other = flip(self.send, *self.line[at])
        two, rows, width = self.keep.shape
        if at + 1 < len(self.line):
            self.keep, self.send = self.order.call(
                functools.partial(halve_line_kernel, 4 + at),
                "halve_line",
                [shape((two, rows // 2, width))] * 2,
                (self.bits, self.keep, other),
            )
        else:
            (self.send,) = self.order.call(
                last_line_kernel, "last_line", [shape(self.keep.shape)], (self.bits, self.keep, other)
            )

    def double_line(self, at):
        other = flip(self.send, *self.line[at])
        two, rows, width = self.send.shape
        if at > 0:
            (self.send,) = self.order.call(
                functools.partial(double_line_kernel, 3 + at),
                "double_line",
                [shape((two, 2 * rows, width))],
                (self.bits, self.send, other),
            )
        else:
            self.send = self.order.call(
                functools.partial(double_split_kernel, 3 + at),
                "double_split",
                [shape((2 * rows, width))] * 2,
                (self.bits, self.send, other),
            )

    def double_second(self):
        other = self.exchange(1)
        rows, width = self.send[0].shape
        self.send = self.order.call(
            functools.partial(double_plane_kernel, (1, 0)),
            "double_plane",
            [shape((2 * rows, width))] * 2,
            (self.bits, self.send[0], other[0], self.send[1], other[1]),
        )

    def double_first(self, kernel, outs):
        other = self.exchange(0)
        return self.order.call(
            functools.partial(kernel, (0, 1)),
            "last",
            [shape(dims, jnp.float32) for dims in outs],
            (self.bits, self.send[0], other[0], self.send[1], other[1]),
        )


def window_body(
    tokens, cotangent, masked_pos, rand_blocks, ln1_gain, ln1_bias, w_query, b_query, w_key,
    w_value, b_value, w_out, b_out, ln2_gain, ln2_bias, w_inner, b_inner, w_outer, b_outer,
):
    windows, rows, width = tokens.shape
    local = w_query.shape[1]
    hidden = w_inner.shape[1]
    total = windows * rows
    blocks = total // BS
    wide = hidden // 2
    run = rows // 2
    split = width // 2
    place = lax.axis_index("seq")
    core = lax.axis_index("tensor")
    plane, line = stages_of(0)[:2], stages_of(0)[2:]
    bits = jnp.stack(
        [bit_of(*step) for step in plane]
        + [core.astype(jnp.int32)]
        + [bit_of(*step) for step in line]
        + [place.astype(jnp.int32)]
    )
    tile_ids = [jnp.full((1,), at, jnp.int32) for at in range(windows)]

    cut = tokens.reshape(windows, 2, run, width)
    own_rows = []
    for at in range(windows):
        piece = lax.dynamic_slice(cut, (place ^ at, core, 0, 0), (1, 1, run, width))
        piece = piece.reshape(run, width)
        own_rows.append(piece if at == 0 else flip(piece, "seq", at))

    named = masked_pos.shape[1]
    count = -(-named // 16) * 16
    spots = jnp.concatenate(
        [masked_pos, jnp.full((windows, count - named), -1, jnp.int32)], axis=1
    )
    slot = jnp.arange(count, dtype=jnp.int32)
    again = jnp.any(
        (spots[:, :, None] == spots[:, None, :]) & (slot[None, :] < slot[:, None])[None], axis=2
    )
    spots = jnp.where(again, -1, spots)
    spot = lax.dynamic_index_in_dim(spots, place, 0, keepdims=True).reshape(count, 1)
    there, inside = (spot // rows) ^ place, spot % rows
    pos = jnp.where(spot >= 0, there * rows + inside, -1)
    mine = (spot >= 0) & (inside // run == core)
    pos_half = jnp.where(mine, there * run + inside % run, -1)

    here = spots - place * rows
    found = []
    for at in range(windows):
        named_rows = lax.dynamic_index_in_dim(here, place ^ at, 0, keepdims=False)
        pick = (named_rows[:, None] == jnp.arange(rows, dtype=jnp.int32)[None, :]).astype(
            jnp.bfloat16
        )
        shard = lax.dynamic_slice(
            cotangent, (place ^ at, 0, core * split), (1, rows, split)
        ).reshape(rows, split)
        found.append(dot_nn(pick, shard).astype(jnp.bfloat16))

    rand = lax.dynamic_index_in_dim(rand_blocks, place, 0, keepdims=False)
    numbers = jnp.arange(blocks, dtype=jnp.int32)
    shard_blocks = rows // BS
    ids = ((numbers // shard_blocks) ^ place) * shard_blocks + numbers % shard_blocks
    named_blocks = jnp.any(rand[:, :, None] == ids[None, None, :], axis=1)
    named_blocks = jnp.any(
        (ids[:, None] == numbers[None, :])[:, :, None] & named_blocks[None], axis=1
    )
    listed = (
        (jnp.abs(ids[:, None] - ids[None, :]) <= 1)
        | (ids == 0)[None, :]
        | (ids == blocks - 1)[None, :]
        | named_blocks
    )
    allow = jnp.repeat(listed.astype(jnp.bfloat16), BS, axis=1)

    vec = jnp.stack(
        [ln1_gain, ln1_bias, b_out, ln2_gain, ln2_bias, b_outer]
        + [jnp.concatenate([b_query, b_value])]
        + [b_inner[at : at + width] for at in range(0, hidden, width)]
    ).astype(jnp.float32)

    order = Order()
    state = None
    for at in range(windows):
        if at == 1:
            bits, pos, pos_half, allow, *found = lax.optimization_barrier(
                (bits, pos, pos_half, allow, *found)
            )
        kept = () if state is None else tuple(state)
        state = order.call(
            functools.partial(shard_kernel, at),
            "shard",
            [shape((total, width))] * 2 + [shape((total, local))] * 3,
            (bits, own_rows[at], flip(own_rows[at], "tensor", 1), vec, w_query, w_key, w_value)
            + kept,
            aliases={7 + i: i for i in range(len(kept))},
        )
    tok, h, q, k, v = state
    found = [found[0]] + [
        flip(after(found[at], *own_rows[2:]), "seq", at) for at in range(1, windows)
    ]
    xm, hm, qm, om, lse, part = order.call(
        front_kernel,
        "front",
        [shape((count, width))] * 2
        + [shape((count, local))] * 2
        + [shape((count, LANES), jnp.float32), shape((count, width))],
        (bits, pos, allow, w_out, tok, h, q, k, v),
    )
    other = flip(part, "tensor", 1)
    (g_own,) = order.call(sum_rows_kernel, "sum_rows", [shape((count, split))], (bits, *found))
    g_other = flip(g_own, "tensor", 1)
    outs = order.call(
        hidden_kernel,
        "hidden",
        [shape((wide // 2, width))] * 4
        + [shape((width // 2, wide))] * 4
        + [shape((count, width)), shape((1 + hidden // width, width), jnp.float32)]
        + [shape((count, width))],
        (bits, xm, part, other, g_own, g_other, vec, w_inner, w_outer),
        scratch=[
            pltpu.VMEM((count, hidden), jnp.bfloat16),
            pltpu.VMEM((count, width), jnp.bfloat16),
            pltpu.VMEM((count, hidden), jnp.bfloat16),
        ],
    )
    dwf_a, dwf_as, dwf_b, dwf_bs, dwi_a, dwi_as, dwi_b, dwi_bs, dh2, few_hidden, g = outs
    sum_f = Summing(order, bits, (dwf_a, dwf_b), (dwf_as, dwf_bs))
    sum_i = Summing(order, bits, (dwi_a, dwi_b), (dwi_as, dwi_bs))

    dh2_other = flip(dh2, "tensor", 1)
    outs = order.call(
        attend_back_kernel,
        "attend_back",
        [shape((width // 2, 2 * local))] * 2
        + [shape((width // 2, local + width // 2))] * 2
        + [shape((count, width), jnp.float32), shape((count, local))]
        + [shape((total, local))] * 2
        + [shape((4, width), jnp.float32)],
        (bits, xm, part, other, g, dh2, dh2_other, vec, w_out, pos, allow)
        + (qm, om, hm, lse, h, k, v),
        scratch=[
            pltpu.VMEM((count, width), jnp.bfloat16),
            pltpu.VMEM((count, local), jnp.bfloat16),
        ],
    )
    da_a, da_as, da_b, da_bs, dx1, dq, dk, dv, few_attend = outs
    sum_a = Summing(order, bits, (da_a, da_b), (da_as, da_bs))

    def attend(at):
        low, high = order.call(
            attend_kernel,
            "attend",
            [shape((run, width))] * 2,
            (tile_ids[at], q, k, v, allow, w_out),
            scratch=[pltpu.VMEM((rows, local), jnp.bfloat16)],
        )
        return low, high, flip(low, "tensor", 1), flip(high, "tensor", 1)

    def feed(at, parts):
        keep, send = order.call(
            feed_kernel,
            "feed",
            [shape((run, width), jnp.float32), shape((run, width))],
            (tile_ids[at], bits, tok, *parts, vec, w_inner, w_outer),
            smem=2,
            scratch=[pltpu.VMEM((rows, width), jnp.float32)] * 2,
        )
        return keep, flip(send, "tensor", 1)

    small_steps = iter(stages_of(0))
    small = None

    def add_small():
        (found,) = order.call(
            add_small_kernel,
            "add_small",
            [shape(small.shape, jnp.float32)],
            (bits, small, flip(small, *next(small_steps))),
        )
        return found

    def send_back(pieces, at):
        return flip(after(pieces[at], order.last), "seq", at)

    def swap_back(pieces):
        pieces = [after(piece, order.last) for piece in pieces]
        return pieces + [flip(piece, "tensor", 1) for piece in pieces]

    sum_f.halve_first()
    dh_own, *dh_send = order.call(
        input_kernel,
        "input_grad",
        [shape((total // 2, width))] + [shape((total // 4, width))] * 2,
        (bits, pos, dq, dk, dv, w_query, w_key, w_value),
        scratch=[pltpu.VMEM((total, local), jnp.bfloat16)],
    )
    dh_other = [flip(piece, "tensor", 1) for piece in dh_send]
    sum_f.halve_second()
    sum_i.hold(order.last)
    parts = [attend(0)]
    *grad_half, few_first = order.call(
        functools.partial(first_norm_kernel, windows),
        "first_norm",
        [shape((run, width))] * windows + [shape((2, width), jnp.float32)],
        (bits, pos_half, dh_own, dx1, vec, *own_rows, *dh_other),
        scratch=[pltpu.VMEM((total // 2, width), jnp.bfloat16)] * 2,
    )
    first_other = flip(few_first, "tensor", 1)
    sum_f.halve_line(0)
    grad_back = [grad_half[0], send_back(grad_half, 1)]
    sum_i.halve_first()
    parts.append(attend(1))
    (small,) = order.call(
        gather_small_kernel,
        "gather_small",
        [shape((7 + hidden // width, width), jnp.float32)],
        (bits, few_first, first_other, few_attend, few_hidden),
    )
    sum_f.halve_line(1)
    grad_back.append(send_back(grad_half, 2))
    sum_i.halve_second()
    sum_a.hold(order.last)
    parts.append(attend(2))
    sum_f.double_line(1)
    grad_back.append(send_back(grad_half, 3))
    small = add_small()
    sum_i.halve_line(0)
    parts.append(attend(3))
    sum_a.halve_first()
    sum_f.double_line(0)
    small = add_small()
    sum_i.halve_line(1)
    grad_pair = swap_back(grad_back)
    fed = [feed(0, parts[0])]
    sum_a.halve_second()
    sum_i.double_line(1)
    whole = [shape((windows, rows, width))]
    (grad_tokens,) = order.call(interleave_kernel, "interleave", whole, (bits, *grad_pair))
    fed.append(feed(1, parts[1]))
    sum_a.halve_line(0)
    sum_f.double_second()
    sum_i.double_line(0)
    small = add_small()
    sum_a.halve_line(1)
    fed.append(feed(2, parts[2]))
    sum_a.double_line(1)
    small = add_small()
    fed.append(feed(3, parts[3]))
    sum_a.double_line(0)
    out_half = order.call(
        functools.partial(finish_kernel, windows),
        "finish",
        [shape((run, width))] * windows,
        [bits] + [f[0] for f in fed] + [f[1] for f in fed],
    )
    out_back = [out_half[0]] + [flip(out_half[at], "seq", at) for at in range(1, windows)]
    (grad_wf,) = sum_f.double_first(last_rows_kernel, [(hidden, width)])
    sum_i.double_second()
    (grad_wi,) = sum_i.double_first(last_columns_kernel, [(width, hidden)])
    out_pair = swap_back(out_back)
    sum_a.double_second()
    (out,) = order.call(interleave_kernel, "interleave", whole, (bits, *out_pair))
    grad_q, grad_k, grad_v, grad_o = sum_a.double_first(
        last_attend_kernel, [(width, local)] * 3 + [(local, width)]
    )
    return (
        out,
        grad_tokens,
        small[0],
        small[1],
        grad_q,
        small[5, :local],
        grad_k,
        grad_v,
        small[5, local:],
        grad_o,
        small[4],
        small[2],
        small[3],
        grad_wi,
        small[7:].reshape(-1),
        grad_wf,
        small[6],
    )


def with_halo(block, sides, width):
    for axis, dim in sides:
        count = lax.axis_size(axis)
        forward = [(i, i + 1) for i in range(count - 1)]
        backward = [(target, source) for source, target in forward]
        low = lax.ppermute(
            lax.slice_in_dim(block, block.shape[dim] - width, None, axis=dim), axis, forward
        )
        high = lax.ppermute(lax.slice_in_dim(block, 0, width, axis=dim), axis, backward)
        block = jnp.concatenate([low, block, high], axis=dim)
    return block


def broadcast(value, axis, root):
    mine = lax.axis_index(axis) == root
    return lax.psum(jnp.where(mine, value, jnp.zeros_like(value)), axis)


def norm_forward(values, gain, shift):
    center = values - jnp.mean(values, axis=-1, keepdims=True)
    scaled = lax.rsqrt(jnp.mean(center * center, axis=-1, keepdims=True) + eps_norm)
    normed = center * scaled
    return (normed * gain + shift, normed, scaled)


def norm_backward(upstream, gain, normed, scaled):
    weighted = upstream * gain
    centered = weighted - jnp.mean(weighted, axis=-1, keepdims=True)
    return scaled * (centered - normed * jnp.mean(weighted * normed, axis=-1, keepdims=True))


def row_dot(left, right):
    return lax.dot_general(
        left, right, (((left.ndim - 1,), (0,)), ((), ())), preferred_element_type=jnp.float32
    )


def back_dot(left, right):
    return lax.dot_general(
        left, right, (((left.ndim - 1,), (1,)), ((), ())), preferred_element_type=jnp.float32
    )


def outer_sum(left, right):
    return lax.dot_general(
        left, right, (((0, 1), (0, 1)), ((), ())), preferred_element_type=jnp.float32
    )


def column_sum(values):
    return jnp.sum(values, axis=(0, 1), dtype=jnp.float32)


def list_masks(rand_local, first_block, block_count):
    window_count, local_count = (rand_local.shape[0], rand_local.shape[1])
    query_ids = first_block + jnp.arange(local_count, dtype=jnp.int32)
    slide_ok = jnp.stack(
        [query_ids - 1 >= 0, query_ids >= 0, query_ids + 1 <= block_count - 1], axis=1
    )
    end_ok = jnp.stack([jnp.abs(query_ids) > 1, jnp.abs(block_count - 1 - query_ids) > 1], axis=1)
    rand_ok = (
        (jnp.abs(rand_local - query_ids[None, :, None]) > 1)
        & (rand_local != 0)
        & (rand_local != block_count - 1)
    )
    fixed_ok = jnp.broadcast_to(
        jnp.concatenate([slide_ok, end_ok], axis=1)[None], (window_count, local_count, 5)
    )
    return jnp.concatenate([fixed_ok, rand_ok], axis=-1)


def build_routing(rand_batch, position, devices, local_count, capacity):
    window_count = rand_batch.shape[0]
    item_count = window_count * local_count * 3

    def arrange(grid_values):
        grid_values = grid_values.reshape(window_count, devices, local_count, 3)
        return jnp.transpose(grid_values, (1, 0, 2, 3)).reshape(devices, item_count)

    window_grid = jnp.broadcast_to(
        jnp.arange(window_count, dtype=jnp.int32)[:, None, None], rand_batch.shape
    )
    owner_table = arrange(rand_batch // local_count)
    source_table = arrange(window_grid * local_count + rand_batch % local_count)
    device_ids = jnp.arange(devices, dtype=jnp.int32)
    matches = (owner_table[:, :, None] == device_ids[None, None, :]).astype(jnp.int32)
    earlier = jnp.cumsum(matches, axis=1) - matches
    slot_table = jnp.sum(earlier * matches, axis=2)
    owned_here = (owner_table == position).astype(jnp.int32)
    slot_ids = jnp.arange(capacity, dtype=jnp.int32)
    slot_matches = (slot_table[:, :, None] == slot_ids[None, None, :]).astype(
        jnp.int32
    ) * owned_here[:, :, None]
    send_rows = jnp.sum(slot_matches * source_table[:, :, None], axis=1).reshape(devices * capacity)
    send_live = jnp.sum(slot_matches, axis=1).reshape(devices * capacity)
    my_owner = lax.dynamic_index_in_dim(owner_table, position, 0, keepdims=False)
    my_slot = lax.dynamic_index_in_dim(slot_table, position, 0, keepdims=False)
    take_rows = my_owner * capacity + my_slot
    return (send_rows, send_live, take_rows)


def fetch_blocks(packed, routing, block_rows):
    window_count, local_rows, kv_width = packed.shape
    local_count = local_rows // block_rows
    devices = lax.axis_size("seq")
    padded = with_halo(packed, (("seq", 1),), block_rows)
    padded = padded.reshape(window_count, local_count + 2, block_rows, kv_width)
    sliding = jnp.stack([padded[:, offset : offset + local_count] for offset in range(3)], axis=2)
    first_part = broadcast(packed[:, :block_rows], "seq", 0)
    last_part = broadcast(packed[:, local_rows - block_rows :], "seq", devices - 1)
    end_blocks = jnp.stack([first_part, last_part], axis=1)
    end_blocks = jnp.broadcast_to(
        end_blocks[:, None], (window_count, local_count, 2, block_rows, kv_width)
    )
    send_rows, send_live, take_rows = routing
    sources = packed.reshape(window_count * local_count, block_rows, kv_width)
    outgoing = jnp.take(sources, send_rows, axis=0).reshape(devices, -1, block_rows, kv_width)
    incoming = lax.all_to_all(outgoing, "seq", split_axis=0, concat_axis=0, tiled=True).reshape(
        -1, block_rows, kv_width
    )
    fetched = jnp.take(incoming, take_rows, axis=0).reshape(
        window_count, local_count, 3, block_rows, kv_width
    )
    return jnp.concatenate([sliding, end_blocks, fetched], axis=2)


def return_blocks(kv_grads, routing, block_rows):
    window_count, local_count = (kv_grads.shape[0], kv_grads.shape[1])
    kv_width = kv_grads.shape[-1]
    local_rows = local_count * block_rows
    devices = lax.axis_size("seq")
    position = lax.axis_index("seq")
    padded_grad = jnp.zeros((window_count, local_count + 2, block_rows, kv_width), jnp.float32)
    for offset in range(3):
        padded_grad = padded_grad.at[:, offset : offset + local_count].add(kv_grads[:, :, offset])
    rim_rows = jnp.concatenate([padded_grad[:, 0], padded_grad[:, local_count + 1]], axis=1)
    rim_back = with_halo(rim_rows.astype(jnp.bfloat16), (("seq", 1),), block_rows).astype(
        rim_rows.dtype
    )
    end_grads = lax.psum(jnp.sum(kv_grads[:, :, 3:5], axis=1).astype(jnp.bfloat16), "seq").astype(
        jnp.float32
    )
    zeros_block = jnp.zeros((window_count, block_rows, kv_width), jnp.float32)
    first_add = rim_back[:, :block_rows] + jnp.where(position == 0, end_grads[:, 0], zeros_block)
    last_add = rim_back[:, 3 * block_rows :] + jnp.where(
        position == devices - 1, end_grads[:, 1], zeros_block
    )
    send_rows, send_live, take_rows = routing
    rand_items = kv_grads[:, :, 5:8].reshape(-1, block_rows, kv_width)
    capacity_rows = send_rows.shape[0]
    outgoing = (
        jnp.zeros((capacity_rows, block_rows, kv_width), jnp.float32).at[take_rows].set(rand_items)
    )
    incoming = lax.all_to_all(
        outgoing.reshape(devices, -1, block_rows, kv_width).astype(jnp.bfloat16),
        "seq",
        split_axis=0,
        concat_axis=0,
        tiled=True,
    ).astype(jnp.float32)
    incoming = (
        incoming.reshape(capacity_rows, block_rows, kv_width)
        * send_live.astype(jnp.float32)[:, None, None]
    )
    from_owners = (
        jnp.zeros((window_count * local_count, block_rows, kv_width), jnp.float32)
        .at[send_rows]
        .add(incoming)
    )
    summed = padded_grad[:, 1 : local_count + 1].reshape(window_count, local_rows, kv_width)
    summed = summed + from_owners.reshape(window_count, local_rows, kv_width)
    summed = summed.at[:, :block_rows].add(first_add)
    summed = summed.at[:, local_rows - block_rows :].add(last_add)
    return summed


def split_scores(query_low, keyset, key_valid):
    window_count, local_rows, local_width = query_low.shape
    local_count = keyset.shape[1]
    head_count = local_width // HD
    key_rows = keyset.shape[2] * BS
    query_split = query_low.reshape(window_count, local_count, BS, head_count, HD)
    paired = keyset.reshape(window_count, local_count, key_rows, 2, head_count, HD)
    key_part = paired[:, :, :, 0]
    value_part = paired[:, :, :, 1]
    scores = jnp.einsum(
        "wbqhd,wbkhd->wbhqk", query_split, key_part, preferred_element_type=jnp.float32
    ) * HD ** (-0.5)
    allowed = jnp.repeat(key_valid, BS, axis=2)[:, :, None, None, :]
    scores = jnp.where(allowed, scores, -1e30)
    return (scores, query_split, key_part, value_part)


def attend_forward(query_low, keyset, key_valid):
    scores, query_split, key_part, value_part = split_scores(query_low, keyset, key_valid)
    top_score = jnp.max(scores, axis=-1, keepdims=True)
    log_total = top_score + jnp.log(jnp.sum(jnp.exp(scores - top_score), axis=-1, keepdims=True))
    weights = jnp.exp(scores - log_total).astype(jnp.bfloat16)
    mixed = jnp.einsum(
        "wbhqk,wbkhd->wbqhd", weights, value_part, preferred_element_type=jnp.float32
    )
    return (mixed.reshape(query_low.shape).astype(jnp.bfloat16), log_total)


def attend_backward(query_low, keyset, key_valid, log_total, grad_mixed):
    scores, query_split, key_part, value_part = split_scores(query_low, keyset, key_valid)
    window_count, local_count = (keyset.shape[0], keyset.shape[1])
    local_width = query_low.shape[2]
    weights = jnp.exp(scores - log_total)
    grad_split = grad_mixed.reshape(query_split.shape)
    grad_weights = jnp.einsum(
        "wbqhd,wbkhd->wbhqk", grad_split, value_part, preferred_element_type=jnp.float32
    )
    delta_sum = jnp.sum(weights * grad_weights, axis=-1, keepdims=True)
    grad_scores = (weights * (grad_weights - delta_sum)).astype(jnp.bfloat16)
    grad_query = jnp.einsum(
        "wbhqk,wbkhd->wbqhd", grad_scores, key_part, preferred_element_type=jnp.float32
    ) * HD ** (-0.5)
    grad_key = jnp.einsum(
        "wbhqk,wbqhd->wbkhd", grad_scores, query_split, preferred_element_type=jnp.float32
    ) * HD ** (-0.5)
    grad_value = jnp.einsum(
        "wbhqk,wbqhd->wbkhd",
        weights.astype(jnp.bfloat16),
        grad_split,
        preferred_element_type=jnp.float32,
    )
    list_shape = (window_count, local_count, keyset.shape[2], BS, local_width)
    kv_grads = jnp.concatenate(
        [grad_key.reshape(list_shape), grad_value.reshape(list_shape)], axis=-1
    )
    return (grad_query.reshape(query_low.shape), kv_grads)


def flatten_all(members):
    return jnp.concatenate([member.reshape(-1) for member in members])


def share_sum(vector):
    return lax.psum_scatter(vector, ("dp", "seq"), scatter_dimension=0, tiled=True)


def spread_body(
    tokens,
    cotangent,
    masked_pos,
    rand_blocks,
    ln1_gain,
    ln1_bias,
    w_query,
    b_query,
    w_key,
    w_value,
    b_value,
    w_out,
    b_out,
    ln2_gain,
    ln2_bias,
    w_inner,
    b_inner,
    w_outer,
    b_outer,
):
    local_rows = tokens.shape[1]
    devices = lax.axis_size("seq")
    position = lax.axis_index("seq")
    block_count = rand_blocks.shape[1]
    local_count = block_count // devices
    capacity = (3 * WIN_MB * local_count + devices - 1) // devices
    gain_one = ln1_gain.astype(jnp.float32)
    bias_one = ln1_bias.astype(jnp.float32)
    gain_two = ln2_gain.astype(jnp.float32)
    bias_two = ln2_bias.astype(jnp.float32)
    row_ids = position * local_rows + jnp.arange(local_rows, dtype=jnp.int32)
    first_block = position * local_count
    outputs = []
    input_grads = []
    totals = None
    for batch_index in range(MB):
        batch_start = batch_index * WIN_MB
        batch_stop = batch_start + WIN_MB
        tokens_now = tokens[batch_start:batch_stop].astype(jnp.float32)
        rand_now = rand_blocks[batch_start:batch_stop]
        routing = build_routing(rand_now, position, devices, local_count, capacity)
        rand_local = lax.dynamic_slice_in_dim(rand_now, first_block, local_count, 1)
        key_valid = list_masks(rand_local, first_block, block_count)
        hidden_one, normed_one, scaled_one = norm_forward(tokens_now, gain_one, bias_one)
        hidden_low = hidden_one.astype(jnp.bfloat16)
        query_low = (row_dot(hidden_low, w_query) + b_query.astype(jnp.float32)).astype(
            jnp.bfloat16
        )
        key_low = row_dot(hidden_low, w_key).astype(jnp.bfloat16)
        value_low = (row_dot(hidden_low, w_value) + b_value.astype(jnp.float32)).astype(
            jnp.bfloat16
        )
        packed = jnp.concatenate([key_low, value_low], axis=2)
        keyset = fetch_blocks(packed, routing, BS)
        mixed_low, log_total = attend_forward(query_low, keyset, key_valid)
        attn_out = lax.psum(row_dot(mixed_low, w_out).astype(jnp.bfloat16), "tensor").astype(
            jnp.float32
        ) + b_out.astype(jnp.float32)
        middle = tokens_now + attn_out
        hidden_two, normed_two, scaled_two = norm_forward(middle, gain_two, bias_two)
        hidden_two_low = hidden_two.astype(jnp.bfloat16)
        inner_pre = row_dot(hidden_two_low, w_inner) + b_inner.astype(jnp.float32)
        active = jax.nn.gelu(inner_pre, approximate=False).astype(jnp.bfloat16)
        ffn_out = lax.psum(row_dot(active, w_outer).astype(jnp.bfloat16), "tensor").astype(
            jnp.float32
        ) + b_outer.astype(jnp.float32)
        outputs.append((middle + ffn_out).astype(jnp.bfloat16))
        masked_now = masked_pos[batch_start:batch_stop]
        chosen = jnp.any(row_ids[None, :, None] == masked_now[:, None, :], axis=2)
        cot_now = cotangent[batch_start:batch_stop]
        grad_top = jnp.where(chosen[:, :, None], cot_now, jnp.zeros_like(cot_now))
        grad_active = back_dot(grad_top, w_outer)
        normal_cdf = 0.5 * (1.0 + lax.erf(inner_pre * inv_root_two))
        density = jnp.exp(-0.5 * inner_pre * inner_pre) * inv_root_two_pi
        grad_inner = (grad_active * (normal_cdf + inner_pre * density)).astype(jnp.bfloat16)
        grad_hidden_two = lax.psum(
            back_dot(grad_inner, w_inner).astype(jnp.bfloat16), "tensor"
        ).astype(jnp.float32)
        grad_middle = grad_top.astype(jnp.float32) + norm_backward(
            grad_hidden_two, gain_two, normed_two, scaled_two
        )
        grad_attn = grad_middle.astype(jnp.bfloat16)
        grad_mixed = back_dot(grad_attn, w_out).astype(jnp.bfloat16)
        keyset_back = fetch_blocks(packed, routing, BS)
        grad_query, kv_grads = attend_backward(
            query_low, keyset_back, key_valid, log_total, grad_mixed
        )
        grad_query = grad_query.astype(jnp.bfloat16)
        grad_packed = return_blocks(kv_grads, routing, BS)
        local_width = query_low.shape[2]
        grad_key = grad_packed[:, :, :local_width].astype(jnp.bfloat16)
        grad_value = grad_packed[:, :, local_width:].astype(jnp.bfloat16)
        grad_partial = (
            back_dot(grad_query, w_query)
            + back_dot(grad_key, w_key)
            + back_dot(grad_value, w_value)
        )
        grad_hidden_one = lax.psum(grad_partial.astype(jnp.bfloat16), "tensor").astype(jnp.float32)
        grad_tokens_now = grad_middle + norm_backward(
            grad_hidden_one, gain_one, normed_one, scaled_one
        )
        input_grads.append(grad_tokens_now.astype(jnp.bfloat16))
        batch_grads = (
            jnp.sum(grad_hidden_one * normed_one, axis=(0, 1)),
            jnp.sum(grad_hidden_one, axis=(0, 1)),
            outer_sum(hidden_low, grad_query),
            column_sum(grad_query),
            outer_sum(hidden_low, grad_key),
            outer_sum(hidden_low, grad_value),
            column_sum(grad_value),
            outer_sum(mixed_low, grad_attn),
            column_sum(grad_attn),
            jnp.sum(grad_hidden_two * normed_two, axis=(0, 1)),
            jnp.sum(grad_hidden_two, axis=(0, 1)),
            outer_sum(hidden_two_low, grad_inner),
            column_sum(grad_inner),
            outer_sum(active, grad_top),
            column_sum(grad_top),
        )
        totals = batch_grads if totals is None else jax.tree.map(jnp.add, totals, batch_grads)
    final_share = share_sum(flatten_all(totals))
    gathered = lax.all_gather(
        final_share.astype(jnp.bfloat16), ("dp", "seq"), axis=0, tiled=True
    ).astype(final_share.dtype)
    param_shapes = [
        member.shape
        for member in (
            ln1_gain,
            ln1_bias,
            w_query,
            b_query,
            w_key,
            w_value,
            b_value,
            w_out,
            b_out,
            ln2_gain,
            ln2_bias,
            w_inner,
            b_inner,
            w_outer,
            b_outer,
        )
    ]
    results = []
    cursor = 0
    for shape_now in param_shapes:
        length = 1
        for extent in shape_now:
            length = length * extent
        results.append(gathered[cursor : cursor + length].reshape(shape_now))
        cursor = cursor + length
    out_all = jnp.concatenate(outputs, axis=0)
    grad_all = jnp.concatenate(input_grads, axis=0)
    return (
        out_all,
        grad_all,
        results[0],
        results[1],
        results[2],
        results[3],
        results[4],
        results[5],
        results[6],
        results[7],
        results[8],
        results[9],
        results[10],
        results[11],
        results[12],
        results[13],
        results[14],
    )


def power_of_two(number):
    return number & (number - 1) == 0


def body(tokens, *rest):
    dp, seq, tensor = (lax.axis_size(axis) for axis in ("dp", "seq", "tensor"))
    fits = seq == tokens.shape[0] and tensor == 2 and dp == 4 and power_of_two(seq)
    return (window_body if fits else spread_body)(tokens, *rest)


def solution(mesh):
    in_specs = (
        P("dp", "seq", None),
        P("dp", "seq", None),
        P("dp", None),
        P("dp", None, None),
        P(),
        P(),
        P(None, "tensor"),
        P("tensor"),
        P(None, "tensor"),
        P(None, "tensor"),
        P("tensor"),
        P("tensor", None),
        P(),
        P(),
        P(),
        P(None, "tensor"),
        P("tensor"),
        P("tensor", None),
        P(),
    )
    out_specs = (
        P("dp", "seq", None),
        P("dp", "seq", None),
        P(),
        P(),
        P(None, "tensor"),
        P("tensor"),
        P(None, "tensor"),
        P(None, "tensor"),
        P("tensor"),
        P("tensor", None),
        P(),
        P(),
        P(),
        P(None, "tensor"),
        P("tensor"),
        P("tensor", None),
        P(),
    )
    return jax.shard_map(body, mesh=mesh, in_specs=in_specs, out_specs=out_specs, check_vma=False)
```

```python
import functools

import jax
import jax.numpy as jnp
from jax import lax
from jax.experimental import pallas as pl
from jax.experimental.pallas import tpu as pltpu
from jax.sharding import PartitionSpec as P

HD = 64
BS = 64
MB = 2
WIN_MB = 2


eps_norm = 1e-05
inv_root_two = 0.7071067811865476
inv_root_two_pi = 0.3989422804014327


LANES = 128
NEG = -1e30
VMEM_LIMIT = 16 * 1024 * 1024


def dot_nn(left, right):
    return lax.dot_general(left, right, (((1,), (0,)), ((), ())), preferred_element_type=jnp.float32)


def dot_nt(left, right):
    return lax.dot_general(left, right, (((1,), (1,)), ((), ())), preferred_element_type=jnp.float32)


def dot_tn(left, right):
    return lax.dot_general(left, right, (((0,), (0,)), ((), ())), preferred_element_type=jnp.float32)


def norm_parts(values):
    center = values - jnp.mean(values, axis=-1, keepdims=True)
    scaled = lax.rsqrt(jnp.mean(center * center, axis=-1, keepdims=True) + eps_norm)
    return center * scaled, scaled


def pick_rows(positions, total):
    ids = lax.broadcasted_iota(jnp.int32, (positions.shape[0], total), 1)
    return jnp.where(ids == positions, 1.0, 0.0).astype(jnp.bfloat16)


def row_lists(blocks, allow):
    ids = lax.broadcasted_iota(jnp.int32, (blocks.shape[0], allow.shape[0]), 1)
    return dot_nn(jnp.where(ids == blocks, 1.0, 0.0).astype(jnp.bfloat16), allow)


def head_half(half):
    lane = lax.broadcasted_iota(jnp.int32, (1, LANES), 1)
    return (lane < HD) if half == 0 else (lane >= HD)


def one_head(slab, half):
    return jnp.where(head_half(half), slab, jnp.zeros_like(slab))


class Order:
    def __init__(self):
        self.last = None
        self.needed = []
        self.later = []

    def soon(self, array, kernels=2):
        self.later.append([kernels, array])

    def need(self, *arrays):
        self.needed += arrays

    def call(self, kernel, name, outs, args, smem=1, scratch=(), aliases=None):
        first = args[0]
        for entry in self.later:
            entry[0] -= 1
        self.needed += [array for left, array in self.later if left == 0]
        self.later = [entry for entry in self.later if entry[0] > 0]
        if self.last is not None:
            first = after(first, self.last, *self.needed)
            self.needed = []
        spec = pl.BlockSpec(memory_space=pltpu.VMEM)
        found = pl.pallas_call(
            kernel,
            name=name,
            out_shape=outs,
            in_specs=[pl.BlockSpec(memory_space=pltpu.SMEM)] * smem + [spec] * (len(args) - smem),
            out_specs=[spec] * len(outs),
            scratch_shapes=list(scratch),
            input_output_aliases=aliases or {},
            compiler_params=pltpu.CompilerParams(vmem_limit_bytes=VMEM_LIMIT),
            cost_estimate=pl.CostEstimate(flops=1, bytes_accessed=1, transcendentals=0),
        )(first, *args[1:])
        self.last = min(found, key=lambda a: a.size)
        return found


def after(value, *others):
    return lax.optimization_barrier((value, others))[0]


def shape(dims, dtype=jnp.bfloat16):
    return jax.ShapeDtypeStruct(dims, dtype)


def shard_kernel(at, bits, own, other, vec, wq, wk, wv, *rest):
    tok, h, q, k, v = rest[-5:]
    run = own.shape[0]
    local = wq.shape[1]
    first = bits[2] == 0
    tok[pl.ds(2 * at * run, run), :] = jnp.where(first, own[...], other[...])
    tok[pl.ds((2 * at + 1) * run, run), :] = jnp.where(first, other[...], own[...])
    rows = pl.ds(2 * at * run, 2 * run)
    normed, _ = norm_parts(tok[rows, :].astype(jnp.float32))
    low = (normed * vec[0:1, :] + vec[1:2, :]).astype(jnp.bfloat16)
    h[rows, :] = low
    q[rows, :] = (dot_nn(low, wq[...]) + vec[6:7, :local]).astype(jnp.bfloat16)
    k[rows, :] = dot_nn(low, wk[...]).astype(jnp.bfloat16)
    v[rows, :] = (dot_nn(low, wv[...]) + vec[6:7, local:]).astype(jnp.bfloat16)


def sum_rows_kernel(bits, *refs):
    total = None
    for piece in refs[:-1]:
        value = piece[...].astype(jnp.float32)
        total = value if total is None else total + value
    refs[-1][...] = total.astype(jnp.bfloat16)


def front_kernel(bits, pos, allow, wo, tok, h, q, k, v, xm, hm, qm, om, lse, part):
    total, local = q.shape
    pick = pick_rows(pos[...], total)
    xm[...] = dot_nn(pick, tok[...]).astype(jnp.bfloat16)
    hm[...] = dot_nn(pick, h[...]).astype(jnp.bfloat16)
    qm[...] = dot_nn(pick, q[...]).astype(jnp.bfloat16)
    listed = row_lists(pos[...] >> 6, allow[...]) > 0.5
    lane = lax.broadcasted_iota(jnp.int32, (pos.shape[0], LANES), 1)

    def one_slab(slab, sums):
        cols = pl.ds(pl.multiple_of(slab * LANES, LANES), LANES)
        query = (qm[:, cols].astype(jnp.float32) * HD ** (-0.5)).astype(jnp.bfloat16)
        mixed = None
        for half in range(2):
            scores = jnp.where(listed, dot_nt(one_head(query, half), k[:, cols]), NEG)
            top = jnp.max(scores, axis=-1, keepdims=True)
            weight = jnp.exp(scores - top)
            total_weight = jnp.sum(weight, axis=-1, keepdims=True)
            sums = jnp.where(lane == 2 * slab + half, top + jnp.log(total_weight), sums)
            found = dot_nn(weight.astype(jnp.bfloat16), v[:, cols]) * (1.0 / total_weight)
            mixed = found if half == 0 else jnp.where(head_half(0), mixed, found)
        om[:, cols] = mixed.astype(jnp.bfloat16)
        return sums

    none = jnp.zeros((pos.shape[0], LANES), jnp.float32)
    sums = lax.fori_loop(0, local // LANES, one_slab, none)
    lse[...] = sums
    part[...] = dot_nn(om[...], wo[...]).astype(jnp.bfloat16)


def gelu_parts(z):
    cdf = 0.5 * (1.0 + lax.erf(z * inv_root_two))
    return z * cdf, cdf + z * (jnp.exp(-0.5 * z * z) * inv_root_two_pi)


def middle_of(xm, part, other, vec):
    both = part[...].astype(jnp.float32) + other[...].astype(jnp.float32)
    return xm[...].astype(jnp.float32) + (both + vec[2:3, :])


def hidden_kernel(
    bits, xm, part, other, g_own, g_other, vec, wi, wf,
    wf_a, wf_as, wf_b, wf_bs, wi_a, wi_as, wi_b, wi_bs, dh2, few, g,
    u_all, h2_all, dz_all,
):
    width, hidden = wi.shape
    split = width // 2
    first = bits[2] == 0
    g[:, :split] = jnp.where(first, g_own[...], g_other[...])
    g[:, split:] = jnp.where(first, g_other[...], g_own[...])
    normed, _ = norm_parts(middle_of(xm, part, other, vec))
    h2_all[...] = (normed * vec[3:4, :] + vec[4:5, :]).astype(jnp.bfloat16)
    h2 = h2_all[...]
    for at in range(hidden // width):
        cols = pl.ds(at * width, width)
        z = dot_nn(h2, wi[:, cols]) + vec[7 + at : 8 + at, :]
        act, slope = gelu_parts(z)
        u_all[:, cols] = act.astype(jnp.bfloat16)
        dz = (dot_nt(g[...], wf[cols, :]) * slope).astype(jnp.bfloat16)
        dz_all[:, cols] = dz
        few[1 + at : 2 + at, :] = jnp.sum(dz.astype(jnp.float32), axis=0, keepdims=True)
    few[0:1, :] = jnp.sum(g[...].astype(jnp.float32), axis=0, keepdims=True)
    half = hidden // 2
    count = width // 2
    for order, keep, send in ((0, wf_a, wf_as), (1, wf_b, wf_bs)):
        for out, bit in ((keep, bits[order]), (send, 1 - bits[order])):
            at = pl.multiple_of(order * half + bit * count, LANES)
            out[0] = dot_tn(u_all[:, pl.ds(at, count)], g[...]).astype(jnp.bfloat16)
    for order, keep, send in ((0, wi_a, wi_as), (1, wi_b, wi_bs)):
        for out, bit in ((keep, bits[order]), (send, 1 - bits[order])):
            at = pl.multiple_of(bit * count, LANES)
            out[0] = dot_tn(
                h2_all[:, pl.ds(at, count)], dz_all[:, pl.ds(order * half, half)]
            ).astype(jnp.bfloat16)
    dh2[...] = dot_nt(dz_all[...], wi[...]).astype(jnp.bfloat16)


def attend_back_kernel(
    bits, xm, part, other, g, dh2, dh2_other, vec, wo, pos, allow, qm, om, hm, lse, h, k, v,
    da_a, da_as, da_b, da_bs, dx1, dq, dk, dv, few, da_all, do_all,
):
    width = g.shape[1]
    normed, scaled = norm_parts(middle_of(xm, part, other, vec))
    up = dh2[...].astype(jnp.float32) + dh2_other[...].astype(jnp.float32)
    few[0:1, :] = jnp.sum(up * normed, axis=0, keepdims=True)
    few[1:2, :] = jnp.sum(up, axis=0, keepdims=True)
    weighted = up * vec[3:4, :]
    centered = weighted - jnp.mean(weighted, axis=-1, keepdims=True)
    slope = jnp.mean(weighted * normed, axis=-1, keepdims=True)
    grad = g[...].astype(jnp.float32) + scaled * (centered - normed * slope)
    dx1[...] = grad
    low = grad.astype(jnp.bfloat16)
    da_all[...] = low
    few[2:3, :] = jnp.sum(low.astype(jnp.float32), axis=0, keepdims=True)
    do_all[...] = dot_nt(low, wo[...]).astype(jnp.bfloat16)
    listed = row_lists(pos[...] >> 6, allow[...]) > 0.5
    for slab in range(qm.shape[1] // LANES):
        cols = pl.ds(slab * LANES, LANES)
        query = (qm[:, cols].astype(jnp.float32) * HD ** (-0.5)).astype(jnp.bfloat16)
        grad_q, grad_k, grad_v = None, None, None
        for half in range(2):
            at = 2 * slab + half
            own = one_head(query, half)
            own_do = one_head(do_all[:, cols], half)
            scores = jnp.where(listed, dot_nt(own, k[:, cols]), NEG)
            prob = jnp.exp(scores - lse[:, at : at + 1])
            grad_p = dot_nt(own_do, v[:, cols])
            delta = jnp.sum(prob * grad_p, axis=-1, keepdims=True)
            ds = (prob * (grad_p - delta)).astype(jnp.bfloat16)
            found_q = dot_nn(ds, k[:, cols])
            found_k = dot_tn(ds, own)
            found_v = dot_tn(prob.astype(jnp.bfloat16), own_do)
            grad_q = found_q if half == 0 else jnp.where(head_half(0), grad_q, found_q)
            grad_k = found_k if half == 0 else grad_k + found_k
            grad_v = found_v if half == 0 else grad_v + found_v
        dq[:, cols] = (grad_q * HD ** (-0.5)).astype(jnp.bfloat16)
        dk[:, cols] = grad_k.astype(jnp.bfloat16)
        dv[:, cols] = grad_v.astype(jnp.bfloat16)
    local = qm.shape[1]
    few[3:4, :local] = jnp.sum(dq[...].astype(jnp.float32), axis=0, keepdims=True)
    few[3:4, local:] = jnp.sum(dv[...].astype(jnp.float32), axis=0, keepdims=True)
    count = width // 2
    for keep, bit in ((da_a, bits[0]), (da_as, 1 - bits[0])):
        cols = pl.ds(pl.multiple_of(bit * count, LANES), count)
        keep[0, :, :local] = dot_tn(hm[:, cols], dq[...]).astype(jnp.bfloat16)
        keep[0, :, local:] = dot_tn(h[:, cols], dk[...]).astype(jnp.bfloat16)
    for keep, bit in ((da_b, bits[1]), (da_bs, 1 - bits[1])):
        cols = pl.ds(pl.multiple_of(bit * count, LANES), count)
        keep[0, :, :local] = dot_tn(h[:, cols], dv[...]).astype(jnp.bfloat16)
        keep[0, :, local:] = dot_tn(om[...], da_all[:, cols]).astype(jnp.bfloat16)


def input_kernel(bits, pos, dq, dk, dv, wq, wk, wv, keep, *rest):
    sends, dq_all = rest[:-1], rest[-1]
    total = dk.shape[0]
    dq_all[...] = dot_tn(pick_rows(pos[...], total), dq[...]).astype(jnp.bfloat16)
    run = BS * 2
    for at in range(0, total // (2 * run)):
        own = keep.at[pl.ds(at * run, run), :]
        sent = sends[0].at[pl.ds(at * run, run), :]
        for out, bit in ((own, bits[2]), (sent, 1 - bits[2])):
            rows = pl.ds(pl.multiple_of(at * 2 * run + bit * run, run), run)
            out[...] = (
                dot_nt(dq_all[rows, :], wq[...])
                + dot_nt(dk[rows, :], wk[...])
                + dot_nt(dv[rows, :], wv[...])
            ).astype(jnp.bfloat16)


def first_norm_kernel(count, bits, pos_half, own, dx1, vec, *rest):
    toks, others, grads = rest[:count], rest[count : -3 - count], rest[-3 - count : -3]
    few, tok, other = rest[-3:]
    run = others[0].shape[0]
    for at, piece in enumerate(others):
        other[pl.ds(at * run, run), :] = piece[...]
    run = toks[0].shape[0]
    for at, piece in enumerate(toks):
        tok[pl.ds(at * run, run), :] = piece[...]
    normed, scaled = norm_parts(tok[...].astype(jnp.float32))
    up = own[...].astype(jnp.float32) + other[...].astype(jnp.float32)
    few[0:1, :] = jnp.sum(up * normed, axis=0, keepdims=True)
    few[1:2, :] = jnp.sum(up, axis=0, keepdims=True)
    weighted = up * vec[0:1, :]
    centered = weighted - jnp.mean(weighted, axis=-1, keepdims=True)
    slope = jnp.mean(weighted * normed, axis=-1, keepdims=True)
    pick = pick_rows(pos_half[...], tok.shape[0])
    high = dx1[...].astype(jnp.bfloat16)
    rest = (dx1[...] - high.astype(jnp.float32)).astype(jnp.bfloat16)
    through = dot_tn(pick, high) + dot_tn(pick, rest)
    grad = (through + scaled * (centered - normed * slope)).astype(jnp.bfloat16)
    for at, piece in enumerate(grads):
        piece[0] = grad[at * run : (at + 1) * run, :]


def attend_kernel(at, bits, q, k, v, allow, *refs):
    keep, send, mixed_all = refs[-3:]
    tile = mixed_all.shape[0]
    run = tile // 2
    rows = pl.ds(at * tile, tile)
    ids = lax.broadcasted_iota(jnp.int32, (tile, 1), 0)
    bias = (row_lists(at * (tile // BS) + (ids >> 6), allow[...]) - 1.0) * -NEG

    def one_slab(slab, carry):
        cols = pl.ds(pl.multiple_of(slab * LANES, LANES), LANES)
        query = (q[rows, cols].astype(jnp.float32) * HD ** (-0.5)).astype(jnp.bfloat16)
        mixed = None
        for half in range(2):
            scores = dot_nt(one_head(query, half), k[:, cols]) + bias
            weight = jnp.exp(scores - jnp.max(scores, axis=-1, keepdims=True))
            total_weight = jnp.sum(weight, axis=-1, keepdims=True)
            found = dot_nn(weight.astype(jnp.bfloat16), v[:, cols]) * (1.0 / total_weight)
            mixed = found if half == 0 else jnp.where(head_half(0), mixed, found)
        mixed_all[:, cols] = mixed.astype(jnp.bfloat16)
        return carry

    lax.fori_loop(0, q.shape[1] // LANES, one_slab, 0)
    for out, bit in ((keep, bits[2]), (send, 1 - bits[2])):
        out[pl.ds(at * run, run), :] = mixed_all[pl.ds(pl.multiple_of(bit * run, run), run), :]


def feed_kernel(base, count, bits, *refs):
    toks, refs = refs[:count], refs[count:]
    own, other, vec, bi_other, wo, wo_other, wi, wi_other, wf, wf_other = refs[:10]
    outs, mid_all = refs[-1 - count : -1], refs[-1]
    width, hidden = wi.shape
    run = toks[0].shape[0]
    rows = pl.ds(base * run, count * run)
    mid_all[...] = dot_nn(own[rows, :], wo[...]) + dot_nn(other[rows, :], wo_other[...])
    for at in range(count):
        piece = pl.ds(at * run, run)
        mid_all[piece, :] = toks[at][...].astype(jnp.float32) + (mid_all[piece, :] + vec[2:3, :])
    middle = mid_all[...]
    normed, _ = norm_parts(middle)
    h2 = (normed * vec[3:4, :] + vec[4:5, :]).astype(jnp.bfloat16)
    total = middle + vec[5:6, :]
    for row, bias, inner, outer in ((7, vec, wi, wf), (0, bi_other, wi_other, wf_other)):
        for at in range(hidden // width):
            cols = pl.ds(at * width, width)
            z = dot_nn(h2, inner[:, cols]) + bias[row + at : row + at + 1, :]
            act = z * (0.5 * (1.0 + lax.erf(z * inv_root_two)))
            total = total + dot_nn(act.astype(jnp.bfloat16), outer[cols, :])
    low = total.astype(jnp.bfloat16)
    for at in range(count):
        outs[at][1] = low[at * run : (at + 1) * run, :]


def gather_small_kernel(bits, first, first_other, attend, hidden, out):
    out[0:2, :] = first[...] + first_other[...]
    out[2:6, :] = attend[...]
    out[6:, :] = hidden[...]


def add_small_kernel(bits, own, other, out):
    out[...] = own[...] + other[...]


def interleave_kernel(bits, *refs):
    count = (len(refs) - 2) // 2
    own, over, outs = refs[:count], refs[count : 2 * count], refs[2 * count :]
    run = own[0].shape[1]
    for at in range(count):
        window = bits[5] ^ at
        for which, out in enumerate(outs):
            for pieces, side in ((own, bits[2]), (over, 1 - bits[2])):
                rows = pl.ds(pl.multiple_of(side * run, run), run)
                out[window, rows, :] = pieces[at][which]


def add_low(left, right):
    return (left.astype(jnp.float32) + right.astype(jnp.float32)).astype(jnp.bfloat16)


def part_rows(bit, count):
    return pl.ds(pl.multiple_of(bit * count, 16), count)


def halve_plane_kernel(at, bits, ka, ra, kb, rb, keep_a, send_a, keep_b, send_b):
    count = keep_a.shape[1]
    groups = ((ka, ra, keep_a, send_a, bits[at[0]]), (kb, rb, keep_b, send_b, bits[at[1]]))
    for k, r, keep, send, bit in groups:
        for out, side in ((keep, bit), (send, 1 - bit)):
            rows = part_rows(side, count)
            out[...] = add_low(k[:, rows, :], r[:, rows, :])


def halve_join_kernel(at, bits, ka, ra, kb, rb, keep, send):
    group, count = ka.shape[0], keep.shape[1]
    for out, side in ((keep, bits[at]), (send, 1 - bits[at])):
        rows = part_rows(side, count)
        out[:group] = add_low(ka[:, rows, :], ra[:, rows, :])
        out[group:] = add_low(kb[:, rows, :], rb[:, rows, :])


def halve_line_kernel(at, bits, k, r, keep, send):
    count = keep.shape[1]
    for out, side in ((keep, bits[at]), (send, 1 - bits[at])):
        rows = part_rows(side, count)
        out[...] = add_low(k[:, rows, :], r[:, rows, :])


def last_line_kernel(bits, k, r, out):
    out[...] = add_low(k[...], r[...])


def double_line_kernel(at, bits, own, other, out):
    count = own.shape[1]
    out[:, part_rows(bits[at], count), :] = own[...]
    out[:, part_rows(1 - bits[at], count), :] = other[...]


def double_split_kernel(at, bits, own, other, out_a, out_b):
    count = own.shape[1]
    group = out_a.shape[0]
    for which, out in ((0, out_a), (1, out_b)):
        part = pl.ds(which * group, group)
        out[:, part_rows(bits[at], count), :] = own[part]
        out[:, part_rows(1 - bits[at], count), :] = other[part]


def double_plane_kernel(at, bits, own_a, other_a, own_b, other_b, out_a, out_b):
    groups = ((own_a, other_a, out_a, bits[at[0]]), (own_b, other_b, out_b, bits[at[1]]))
    for own, other, out, bit in groups:
        count = own.shape[1]
        out[:, part_rows(bit, count), :] = own[...]
        out[:, part_rows(1 - bit, count), :] = other[...]


def last_rows_kernel(at, bits, own_a, other_a, own_b, other_b, out):
    count = own_a.shape[1]
    groups = ((own_a, other_a, bits[at[0]]), (own_b, other_b, bits[at[1]]))
    for which, (own, other, bit) in enumerate(groups):
        for value, side in ((own, bit), (other, 1 - bit)):
            out[part_rows(2 * which + side, count), :] = value[0].astype(jnp.float32)


def last_columns_kernel(at, bits, own_a, other_a, own_b, other_b, out):
    count, width = own_a.shape[1:]
    groups = ((own_a, other_a, bits[at[0]]), (own_b, other_b, bits[at[1]]))
    for which, (own, other, bit) in enumerate(groups):
        for value, side in ((own, bit), (other, 1 - bit)):
            out[part_rows(side, count), pl.ds(which * width, width)] = value[0].astype(
                jnp.float32
            )


def last_attend_kernel(
    at, bits, own_a, other_a, own_b, other_b, grad_q, grad_k, grad_v, grad_o
):
    count = own_a.shape[1]
    local = grad_q.shape[1]
    for value, side in ((own_a, bits[at[0]]), (other_a, 1 - bits[at[0]])):
        grad_q[part_rows(side, count), :] = value[0, :, :local].astype(jnp.float32)
        grad_k[part_rows(side, count), :] = value[0, :, local:].astype(jnp.float32)
    for value, side in ((own_b, bits[at[1]]), (other_b, 1 - bits[at[1]])):
        grad_v[part_rows(side, count), :] = value[0, :, :local].astype(jnp.float32)
        cols = pl.ds(pl.multiple_of(side * count, LANES), count)
        grad_o[:, cols] = value[0, :, local:].astype(jnp.float32)


def joined_size(piece):
    group, rows, width = piece.shape
    return shape((group, 2 * rows, width))


def halved_size(piece):
    group, rows, width = piece.shape
    return shape((group, rows // 2, width))


def flip(value, axis, bit):
    return lax.ppermute(value, axis, [(i, i ^ bit) for i in range(lax.axis_size(axis))])


def bit_of(axis, bit):
    return jnp.where((lax.axis_index(axis) & bit) != 0, 1, 0).astype(jnp.int32)


def stages_of(order):
    dp_bits = [("dp", 1 << i) for i in range(lax.axis_size("dp").bit_length() - 1)]
    seq_bits = [("seq", 1 << i) for i in range(lax.axis_size("seq").bit_length() - 1)]
    return (dp_bits if order == 0 else dp_bits[::-1]) + seq_bits


class Summing:
    def __init__(self, order, bits, keep, send):
        self.order, self.bits = order, bits
        self.keep, self.send = list(keep), list(send)
        self.plane = [stages_of(which)[:2] for which in range(2)]
        self.line = stages_of(0)[2:]

    def hold(self, *others):
        self.send = [after(value, *others) for value in self.send]

    def exchange(self, at):
        self.got = [flip(s, *self.plane[which][at]) for which, s in enumerate(self.send)]
        return self.got

    def exchange_line(self, at):
        return flip(self.send, *self.line[at])

    def halve_first(self):
        other = self.got
        ka, sa, kb, sb = self.order.call(
            functools.partial(halve_plane_kernel, (1, 0)),
            "halve_plane",
            [halved_size(self.keep[0])] * 4,
            (self.bits, self.keep[0], other[0], self.keep[1], other[1]),
        )
        self.keep, self.send = [ka, kb], [sa, sb]

    def halve_second(self):
        other = self.got
        group, rows, width = self.keep[0].shape
        self.keep, self.send = self.order.call(
            functools.partial(halve_join_kernel, 3),
            "halve_join",
            [shape((2 * group, rows // 2, width))] * 2,
            (self.bits, self.keep[0], other[0], self.keep[1], other[1]),
        )

    def halve_line(self, at, other):
        two, rows, width = self.keep.shape
        if at + 1 < len(self.line):
            self.keep, self.send = self.order.call(
                functools.partial(halve_line_kernel, 4 + at),
                "halve_line",
                [shape((two, rows // 2, width))] * 2,
                (self.bits, self.keep, other),
            )
        else:
            (self.send,) = self.order.call(
                last_line_kernel, "last_line", [shape(self.keep.shape)], (self.bits, self.keep, other)
            )

    def double_line(self, at, other):
        two, rows, width = self.send.shape
        if at > 0:
            (self.send,) = self.order.call(
                functools.partial(double_line_kernel, 3 + at),
                "double_line",
                [shape((two, 2 * rows, width))],
                (self.bits, self.send, other),
            )
        else:
            self.send = self.order.call(
                functools.partial(double_split_kernel, 3 + at),
                "double_split",
                [shape((two // 2, 2 * rows, width))] * 2,
                (self.bits, self.send, other),
            )

    def double_second(self):
        other = self.got
        self.send = self.order.call(
            functools.partial(double_plane_kernel, (1, 0)),
            "double_plane",
            [joined_size(self.send[0])] * 2,
            (self.bits, self.send[0], other[0], self.send[1], other[1]),
        )

    def write(self, kernel, outs):
        return self.order.call(
            functools.partial(kernel, (0, 1)),
            "last",
            [shape(dims, jnp.float32) for dims in outs],
            (self.bits, self.send[0], self.got[0], self.send[1], self.got[1]),
        )


STEPS = (
    "i.go", "I.0", "W.wf", "f.h1", "W.wi", "f.h2", "A.0", "f.l0", "i.h1", "a.go", "W.wo",
    "i.h2", "A.1", "A.2", "i.l0", "f.l1", "A.3", "i.l1", "a.h1", "W.bi", "X.0", "f.d1", "N.0",
    "a.h2", "f.d0", "F.0", "a.l0", "S.0", "i.d1", "f.e2", "F.1", "i.d0", "a.l1", "f.wr",
    "i.e2", "S.1", "a.d1", "a.d0", "S.2", "i.wr", "S.3", "R.1", "R.3", "a.e2", "R.2", "Q.0",
    "Q.1", "Q.2", "Q.3", "a.wr", "S.4", "L.all",
)


def window_body(
    tokens, cotangent, masked_pos, rand_blocks, ln1_gain, ln1_bias, w_query, b_query, w_key,
    w_value, b_value, w_out, b_out, ln2_gain, ln2_bias, w_inner, b_inner, w_outer, b_outer,
):
    windows, rows, width = tokens.shape
    local = w_query.shape[1]
    hidden = w_inner.shape[1]
    total = windows * rows
    blocks = total // BS
    run = rows // 2
    split = width // 2
    place = lax.axis_index("seq")
    core = lax.axis_index("tensor")
    plane, line = stages_of(0)[:2], stages_of(0)[2:]
    bits = jnp.stack(
        [bit_of(*step) for step in plane]
        + [core.astype(jnp.int32)]
        + [bit_of(*step) for step in line]
        + [place.astype(jnp.int32)]
    )

    cut = tokens.reshape(windows, 2, run, width)
    own_rows = []
    for at in range(windows):
        piece = lax.dynamic_slice(cut, (place ^ at, core, 0, 0), (1, 1, run, width))
        piece = piece.reshape(run, width)
        own_rows.append(piece if at == 0 else flip(piece, "seq", at))

    named = masked_pos.shape[1]
    count = -(-named // 16) * 16
    spots = jnp.concatenate(
        [masked_pos, jnp.full((windows, count - named), -1, jnp.int32)], axis=1
    )
    slot = jnp.arange(count, dtype=jnp.int32)
    again = jnp.any(
        (spots[:, :, None] == spots[:, None, :]) & (slot[None, :] < slot[:, None])[None], axis=2
    )
    spots = jnp.where(again, -1, spots)
    spot = lax.dynamic_index_in_dim(spots, place, 0, keepdims=True).reshape(count, 1)
    there, inside = (spot // rows) ^ place, spot % rows
    pos = jnp.where(spot >= 0, there * rows + inside, -1)
    mine = (spot >= 0) & (inside // run == core)
    pos_half = jnp.where(mine, there * run + inside % run, -1)

    here = spots - place * rows
    found = []
    for at in range(windows):
        named_rows = lax.dynamic_index_in_dim(here, place ^ at, 0, keepdims=False)
        pick = (named_rows[:, None] == jnp.arange(rows, dtype=jnp.int32)[None, :]).astype(
            jnp.bfloat16
        )
        shard = lax.dynamic_slice(
            cotangent, (place ^ at, 0, core * split), (1, rows, split)
        ).reshape(rows, split)
        found.append(dot_nn(pick, shard).astype(jnp.bfloat16))

    rand = lax.dynamic_index_in_dim(rand_blocks, place, 0, keepdims=False)
    numbers = jnp.arange(blocks, dtype=jnp.int32)
    shard_blocks = rows // BS
    ids = ((numbers // shard_blocks) ^ place) * shard_blocks + numbers % shard_blocks
    named_blocks = jnp.any(rand[:, :, None] == ids[None, None, :], axis=1)
    named_blocks = jnp.any(
        (ids[:, None] == numbers[None, :])[:, :, None] & named_blocks[None], axis=1
    )
    listed = (
        (jnp.abs(ids[:, None] - ids[None, :]) <= 1)
        | (ids == 0)[None, :]
        | (ids == blocks - 1)[None, :]
        | named_blocks
    )
    allow = jnp.repeat(listed.astype(jnp.bfloat16), BS, axis=1)

    rows_wide = [ln1_gain, ln1_bias, b_out, ln2_gain, ln2_bias, b_outer, b_query, b_value, b_inner]
    vec = jnp.concatenate([x.astype(jnp.float32) for x in rows_wide]).reshape(-1, width)

    order = Order()
    state = None
    for at in range(windows):
        if at == 1:
            order.need(pos, pos_half, allow, *own_rows[1:], *found)
        kept = () if state is None else tuple(state)
        over = own_rows[at] if at == 0 else after(own_rows[at], entry)
        state = order.call(
            functools.partial(shard_kernel, at),
            "shard",
            [shape((total, width))] * 2 + [shape((total, local))] * 3,
            (bits, own_rows[at], flip(over, "tensor", 1), vec, w_query, w_key, w_value) + kept,
            aliases={7 + i: i for i in range(len(kept))},
        )
        if at == 0:
            entry = order.last
    tok, h, q, k, v = state
    found = [found[0]] + [
        flip(after(found[i], *own_rows[1:]), "seq", i) for i in range(1, windows)
    ]
    xm, hm, qm, om, lse, part = order.call(
        front_kernel,
        "front",
        [shape((count, width))] * 2
        + [shape((count, local))] * 2
        + [shape((count, LANES), jnp.float32), shape((count, width))],
        (bits, pos, allow, w_out, tok, h, q, k, v),
    )
    other = flip(part, "tensor", 1)
    (g_own,) = order.call(sum_rows_kernel, "sum_rows", [shape((count, split))], (bits, *found))
    g_other = flip(g_own, "tensor", 1)
    outs = order.call(
        hidden_kernel,
        "hidden",
        [shape((1, width // 2, width))] * 8
        + [shape((count, width)), shape((1 + hidden // width, width), jnp.float32)]
        + [shape((count, width))],
        (bits, xm, part, other, g_own, g_other, vec, w_inner, w_outer),
        scratch=[
            pltpu.VMEM((count, hidden), jnp.bfloat16),
            pltpu.VMEM((count, width), jnp.bfloat16),
            pltpu.VMEM((count, hidden), jnp.bfloat16),
        ],
    )
    wf_a, wf_as, wf_b, wf_bs, wi_a, wi_as, wi_b, wi_bs, dh2, few_hidden, g = outs
    sum_f = Summing(order, bits, (wf_a, wf_b), (wf_as, wf_bs))
    sum_i = Summing(order, bits, (wi_a, wi_b), (wi_as, wi_bs))

    held = {}
    sum_f.exchange(0)
    dh2_other = flip(dh2, "tensor", 1)
    outs = order.call(
        attend_back_kernel,
        "attend_back",
        [shape((1, width // 2, 2 * local))] * 2
        + [shape((1, width // 2, local + width // 2))] * 2
        + [shape((count, width), jnp.float32), shape((count, local))]
        + [shape((total, local))] * 2
        + [shape((4, width), jnp.float32)],
        (bits, xm, part, other, g, dh2, dh2_other, vec, w_out, pos, allow)
        + (qm, om, hm, lse, h, k, v),
        scratch=[
            pltpu.VMEM((count, width), jnp.bfloat16),
            pltpu.VMEM((count, local), jnp.bfloat16),
        ],
    )
    da_a, da_as, da_b, da_bs, dx1, dq, dk, dv, few_attend = outs
    sum_a = Summing(order, bits, (da_a, da_b), (da_as, da_bs))

    def attend(at):
        kept = held.get("mixed", ())
        held["mixed"] = order.call(
            functools.partial(attend_kernel, at),
            "attend",
            [shape((windows * run, local))] * 2,
            (bits, q, k, v, allow, *kept),
            scratch=[pltpu.VMEM((rows, local), jnp.bfloat16)],
            aliases={5 + i: i for i in range(len(kept))},
        )

    def feed(base, pieces):
        span = slice(base, base + pieces)
        held["pair"][span] = order.call(
            functools.partial(feed_kernel, base, pieces),
            "feed",
            [shape((2, run, width))] * pieces,
            (bits, *own_rows[span], held["mixed"][0], held["mixed_other"], vec, held["bi"], w_out)
            + (held["wo"], w_inner, held["wi"], w_outer, held["wf"], *held["pair"][span]),
            scratch=[pltpu.VMEM((pieces * run, width), jnp.float32)],
            aliases={11 + pieces + i: i for i in range(pieces)},
        )

    small_steps = iter(stages_of(0)[::-1])
    sums = {"f": sum_f, "i": sum_i, "a": sum_a}

    def swap(value, kernels=2):
        other = flip(after(value, order.last), "tensor", 1)
        order.soon(other, kernels)
        return other

    def sum_step(of, step):
        one = sums[of]
        if step == "go":
            one.hold(order.last)
            one.exchange(0)
        elif step == "h1":
            one.halve_first()
            one.exchange(1)
        elif step == "h2":
            one.halve_second()
            held[of] = one.exchange_line(0)
        elif step == "l0":
            one.halve_line(0, held[of])
            held[of] = one.exchange_line(1)
        elif step == "l1":
            one.halve_line(1, held[of])
            held[of] = one.exchange_line(1)
        elif step == "d1":
            one.double_line(1, held[of])
            held[of] = one.exchange_line(0)
        elif step == "d0":
            one.double_line(0, held[of])
            one.exchange(1)
        elif step == "e2":
            one.double_second()
            one.exchange(0)
        elif of == "f":
            (held["grad_wf"],) = one.write(last_rows_kernel, [(hidden, width)])
        elif of == "i":
            (held["grad_wi"],) = one.write(last_columns_kernel, [(width, hidden)])
        else:
            held["grad_a"] = one.write(last_attend_kernel, [(width, local)] * 3 + [(local, width)])

    def input_grad():
        held["dh_own"], dh_send = order.call(
            input_kernel,
            "input_grad",
            [shape((total // 2, width))] * 2,
            (bits, pos, dq, dk, dv, w_query, w_key, w_value),
            scratch=[pltpu.VMEM((total, local), jnp.bfloat16)],
        )
        held["dh_other"] = flip(dh_send, "tensor", 1)

    def first_norm():
        *held["pair"], held["few"] = order.call(
            functools.partial(first_norm_kernel, windows),
            "first_norm",
            [shape((2, run, width))] * windows + [shape((2, width), jnp.float32)],
            (bits, pos_half, held["dh_own"], dx1, vec, *own_rows, held["dh_other"]),
            scratch=[pltpu.VMEM((total // 2, width), jnp.bfloat16)] * 2,
        )
        held["few_other"] = flip(held["few"], "tensor", 1)
        order.soon(held["few_other"])

    def small(step):
        if step == "0":
            (held["small"],) = order.call(
                gather_small_kernel,
                "gather_small",
                [shape((7 + hidden // width, width), jnp.float32)],
                (bits, held["few"], held["few_other"], few_attend, few_hidden),
            )
        else:
            (held["small"],) = order.call(
                add_small_kernel,
                "add_small",
                [shape(held["small"].shape, jnp.float32)],
                (bits, held["small"], held["small_other"]),
            )
        if step != "4":
            held["small_other"] = flip(held["small"], *next(small_steps))

    def send_back(at):
        held["pair"][at] = flip(after(held["pair"][at], order.last), "seq", at)
        order.soon(held["pair"][at], 3)

    def swap_back(at):
        held.setdefault("over", {})[at] = swap(held["pair"][at])

    def interleave():
        over = [held["over"][at] for at in range(windows)]
        held["all"] = order.call(
            interleave_kernel,
            "interleave",
            [shape((windows, rows, width))] * 2,
            (bits, *held["pair"], *over),
        )

    for step in STEPS:
        kind, what = step[0], step[2:]
        if kind in sums:
            sum_step(kind, what)
        elif kind == "A":
            attend(int(what))
        elif kind == "F":
            feed(int(what) * windows // 2, windows // 2)
        elif kind == "W":
            held[what] = swap({"wi": w_inner, "wf": w_outer, "wo": w_out, "bi": vec[7:]}[what])
        elif kind == "X":
            held["mixed_other"] = swap(held["mixed"][1])
        elif kind == "S":
            small(what)
        elif kind == "R":
            send_back(int(what))
        elif kind == "Q":
            swap_back(int(what))
        elif kind == "L":
            interleave()
        elif kind == "I":
            input_grad()
        else:
            first_norm()
    grad_tokens, out = held["all"]
    grad_q, grad_k, grad_v, grad_o = held["grad_a"]
    grad_wf, grad_wi, small_all = held["grad_wf"], held["grad_wi"], held["small"]
    return (
        out,
        grad_tokens,
        small_all[0],
        small_all[1],
        grad_q,
        small_all[5, :local],
        grad_k,
        grad_v,
        small_all[5, local:],
        grad_o,
        small_all[4],
        small_all[2],
        small_all[3],
        grad_wi,
        small_all[7:].reshape(-1),
        grad_wf,
        small_all[6],
    )


def with_halo(block, sides, width):
    for axis, dim in sides:
        count = lax.axis_size(axis)
        forward = [(i, i + 1) for i in range(count - 1)]
        backward = [(target, source) for source, target in forward]
        low = lax.ppermute(
            lax.slice_in_dim(block, block.shape[dim] - width, None, axis=dim), axis, forward
        )
        high = lax.ppermute(lax.slice_in_dim(block, 0, width, axis=dim), axis, backward)
        block = jnp.concatenate([low, block, high], axis=dim)
    return block


def broadcast(value, axis, root):
    mine = lax.axis_index(axis) == root
    return lax.psum(jnp.where(mine, value, jnp.zeros_like(value)), axis)


def norm_forward(values, gain, shift):
    center = values - jnp.mean(values, axis=-1, keepdims=True)
    scaled = lax.rsqrt(jnp.mean(center * center, axis=-1, keepdims=True) + eps_norm)
    normed = center * scaled
    return (normed * gain + shift, normed, scaled)


def norm_backward(upstream, gain, normed, scaled):
    weighted = upstream * gain
    centered = weighted - jnp.mean(weighted, axis=-1, keepdims=True)
    return scaled * (centered - normed * jnp.mean(weighted * normed, axis=-1, keepdims=True))


def row_dot(left, right):
    return lax.dot_general(
        left, right, (((left.ndim - 1,), (0,)), ((), ())), preferred_element_type=jnp.float32
    )


def back_dot(left, right):
    return lax.dot_general(
        left, right, (((left.ndim - 1,), (1,)), ((), ())), preferred_element_type=jnp.float32
    )


def outer_sum(left, right):
    return lax.dot_general(
        left, right, (((0, 1), (0, 1)), ((), ())), preferred_element_type=jnp.float32
    )


def column_sum(values):
    return jnp.sum(values, axis=(0, 1), dtype=jnp.float32)


def list_masks(rand_local, first_block, block_count):
    window_count, local_count = (rand_local.shape[0], rand_local.shape[1])
    query_ids = first_block + jnp.arange(local_count, dtype=jnp.int32)
    slide_ok = jnp.stack(
        [query_ids - 1 >= 0, query_ids >= 0, query_ids + 1 <= block_count - 1], axis=1
    )
    end_ok = jnp.stack([jnp.abs(query_ids) > 1, jnp.abs(block_count - 1 - query_ids) > 1], axis=1)
    rand_ok = (
        (jnp.abs(rand_local - query_ids[None, :, None]) > 1)
        & (rand_local != 0)
        & (rand_local != block_count - 1)
    )
    fixed_ok = jnp.broadcast_to(
        jnp.concatenate([slide_ok, end_ok], axis=1)[None], (window_count, local_count, 5)
    )
    return jnp.concatenate([fixed_ok, rand_ok], axis=-1)


def build_routing(rand_batch, position, devices, local_count, capacity):
    window_count = rand_batch.shape[0]
    item_count = window_count * local_count * 3

    def arrange(grid_values):
        grid_values = grid_values.reshape(window_count, devices, local_count, 3)
        return jnp.transpose(grid_values, (1, 0, 2, 3)).reshape(devices, item_count)

    window_grid = jnp.broadcast_to(
        jnp.arange(window_count, dtype=jnp.int32)[:, None, None], rand_batch.shape
    )
    owner_table = arrange(rand_batch // local_count)
    source_table = arrange(window_grid * local_count + rand_batch % local_count)
    device_ids = jnp.arange(devices, dtype=jnp.int32)
    matches = (owner_table[:, :, None] == device_ids[None, None, :]).astype(jnp.int32)
    earlier = jnp.cumsum(matches, axis=1) - matches
    slot_table = jnp.sum(earlier * matches, axis=2)
    owned_here = (owner_table == position).astype(jnp.int32)
    slot_ids = jnp.arange(capacity, dtype=jnp.int32)
    slot_matches = (slot_table[:, :, None] == slot_ids[None, None, :]).astype(
        jnp.int32
    ) * owned_here[:, :, None]
    send_rows = jnp.sum(slot_matches * source_table[:, :, None], axis=1).reshape(devices * capacity)
    send_live = jnp.sum(slot_matches, axis=1).reshape(devices * capacity)
    my_owner = lax.dynamic_index_in_dim(owner_table, position, 0, keepdims=False)
    my_slot = lax.dynamic_index_in_dim(slot_table, position, 0, keepdims=False)
    take_rows = my_owner * capacity + my_slot
    return (send_rows, send_live, take_rows)


def fetch_blocks(packed, routing, block_rows):
    window_count, local_rows, kv_width = packed.shape
    local_count = local_rows // block_rows
    devices = lax.axis_size("seq")
    padded = with_halo(packed, (("seq", 1),), block_rows)
    padded = padded.reshape(window_count, local_count + 2, block_rows, kv_width)
    sliding = jnp.stack([padded[:, offset : offset + local_count] for offset in range(3)], axis=2)
    first_part = broadcast(packed[:, :block_rows], "seq", 0)
    last_part = broadcast(packed[:, local_rows - block_rows :], "seq", devices - 1)
    end_blocks = jnp.stack([first_part, last_part], axis=1)
    end_blocks = jnp.broadcast_to(
        end_blocks[:, None], (window_count, local_count, 2, block_rows, kv_width)
    )
    send_rows, send_live, take_rows = routing
    sources = packed.reshape(window_count * local_count, block_rows, kv_width)
    outgoing = jnp.take(sources, send_rows, axis=0).reshape(devices, -1, block_rows, kv_width)
    incoming = lax.all_to_all(outgoing, "seq", split_axis=0, concat_axis=0, tiled=True).reshape(
        -1, block_rows, kv_width
    )
    fetched = jnp.take(incoming, take_rows, axis=0).reshape(
        window_count, local_count, 3, block_rows, kv_width
    )
    return jnp.concatenate([sliding, end_blocks, fetched], axis=2)


def return_blocks(kv_grads, routing, block_rows):
    window_count, local_count = (kv_grads.shape[0], kv_grads.shape[1])
    kv_width = kv_grads.shape[-1]
    local_rows = local_count * block_rows
    devices = lax.axis_size("seq")
    position = lax.axis_index("seq")
    padded_grad = jnp.zeros((window_count, local_count + 2, block_rows, kv_width), jnp.float32)
    for offset in range(3):
        padded_grad = padded_grad.at[:, offset : offset + local_count].add(kv_grads[:, :, offset])
    rim_rows = jnp.concatenate([padded_grad[:, 0], padded_grad[:, local_count + 1]], axis=1)
    rim_back = with_halo(rim_rows.astype(jnp.bfloat16), (("seq", 1),), block_rows).astype(
        rim_rows.dtype
    )
    end_grads = lax.psum(jnp.sum(kv_grads[:, :, 3:5], axis=1).astype(jnp.bfloat16), "seq").astype(
        jnp.float32
    )
    zeros_block = jnp.zeros((window_count, block_rows, kv_width), jnp.float32)
    first_add = rim_back[:, :block_rows] + jnp.where(position == 0, end_grads[:, 0], zeros_block)
    last_add = rim_back[:, 3 * block_rows :] + jnp.where(
        position == devices - 1, end_grads[:, 1], zeros_block
    )
    send_rows, send_live, take_rows = routing
    rand_items = kv_grads[:, :, 5:8].reshape(-1, block_rows, kv_width)
    capacity_rows = send_rows.shape[0]
    outgoing = (
        jnp.zeros((capacity_rows, block_rows, kv_width), jnp.float32).at[take_rows].set(rand_items)
    )
    incoming = lax.all_to_all(
        outgoing.reshape(devices, -1, block_rows, kv_width).astype(jnp.bfloat16),
        "seq",
        split_axis=0,
        concat_axis=0,
        tiled=True,
    ).astype(jnp.float32)
    incoming = (
        incoming.reshape(capacity_rows, block_rows, kv_width)
        * send_live.astype(jnp.float32)[:, None, None]
    )
    from_owners = (
        jnp.zeros((window_count * local_count, block_rows, kv_width), jnp.float32)
        .at[send_rows]
        .add(incoming)
    )
    summed = padded_grad[:, 1 : local_count + 1].reshape(window_count, local_rows, kv_width)
    summed = summed + from_owners.reshape(window_count, local_rows, kv_width)
    summed = summed.at[:, :block_rows].add(first_add)
    summed = summed.at[:, local_rows - block_rows :].add(last_add)
    return summed


def split_scores(query_low, keyset, key_valid):
    window_count, local_rows, local_width = query_low.shape
    local_count = keyset.shape[1]
    head_count = local_width // HD
    key_rows = keyset.shape[2] * BS
    query_split = query_low.reshape(window_count, local_count, BS, head_count, HD)
    paired = keyset.reshape(window_count, local_count, key_rows, 2, head_count, HD)
    key_part = paired[:, :, :, 0]
    value_part = paired[:, :, :, 1]
    scores = jnp.einsum(
        "wbqhd,wbkhd->wbhqk", query_split, key_part, preferred_element_type=jnp.float32
    ) * HD ** (-0.5)
    allowed = jnp.repeat(key_valid, BS, axis=2)[:, :, None, None, :]
    scores = jnp.where(allowed, scores, -1e30)
    return (scores, query_split, key_part, value_part)


def attend_forward(query_low, keyset, key_valid):
    scores, query_split, key_part, value_part = split_scores(query_low, keyset, key_valid)
    top_score = jnp.max(scores, axis=-1, keepdims=True)
    log_total = top_score + jnp.log(jnp.sum(jnp.exp(scores - top_score), axis=-1, keepdims=True))
    weights = jnp.exp(scores - log_total).astype(jnp.bfloat16)
    mixed = jnp.einsum(
        "wbhqk,wbkhd->wbqhd", weights, value_part, preferred_element_type=jnp.float32
    )
    return (mixed.reshape(query_low.shape).astype(jnp.bfloat16), log_total)


def attend_backward(query_low, keyset, key_valid, log_total, grad_mixed):
    scores, query_split, key_part, value_part = split_scores(query_low, keyset, key_valid)
    window_count, local_count = (keyset.shape[0], keyset.shape[1])
    local_width = query_low.shape[2]
    weights = jnp.exp(scores - log_total)
    grad_split = grad_mixed.reshape(query_split.shape)
    grad_weights = jnp.einsum(
        "wbqhd,wbkhd->wbhqk", grad_split, value_part, preferred_element_type=jnp.float32
    )
    delta_sum = jnp.sum(weights * grad_weights, axis=-1, keepdims=True)
    grad_scores = (weights * (grad_weights - delta_sum)).astype(jnp.bfloat16)
    grad_query = jnp.einsum(
        "wbhqk,wbkhd->wbqhd", grad_scores, key_part, preferred_element_type=jnp.float32
    ) * HD ** (-0.5)
    grad_key = jnp.einsum(
        "wbhqk,wbqhd->wbkhd", grad_scores, query_split, preferred_element_type=jnp.float32
    ) * HD ** (-0.5)
    grad_value = jnp.einsum(
        "wbhqk,wbqhd->wbkhd",
        weights.astype(jnp.bfloat16),
        grad_split,
        preferred_element_type=jnp.float32,
    )
    list_shape = (window_count, local_count, keyset.shape[2], BS, local_width)
    kv_grads = jnp.concatenate(
        [grad_key.reshape(list_shape), grad_value.reshape(list_shape)], axis=-1
    )
    return (grad_query.reshape(query_low.shape), kv_grads)


def flatten_all(members):
    return jnp.concatenate([member.reshape(-1) for member in members])


def share_sum(vector):
    return lax.psum_scatter(vector, ("dp", "seq"), scatter_dimension=0, tiled=True)


def spread_body(
    tokens,
    cotangent,
    masked_pos,
    rand_blocks,
    ln1_gain,
    ln1_bias,
    w_query,
    b_query,
    w_key,
    w_value,
    b_value,
    w_out,
    b_out,
    ln2_gain,
    ln2_bias,
    w_inner,
    b_inner,
    w_outer,
    b_outer,
):
    local_rows = tokens.shape[1]
    devices = lax.axis_size("seq")
    position = lax.axis_index("seq")
    block_count = rand_blocks.shape[1]
    local_count = block_count // devices
    capacity = (3 * WIN_MB * local_count + devices - 1) // devices
    gain_one = ln1_gain.astype(jnp.float32)
    bias_one = ln1_bias.astype(jnp.float32)
    gain_two = ln2_gain.astype(jnp.float32)
    bias_two = ln2_bias.astype(jnp.float32)
    row_ids = position * local_rows + jnp.arange(local_rows, dtype=jnp.int32)
    first_block = position * local_count
    outputs = []
    input_grads = []
    totals = None
    for batch_index in range(MB):
        batch_start = batch_index * WIN_MB
        batch_stop = batch_start + WIN_MB
        tokens_now = tokens[batch_start:batch_stop].astype(jnp.float32)
        rand_now = rand_blocks[batch_start:batch_stop]
        routing = build_routing(rand_now, position, devices, local_count, capacity)
        rand_local = lax.dynamic_slice_in_dim(rand_now, first_block, local_count, 1)
        key_valid = list_masks(rand_local, first_block, block_count)
        hidden_one, normed_one, scaled_one = norm_forward(tokens_now, gain_one, bias_one)
        hidden_low = hidden_one.astype(jnp.bfloat16)
        query_low = (row_dot(hidden_low, w_query) + b_query.astype(jnp.float32)).astype(
            jnp.bfloat16
        )
        key_low = row_dot(hidden_low, w_key).astype(jnp.bfloat16)
        value_low = (row_dot(hidden_low, w_value) + b_value.astype(jnp.float32)).astype(
            jnp.bfloat16
        )
        packed = jnp.concatenate([key_low, value_low], axis=2)
        keyset = fetch_blocks(packed, routing, BS)
        mixed_low, log_total = attend_forward(query_low, keyset, key_valid)
        attn_out = lax.psum(row_dot(mixed_low, w_out).astype(jnp.bfloat16), "tensor").astype(
            jnp.float32
        ) + b_out.astype(jnp.float32)
        middle = tokens_now + attn_out
        hidden_two, normed_two, scaled_two = norm_forward(middle, gain_two, bias_two)
        hidden_two_low = hidden_two.astype(jnp.bfloat16)
        inner_pre = row_dot(hidden_two_low, w_inner) + b_inner.astype(jnp.float32)
        active = jax.nn.gelu(inner_pre, approximate=False).astype(jnp.bfloat16)
        ffn_out = lax.psum(row_dot(active, w_outer).astype(jnp.bfloat16), "tensor").astype(
            jnp.float32
        ) + b_outer.astype(jnp.float32)
        outputs.append((middle + ffn_out).astype(jnp.bfloat16))
        masked_now = masked_pos[batch_start:batch_stop]
        chosen = jnp.any(row_ids[None, :, None] == masked_now[:, None, :], axis=2)
        cot_now = cotangent[batch_start:batch_stop]
        grad_top = jnp.where(chosen[:, :, None], cot_now, jnp.zeros_like(cot_now))
        grad_active = back_dot(grad_top, w_outer)
        normal_cdf = 0.5 * (1.0 + lax.erf(inner_pre * inv_root_two))
        density = jnp.exp(-0.5 * inner_pre * inner_pre) * inv_root_two_pi
        grad_inner = (grad_active * (normal_cdf + inner_pre * density)).astype(jnp.bfloat16)
        grad_hidden_two = lax.psum(
            back_dot(grad_inner, w_inner).astype(jnp.bfloat16), "tensor"
        ).astype(jnp.float32)
        grad_middle = grad_top.astype(jnp.float32) + norm_backward(
            grad_hidden_two, gain_two, normed_two, scaled_two
        )
        grad_attn = grad_middle.astype(jnp.bfloat16)
        grad_mixed = back_dot(grad_attn, w_out).astype(jnp.bfloat16)
        keyset_back = fetch_blocks(packed, routing, BS)
        grad_query, kv_grads = attend_backward(
            query_low, keyset_back, key_valid, log_total, grad_mixed
        )
        grad_query = grad_query.astype(jnp.bfloat16)
        grad_packed = return_blocks(kv_grads, routing, BS)
        local_width = query_low.shape[2]
        grad_key = grad_packed[:, :, :local_width].astype(jnp.bfloat16)
        grad_value = grad_packed[:, :, local_width:].astype(jnp.bfloat16)
        grad_partial = (
            back_dot(grad_query, w_query)
            + back_dot(grad_key, w_key)
            + back_dot(grad_value, w_value)
        )
        grad_hidden_one = lax.psum(grad_partial.astype(jnp.bfloat16), "tensor").astype(jnp.float32)
        grad_tokens_now = grad_middle + norm_backward(
            grad_hidden_one, gain_one, normed_one, scaled_one
        )
        input_grads.append(grad_tokens_now.astype(jnp.bfloat16))
        batch_grads = (
            jnp.sum(grad_hidden_one * normed_one, axis=(0, 1)),
            jnp.sum(grad_hidden_one, axis=(0, 1)),
            outer_sum(hidden_low, grad_query),
            column_sum(grad_query),
            outer_sum(hidden_low, grad_key),
            outer_sum(hidden_low, grad_value),
            column_sum(grad_value),
            outer_sum(mixed_low, grad_attn),
            column_sum(grad_attn),
            jnp.sum(grad_hidden_two * normed_two, axis=(0, 1)),
            jnp.sum(grad_hidden_two, axis=(0, 1)),
            outer_sum(hidden_two_low, grad_inner),
            column_sum(grad_inner),
            outer_sum(active, grad_top),
            column_sum(grad_top),
        )
        totals = batch_grads if totals is None else jax.tree.map(jnp.add, totals, batch_grads)
    final_share = share_sum(flatten_all(totals))
    gathered = lax.all_gather(
        final_share.astype(jnp.bfloat16), ("dp", "seq"), axis=0, tiled=True
    ).astype(final_share.dtype)
    param_shapes = [
        member.shape
        for member in (
            ln1_gain,
            ln1_bias,
            w_query,
            b_query,
            w_key,
            w_value,
            b_value,
            w_out,
            b_out,
            ln2_gain,
            ln2_bias,
            w_inner,
            b_inner,
            w_outer,
            b_outer,
        )
    ]
    results = []
    cursor = 0
    for shape_now in param_shapes:
        length = 1
        for extent in shape_now:
            length = length * extent
        results.append(gathered[cursor : cursor + length].reshape(shape_now))
        cursor = cursor + length
    out_all = jnp.concatenate(outputs, axis=0)
    grad_all = jnp.concatenate(input_grads, axis=0)
    return (
        out_all,
        grad_all,
        results[0],
        results[1],
        results[2],
        results[3],
        results[4],
        results[5],
        results[6],
        results[7],
        results[8],
        results[9],
        results[10],
        results[11],
        results[12],
        results[13],
        results[14],
    )


def power_of_two(number):
    return number & (number - 1) == 0


def body(tokens, *rest):
    dp, seq, tensor = (lax.axis_size(axis) for axis in ("dp", "seq", "tensor"))
    fits = seq == tokens.shape[0] and tensor == 2 and dp == 4 and power_of_two(seq)
    return (window_body if fits else spread_body)(tokens, *rest)


def solution(mesh):
    in_specs = (
        P("dp", "seq", None),
        P("dp", "seq", None),
        P("dp", None),
        P("dp", None, None),
        P(),
        P(),
        P(None, "tensor"),
        P("tensor"),
        P(None, "tensor"),
        P(None, "tensor"),
        P("tensor"),
        P("tensor", None),
        P(),
        P(),
        P(),
        P(None, "tensor"),
        P("tensor"),
        P("tensor", None),
        P(),
    )
    out_specs = (
        P("dp", "seq", None),
        P("dp", "seq", None),
        P(),
        P(),
        P(None, "tensor"),
        P("tensor"),
        P(None, "tensor"),
        P(None, "tensor"),
        P("tensor"),
        P("tensor", None),
        P(),
        P(),
        P(),
        P(None, "tensor"),
        P("tensor"),
        P("tensor", None),
        P(),
    )
    return jax.shard_map(body, mesh=mesh, in_specs=in_specs, out_specs=out_specs, check_vma=False)
```

```python
import functools

import jax
import jax.numpy as jnp
from jax import lax
from jax.experimental import pallas as pl
from jax.experimental.pallas import tpu as pltpu
from jax.sharding import PartitionSpec as P

HD = 64
BS = 64
MB = 2
WIN_MB = 2


eps_norm = 1e-05
inv_root_two = 0.7071067811865476
inv_root_two_pi = 0.3989422804014327


LANES = 128
NEG = -1e30
VMEM_LIMIT = 16 * 1024 * 1024


def dot_nn(left, right):
    return lax.dot_general(left, right, (((1,), (0,)), ((), ())), preferred_element_type=jnp.float32)


def dot_nt(left, right):
    return lax.dot_general(left, right, (((1,), (1,)), ((), ())), preferred_element_type=jnp.float32)


def dot_tn(left, right):
    return lax.dot_general(left, right, (((0,), (0,)), ((), ())), preferred_element_type=jnp.float32)


def norm_parts(values):
    center = values - jnp.mean(values, axis=-1, keepdims=True)
    scaled = lax.rsqrt(jnp.mean(center * center, axis=-1, keepdims=True) + eps_norm)
    return center * scaled, scaled


def pick_rows(positions, total):
    ids = lax.broadcasted_iota(jnp.int32, (positions.shape[0], total), 1)
    return jnp.where(ids == positions, 1.0, 0.0).astype(jnp.bfloat16)


def row_lists(blocks, allow):
    ids = lax.broadcasted_iota(jnp.int32, (blocks.shape[0], allow.shape[0]), 1)
    return dot_nn(jnp.where(ids == blocks, 1.0, 0.0).astype(jnp.bfloat16), allow)


def head_half(half):
    lane = lax.broadcasted_iota(jnp.int32, (1, LANES), 1)
    return (lane < HD) if half == 0 else (lane >= HD)


def one_head(slab, half):
    return jnp.where(head_half(half), slab, jnp.zeros_like(slab))


class Order:
    def __init__(self):
        self.last = None
        self.needed = []
        self.later = []

    def soon(self, array, kernels=2):
        self.later.append([kernels, array])

    def need(self, *arrays):
        self.needed += arrays

    def call(self, kernel, outs, args, smem=1, scratch=(), aliases=None):
        first = args[0]
        for entry in self.later:
            entry[0] -= 1
        self.needed += [array for left, array in self.later if left == 0]
        self.later = [entry for entry in self.later if entry[0] > 0]
        if self.last is not None:
            first = after(first, self.last, *self.needed)
            self.needed = []
        spec = pl.BlockSpec(memory_space=pltpu.VMEM)
        found = pl.pallas_call(
            kernel,
            name=getattr(kernel, "func", kernel).__name__.removesuffix("_kernel"),
            out_shape=outs,
            in_specs=[pl.BlockSpec(memory_space=pltpu.SMEM)] * smem + [spec] * (len(args) - smem),
            out_specs=[spec] * len(outs),
            scratch_shapes=list(scratch),
            input_output_aliases=aliases or {},
            compiler_params=pltpu.CompilerParams(vmem_limit_bytes=VMEM_LIMIT),
            cost_estimate=pl.CostEstimate(flops=1, bytes_accessed=1, transcendentals=0),
        )(first, *args[1:])
        self.last = min(found, key=lambda a: a.size)
        return found


def after(value, *others):
    return lax.optimization_barrier((value, others))[0]


def shape(dims, dtype=jnp.bfloat16):
    return jax.ShapeDtypeStruct(dims, dtype)


def shard_kernel(at, bits, own, other, vec, wq, wk, wv, *rest):
    tok, h, q, k, v = rest[-5:]
    run = own.shape[0]
    for kept, out in zip(rest[:-5], rest[-5:]):
        out[pl.ds(0, 2 * at * run), :] = kept[pl.ds(0, 2 * at * run), :]
    local = wq.shape[1]
    first = bits[2] == 0
    tok[pl.ds(2 * at * run, run), :] = jnp.where(first, own[...], other[...])
    tok[pl.ds((2 * at + 1) * run, run), :] = jnp.where(first, other[...], own[...])
    rows = pl.ds(2 * at * run, 2 * run)
    normed, _ = norm_parts(tok[rows, :].astype(jnp.float32))
    low = (normed * vec[0:1, :] + vec[1:2, :]).astype(jnp.bfloat16)
    h[rows, :] = low
    q[rows, :] = (dot_nn(low, wq[...]) + vec[6:7, :local]).astype(jnp.bfloat16)
    k[rows, :] = dot_nn(low, wk[...]).astype(jnp.bfloat16)
    v[rows, :] = (dot_nn(low, wv[...]) + vec[6:7, local:]).astype(jnp.bfloat16)


def sum_rows_kernel(bits, *refs):
    total = None
    for piece in refs[:-1]:
        value = piece[...].astype(jnp.float32)
        total = value if total is None else total + value
    refs[-1][...] = total.astype(jnp.bfloat16)


def front_kernel(bits, pos, allow, wo, tok, h, q, k, v, xm, hm, qm, om, lse, part):
    total, local = q.shape
    pick = pick_rows(pos[...], total)
    xm[...] = dot_nn(pick, tok[...]).astype(jnp.bfloat16)
    hm[...] = dot_nn(pick, h[...]).astype(jnp.bfloat16)
    qm[...] = dot_nn(pick, q[...]).astype(jnp.bfloat16)
    listed = row_lists(pos[...] >> 6, allow[...]) > 0.5
    lane = lax.broadcasted_iota(jnp.int32, (pos.shape[0], LANES), 1)

    def one_slab(slab, sums):
        cols = pl.ds(pl.multiple_of(slab * LANES, LANES), LANES)
        query = (qm[:, cols].astype(jnp.float32) * HD ** (-0.5)).astype(jnp.bfloat16)
        mixed = None
        for half in range(2):
            scores = jnp.where(listed, dot_nt(one_head(query, half), k[:, cols]), NEG)
            top = jnp.max(scores, axis=-1, keepdims=True)
            weight = jnp.exp(scores - top)
            total_weight = jnp.sum(weight, axis=-1, keepdims=True)
            sums = jnp.where(lane == 2 * slab + half, top + jnp.log(total_weight), sums)
            found = dot_nn(weight.astype(jnp.bfloat16), v[:, cols]) * (1.0 / total_weight)
            mixed = found if half == 0 else jnp.where(head_half(0), mixed, found)
        om[:, cols] = mixed.astype(jnp.bfloat16)
        return sums

    none = jnp.zeros((pos.shape[0], LANES), jnp.float32)
    sums = lax.fori_loop(0, local // LANES, one_slab, none)
    lse[...] = sums
    part[...] = dot_nn(om[...], wo[...]).astype(jnp.bfloat16)


def gelu_parts(z):
    cdf = 0.5 * (1.0 + lax.erf(z * inv_root_two))
    return z * cdf, cdf + z * (jnp.exp(-0.5 * z * z) * inv_root_two_pi)


def middle_of(xm, part, other, vec):
    both = part[...].astype(jnp.float32) + other[...].astype(jnp.float32)
    return xm[...].astype(jnp.float32) + (both + vec[2:3, :])


def hidden_kernel(
    bits, xm, part, other, g_own, g_other, vec, wi, wf,
    wf_a, wf_as, wf_b, wf_bs, wi_a, wi_as, wi_b, wi_bs, dh2, few, g,
    u_all, h2_all, dz_all,
):
    width, hidden = wi.shape
    split = width // 2
    first = bits[2] == 0
    g[:, :split] = jnp.where(first, g_own[...], g_other[...])
    g[:, split:] = jnp.where(first, g_other[...], g_own[...])
    normed, _ = norm_parts(middle_of(xm, part, other, vec))
    h2_all[...] = (normed * vec[3:4, :] + vec[4:5, :]).astype(jnp.bfloat16)
    h2 = h2_all[...]
    for at in range(hidden // width):
        cols = pl.ds(at * width, width)
        z = dot_nn(h2, wi[:, cols]) + vec[7 + at : 8 + at, :]
        act, slope = gelu_parts(z)
        u_all[:, cols] = act.astype(jnp.bfloat16)
        dz = (dot_nt(g[...], wf[cols, :]) * slope).astype(jnp.bfloat16)
        dz_all[:, cols] = dz
        few[1 + at : 2 + at, :] = jnp.sum(dz.astype(jnp.float32), axis=0, keepdims=True)
    few[0:1, :] = jnp.sum(g[...].astype(jnp.float32), axis=0, keepdims=True)
    half = hidden // 2
    count = width // 2
    for order, keep, send in ((0, wf_a, wf_as), (1, wf_b, wf_bs)):
        for out, bit in ((keep, bits[order]), (send, 1 - bits[order])):
            at = pl.multiple_of(order * half + bit * count, LANES)
            out[0] = dot_tn(u_all[:, pl.ds(at, count)], g[...]).astype(jnp.bfloat16)
    for order, keep, send in ((0, wi_a, wi_as), (1, wi_b, wi_bs)):
        for out, bit in ((keep, bits[order]), (send, 1 - bits[order])):
            at = pl.multiple_of(bit * count, LANES)
            out[0] = dot_tn(
                h2_all[:, pl.ds(at, count)], dz_all[:, pl.ds(order * half, half)]
            ).astype(jnp.bfloat16)
    dh2[...] = dot_nt(dz_all[...], wi[...]).astype(jnp.bfloat16)


def attend_back_kernel(
    bits, xm, part, other, g, dh2, dh2_other, vec, wo, pos, allow, qm, om, hm, lse, h, k, v,
    da_a, da_as, da_b, da_bs, dx1, dq, dk, dv, few, da_all, do_all,
):
    width = g.shape[1]
    normed, scaled = norm_parts(middle_of(xm, part, other, vec))
    up = dh2[...].astype(jnp.float32) + dh2_other[...].astype(jnp.float32)
    few[0:1, :] = jnp.sum(up * normed, axis=0, keepdims=True)
    few[1:2, :] = jnp.sum(up, axis=0, keepdims=True)
    weighted = up * vec[3:4, :]
    centered = weighted - jnp.mean(weighted, axis=-1, keepdims=True)
    slope = jnp.mean(weighted * normed, axis=-1, keepdims=True)
    grad = g[...].astype(jnp.float32) + scaled * (centered - normed * slope)
    dx1[...] = grad
    low = grad.astype(jnp.bfloat16)
    da_all[...] = low
    few[2:3, :] = jnp.sum(low.astype(jnp.float32), axis=0, keepdims=True)
    do_all[...] = dot_nt(low, wo[...]).astype(jnp.bfloat16)
    listed = row_lists(pos[...] >> 6, allow[...]) > 0.5
    for slab in range(qm.shape[1] // LANES):
        cols = pl.ds(slab * LANES, LANES)
        query = (qm[:, cols].astype(jnp.float32) * HD ** (-0.5)).astype(jnp.bfloat16)
        grad_q, grad_k, grad_v = None, None, None
        for half in range(2):
            at = 2 * slab + half
            own = one_head(query, half)
            own_do = one_head(do_all[:, cols], half)
            scores = jnp.where(listed, dot_nt(own, k[:, cols]), NEG)
            prob = jnp.exp(scores - lse[:, at : at + 1])
            grad_p = dot_nt(own_do, v[:, cols])
            delta = jnp.sum(prob * grad_p, axis=-1, keepdims=True)
            ds = (prob * (grad_p - delta)).astype(jnp.bfloat16)
            found_q = dot_nn(ds, k[:, cols])
            found_k = dot_tn(ds, own)
            found_v = dot_tn(prob.astype(jnp.bfloat16), own_do)
            grad_q = found_q if half == 0 else jnp.where(head_half(0), grad_q, found_q)
            grad_k = found_k if half == 0 else grad_k + found_k
            grad_v = found_v if half == 0 else grad_v + found_v
        dq[:, cols] = (grad_q * HD ** (-0.5)).astype(jnp.bfloat16)
        dk[:, cols] = grad_k.astype(jnp.bfloat16)
        dv[:, cols] = grad_v.astype(jnp.bfloat16)
    local = qm.shape[1]
    few[3:4, :local] = jnp.sum(dq[...].astype(jnp.float32), axis=0, keepdims=True)
    few[3:4, local:] = jnp.sum(dv[...].astype(jnp.float32), axis=0, keepdims=True)
    count = width // 2
    for keep, bit in ((da_a, bits[0]), (da_as, 1 - bits[0])):
        cols = pl.ds(pl.multiple_of(bit * count, LANES), count)
        keep[0, :, :local] = dot_tn(hm[:, cols], dq[...]).astype(jnp.bfloat16)
        keep[0, :, local:] = dot_tn(h[:, cols], dk[...]).astype(jnp.bfloat16)
    for keep, bit in ((da_b, bits[1]), (da_bs, 1 - bits[1])):
        cols = pl.ds(pl.multiple_of(bit * count, LANES), count)
        keep[0, :, :local] = dot_tn(h[:, cols], dv[...]).astype(jnp.bfloat16)
        keep[0, :, local:] = dot_tn(om[...], da_all[:, cols]).astype(jnp.bfloat16)


def input_kernel(bits, pos, dq, dk, dv, wq, wk, wv, keep, *rest):
    sends, dq_all = rest[:-1], rest[-1]
    total = dk.shape[0]
    dq_all[...] = dot_tn(pick_rows(pos[...], total), dq[...]).astype(jnp.bfloat16)
    run = BS * 2
    for at in range(0, total // (2 * run)):
        own = keep.at[pl.ds(at * run, run), :]
        sent = sends[0].at[pl.ds(at * run, run), :]
        for out, bit in ((own, bits[2]), (sent, 1 - bits[2])):
            rows = pl.ds(pl.multiple_of(at * 2 * run + bit * run, run), run)
            out[...] = (
                dot_nt(dq_all[rows, :], wq[...])
                + dot_nt(dk[rows, :], wk[...])
                + dot_nt(dv[rows, :], wv[...])
            ).astype(jnp.bfloat16)


def first_norm_kernel(count, bits, pos_half, own, dx1, vec, *rest):
    toks, others, grads = rest[:count], rest[count : -3 - count], rest[-3 - count : -3]
    few, tok, other = rest[-3:]
    run = others[0].shape[0]
    for at, piece in enumerate(others):
        other[pl.ds(at * run, run), :] = piece[...]
    run = toks[0].shape[0]
    for at, piece in enumerate(toks):
        tok[pl.ds(at * run, run), :] = piece[...]
    normed, scaled = norm_parts(tok[...].astype(jnp.float32))
    up = own[...].astype(jnp.float32) + other[...].astype(jnp.float32)
    few[0:1, :] = jnp.sum(up * normed, axis=0, keepdims=True)
    few[1:2, :] = jnp.sum(up, axis=0, keepdims=True)
    weighted = up * vec[0:1, :]
    centered = weighted - jnp.mean(weighted, axis=-1, keepdims=True)
    slope = jnp.mean(weighted * normed, axis=-1, keepdims=True)
    pick = pick_rows(pos_half[...], tok.shape[0])
    high = dx1[...].astype(jnp.bfloat16)
    rest = (dx1[...] - high.astype(jnp.float32)).astype(jnp.bfloat16)
    through = dot_tn(pick, high) + dot_tn(pick, rest)
    grad = (through + scaled * (centered - normed * slope)).astype(jnp.bfloat16)
    for at, piece in enumerate(grads):
        piece[0] = grad[at * run : (at + 1) * run, :]


def attend_kernel(at, bits, q, k, v, allow, keep, send, mixed_all):
    tile = mixed_all.shape[0]
    run = tile // 2
    rows = pl.ds(at * tile, tile)
    ids = lax.broadcasted_iota(jnp.int32, (tile, 1), 0)
    bias = (row_lists(at * (tile // BS) + (ids >> 6), allow[...]) - 1.0) * -NEG

    def one_slab(slab, carry):
        cols = pl.ds(pl.multiple_of(slab * LANES, LANES), LANES)
        query = (q[rows, cols].astype(jnp.float32) * HD ** (-0.5)).astype(jnp.bfloat16)
        mixed = None
        for half in range(2):
            scores = dot_nt(one_head(query, half), k[:, cols]) + bias
            weight = jnp.exp(scores - jnp.max(scores, axis=-1, keepdims=True))
            total_weight = jnp.sum(weight, axis=-1, keepdims=True)
            found = dot_nn(weight.astype(jnp.bfloat16), v[:, cols]) * (1.0 / total_weight)
            mixed = found if half == 0 else jnp.where(head_half(0), mixed, found)
        mixed_all[:, cols] = mixed.astype(jnp.bfloat16)
        return carry

    lax.fori_loop(0, q.shape[1] // LANES, one_slab, 0)
    for out, bit in ((keep, bits[2]), (send, 1 - bits[2])):
        out[...] = mixed_all[pl.ds(pl.multiple_of(bit * run, run), run), :]


def lay_kernel(bits, *refs):
    run = refs[0].shape[0]
    for at, piece in enumerate(refs[:-1]):
        refs[-1][pl.ds(at * run, run), :] = piece[...]


def feed_kernel(base, count, bits, *refs):
    toks, refs = refs[:count], refs[count:]
    own, refs = refs[:count], refs[count:]
    other, vec, bi_other, wo, wo_other, wi, wi_other, wf, wf_other = refs[:9]
    pairs, outs, mid_all = refs[9 : 9 + count], refs[-1 - count : -1], refs[-1]
    width, hidden = wi.shape
    run = toks[0].shape[0]
    for at in range(count):
        theirs = other[pl.ds((base + at) * run, run), :]
        mixed = dot_nn(own[at][...], wo[...]) + dot_nn(theirs, wo_other[...])
        mid_all[pl.ds(at * run, run), :] = toks[at][...].astype(jnp.float32) + (
            mixed + vec[2:3, :]
        )
    middle = mid_all[...]
    normed, _ = norm_parts(middle)
    h2 = (normed * vec[3:4, :] + vec[4:5, :]).astype(jnp.bfloat16)
    total = middle + vec[5:6, :]
    for row, bias, inner, outer in ((7, vec, wi, wf), (0, bi_other, wi_other, wf_other)):
        for at in range(hidden // width):
            cols = pl.ds(at * width, width)
            z = dot_nn(h2, inner[:, cols]) + bias[row + at : row + at + 1, :]
            act = z * (0.5 * (1.0 + lax.erf(z * inv_root_two)))
            total = total + dot_nn(act.astype(jnp.bfloat16), outer[cols, :])
    low = total.astype(jnp.bfloat16)
    for at in range(count):
        outs[at][0] = pairs[at][0]
        outs[at][1] = low[at * run : (at + 1) * run, :]


def gather_small_kernel(bits, first, first_other, attend, hidden, out):
    out[0:2, :] = first[...] + first_other[...]
    out[2:6, :] = attend[...]
    out[6:, :] = hidden[...]


def add_small_kernel(bits, own, other, out):
    out[...] = own[...] + other[...]


def interleave_kernel(bits, *refs):
    count = (len(refs) - 2) // 2
    own, over, outs = refs[:count], refs[count : 2 * count], refs[2 * count :]
    run = own[0].shape[1]
    for at in range(count):
        window = bits[5] ^ at
        for which, out in enumerate(outs):
            for pieces, side in ((own, bits[2]), (over, 1 - bits[2])):
                rows = pl.ds(pl.multiple_of(side * run, run), run)
                out[window, rows, :] = pieces[at][which]


def add_low(left, right):
    return (left.astype(jnp.float32) + right.astype(jnp.float32)).astype(jnp.bfloat16)


def part_rows(bit, count):
    return pl.ds(pl.multiple_of(bit * count, 16), count)


def halve_plane_kernel(at, bits, ka, ra, kb, rb, keep_a, send_a, keep_b, send_b):
    count = keep_a.shape[1]
    groups = ((ka, ra, keep_a, send_a, bits[at[0]]), (kb, rb, keep_b, send_b, bits[at[1]]))
    for k, r, keep, send, bit in groups:
        for out, side in ((keep, bit), (send, 1 - bit)):
            rows = part_rows(side, count)
            out[...] = add_low(k[:, rows, :], r[:, rows, :])


def halve_join_kernel(at, bits, ka, ra, kb, rb, keep, send):
    group, count = ka.shape[0], keep.shape[1]
    for out, side in ((keep, bits[at]), (send, 1 - bits[at])):
        rows = part_rows(side, count)
        out[:group] = add_low(ka[:, rows, :], ra[:, rows, :])
        out[group:] = add_low(kb[:, rows, :], rb[:, rows, :])


def halve_line_kernel(at, bits, k, r, keep, send):
    count = keep.shape[1]
    for out, side in ((keep, bits[at]), (send, 1 - bits[at])):
        rows = part_rows(side, count)
        out[...] = add_low(k[:, rows, :], r[:, rows, :])


def last_line_kernel(bits, k, r, out):
    out[...] = add_low(k[...], r[...])


def double_line_kernel(at, bits, own, other, out):
    count = own.shape[1]
    out[:, part_rows(bits[at], count), :] = own[...]
    out[:, part_rows(1 - bits[at], count), :] = other[...]


def double_split_kernel(at, bits, own, other, out_a, out_b):
    count = own.shape[1]
    group = out_a.shape[0]
    for which, out in ((0, out_a), (1, out_b)):
        part = pl.ds(which * group, group)
        out[:, part_rows(bits[at], count), :] = own[part]
        out[:, part_rows(1 - bits[at], count), :] = other[part]


def double_plane_kernel(at, bits, own_a, other_a, own_b, other_b, out_a, out_b):
    groups = ((own_a, other_a, out_a, bits[at[0]]), (own_b, other_b, out_b, bits[at[1]]))
    for own, other, out, bit in groups:
        count = own.shape[1]
        out[:, part_rows(bit, count), :] = own[...]
        out[:, part_rows(1 - bit, count), :] = other[...]


def last_rows_kernel(at, bits, own_a, other_a, own_b, other_b, out):
    count = own_a.shape[1]
    groups = ((own_a, other_a, bits[at[0]]), (own_b, other_b, bits[at[1]]))
    for which, (own, other, bit) in enumerate(groups):
        for value, side in ((own, bit), (other, 1 - bit)):
            out[part_rows(2 * which + side, count), :] = value[0].astype(jnp.float32)


def last_columns_kernel(at, bits, own_a, other_a, own_b, other_b, out):
    count, width = own_a.shape[1:]
    groups = ((own_a, other_a, bits[at[0]]), (own_b, other_b, bits[at[1]]))
    for which, (own, other, bit) in enumerate(groups):
        for value, side in ((own, bit), (other, 1 - bit)):
            out[part_rows(side, count), pl.ds(which * width, width)] = value[0].astype(
                jnp.float32
            )


def last_attend_kernel(
    at, bits, own_a, other_a, own_b, other_b, grad_q, grad_k, grad_v, grad_o
):
    count = own_a.shape[1]
    local = grad_q.shape[1]
    for value, side in ((own_a, bits[at[0]]), (other_a, 1 - bits[at[0]])):
        grad_q[part_rows(side, count), :] = value[0, :, :local].astype(jnp.float32)
        grad_k[part_rows(side, count), :] = value[0, :, local:].astype(jnp.float32)
    for value, side in ((own_b, bits[at[1]]), (other_b, 1 - bits[at[1]])):
        grad_v[part_rows(side, count), :] = value[0, :, :local].astype(jnp.float32)
        cols = pl.ds(pl.multiple_of(side * count, LANES), count)
        grad_o[:, cols] = value[0, :, local:].astype(jnp.float32)


def joined_size(piece):
    group, rows, width = piece.shape
    return shape((group, 2 * rows, width))


def halved_size(piece):
    group, rows, width = piece.shape
    return shape((group, rows // 2, width))


def flip(value, axis, bit):
    return lax.ppermute(value, axis, [(i, i ^ bit) for i in range(lax.axis_size(axis))])


def bit_of(axis, bit):
    return jnp.where((lax.axis_index(axis) & bit) != 0, 1, 0).astype(jnp.int32)


def stages_of(order):
    dp_bits = [("dp", 1 << i) for i in range(lax.axis_size("dp").bit_length() - 1)]
    seq_bits = [("seq", 1 << i) for i in range(lax.axis_size("seq").bit_length() - 1)]
    return (dp_bits if order == 0 else dp_bits[::-1]) + seq_bits


class Summing:
    def __init__(self, order, bits, keep, send):
        self.order, self.bits = order, bits
        self.keep, self.send = list(keep), list(send)
        self.plane = [stages_of(which)[:2] for which in range(2)]
        self.line = stages_of(0)[2:]

    def hold(self, *others):
        self.send = [after(value, *others) for value in self.send]

    def exchange(self, at):
        self.got = [flip(s, *self.plane[which][at]) for which, s in enumerate(self.send)]
        return self.got

    def exchange_line(self, at):
        return flip(self.send, *self.line[at])

    def halve_first(self):
        other = self.got
        ka, sa, kb, sb = self.order.call(
            functools.partial(halve_plane_kernel, (1, 0)),
            [halved_size(self.keep[0])] * 4,
            (self.bits, self.keep[0], other[0], self.keep[1], other[1]),
        )
        self.keep, self.send = [ka, kb], [sa, sb]

    def halve_second(self):
        other = self.got
        group, rows, width = self.keep[0].shape
        self.keep, self.send = self.order.call(
            functools.partial(halve_join_kernel, 3),
            [shape((2 * group, rows // 2, width))] * 2,
            (self.bits, self.keep[0], other[0], self.keep[1], other[1]),
        )

    def halve_line(self, at, other):
        two, rows, width = self.keep.shape
        if at + 1 < len(self.line):
            self.keep, self.send = self.order.call(
                functools.partial(halve_line_kernel, 4 + at),
                [shape((two, rows // 2, width))] * 2,
                (self.bits, self.keep, other),
            )
        else:
            (self.send,) = self.order.call(
                last_line_kernel, [shape(self.keep.shape)], (self.bits, self.keep, other)
            )

    def double_line(self, at, other):
        two, rows, width = self.send.shape
        if at > 0:
            (self.send,) = self.order.call(
                functools.partial(double_line_kernel, 3 + at),
                [shape((two, 2 * rows, width))],
                (self.bits, self.send, other),
            )
        else:
            self.send = self.order.call(
                functools.partial(double_split_kernel, 3 + at),
                [shape((two // 2, 2 * rows, width))] * 2,
                (self.bits, self.send, other),
            )

    def double_second(self):
        other = self.got
        self.send = self.order.call(
            functools.partial(double_plane_kernel, (1, 0)),
            [joined_size(self.send[0])] * 2,
            (self.bits, self.send[0], other[0], self.send[1], other[1]),
        )

    def write(self, kernel, outs):
        return self.order.call(
            functools.partial(kernel, (0, 1)),
            [shape(dims, jnp.float32) for dims in outs],
            (self.bits, self.send[0], self.got[0], self.send[1], self.got[1]),
        )


STEPS = (
    "i.go", "I.0", "W.wf", "f.h1", "W.wi", "f.h2", "A.0", "f.l0", "i.h1", "a.go", "W.wo",
    "A.1", "i.h2", "A.2", "i.l0", "f.l1", "A.3", "a.h1", "i.l1", "W.bi", "X.0", "f.d1", "N.0",
    "f.d0", "a.h2", "F.0", "a.l0", "i.d1", "f.e2", "F.1", "i.d0", "a.l1", "S.0", "f.wr",
    "S.1", "a.d1", "i.e2", "a.d0", "S.2", "R.3", "i.wr", "S.3", "R.2", "S.4", "Q.0", "Q.2",
    "R.1", "a.e2", "Q.3", "Q.1", "a.wr", "L.all",
)


def window_body(
    tokens, cotangent, masked_pos, rand_blocks, ln1_gain, ln1_bias, w_query, b_query, w_key,
    w_value, b_value, w_out, b_out, ln2_gain, ln2_bias, w_inner, b_inner, w_outer, b_outer,
):
    windows, rows, width = tokens.shape
    local = w_query.shape[1]
    hidden = w_inner.shape[1]
    total = windows * rows
    blocks = total // BS
    run = rows // 2
    split = width // 2
    place = lax.axis_index("seq")
    core = lax.axis_index("tensor")
    plane, line = stages_of(0)[:2], stages_of(0)[2:]
    bits = jnp.stack(
        [bit_of(*step) for step in plane]
        + [core.astype(jnp.int32)]
        + [bit_of(*step) for step in line]
        + [place.astype(jnp.int32)]
    )

    cut = tokens.reshape(windows, 2, run, width)
    own_rows = []
    for at in range(windows):
        piece = lax.dynamic_slice(cut, (place ^ at, core, 0, 0), (1, 1, run, width))
        piece = piece.reshape(run, width)
        own_rows.append(piece if at == 0 else flip(piece, "seq", at))

    named = masked_pos.shape[1]
    count = -(-named // 16) * 16
    spots = jnp.concatenate(
        [masked_pos, jnp.full((windows, count - named), -1, jnp.int32)], axis=1
    )
    slot = jnp.arange(count, dtype=jnp.int32)
    again = jnp.any(
        (spots[:, :, None] == spots[:, None, :]) & (slot[None, :] < slot[:, None])[None], axis=2
    )
    spots = jnp.where(again, -1, spots)
    spot = lax.dynamic_index_in_dim(spots, place, 0, keepdims=True).reshape(count, 1)
    there, inside = (spot // rows) ^ place, spot % rows
    pos = jnp.where(spot >= 0, there * rows + inside, -1)
    mine = (spot >= 0) & (inside // run == core)
    pos_half = jnp.where(mine, there * run + inside % run, -1)

    here = spots - place * rows
    found = []
    for at in range(windows):
        named_rows = lax.dynamic_index_in_dim(here, place ^ at, 0, keepdims=False)
        pick = (named_rows[:, None] == jnp.arange(rows, dtype=jnp.int32)[None, :]).astype(
            jnp.bfloat16
        )
        shard = lax.dynamic_slice(
            cotangent, (place ^ at, 0, core * split), (1, rows, split)
        ).reshape(rows, split)
        found.append(dot_nn(pick, shard).astype(jnp.bfloat16))

    rand = lax.dynamic_index_in_dim(rand_blocks, place, 0, keepdims=False)
    numbers = jnp.arange(blocks, dtype=jnp.int32)
    shard_blocks = rows // BS
    ids = ((numbers // shard_blocks) ^ place) * shard_blocks + numbers % shard_blocks
    named_blocks = jnp.any(rand[:, :, None] == ids[None, None, :], axis=1)
    named_blocks = jnp.any(
        (ids[:, None] == numbers[None, :])[:, :, None] & named_blocks[None], axis=1
    )
    listed = (
        (jnp.abs(ids[:, None] - ids[None, :]) <= 1)
        | (ids == 0)[None, :]
        | (ids == blocks - 1)[None, :]
        | named_blocks
    )
    allow = jnp.repeat(listed.astype(jnp.bfloat16), BS, axis=1)

    rows_wide = [ln1_gain, ln1_bias, b_out, ln2_gain, ln2_bias, b_outer, b_query, b_value, b_inner]
    vec = jnp.concatenate([x.astype(jnp.float32) for x in rows_wide]).reshape(-1, width)

    order = Order()
    state = None
    for at in range(windows):
        if at == 1:
            order.need(pos, pos_half, allow, *own_rows[1:], *found)
        kept = () if state is None else tuple(state)
        over = own_rows[at] if at == 0 else after(own_rows[at], entry)
        state = order.call(
            functools.partial(shard_kernel, at),
            [shape((total, width))] * 2 + [shape((total, local))] * 3,
            (bits, own_rows[at], flip(over, "tensor", 1), vec, w_query, w_key, w_value) + kept,
            aliases={7 + i: i for i in range(len(kept))},
        )
        if at == 0:
            entry = order.last
    tok, h, q, k, v = state
    found = [found[0]] + [
        flip(after(found[i], *own_rows[1:]), "seq", i) for i in range(1, windows)
    ]
    xm, hm, qm, om, lse, part = order.call(
        front_kernel,
        [shape((count, width))] * 2
        + [shape((count, local))] * 2
        + [shape((count, LANES), jnp.float32), shape((count, width))],
        (bits, pos, allow, w_out, tok, h, q, k, v),
    )
    other = flip(part, "tensor", 1)
    (g_own,) = order.call(sum_rows_kernel, [shape((count, split))], (bits, *found))
    g_other = flip(g_own, "tensor", 1)
    outs = order.call(
        hidden_kernel,
        [shape((1, width // 2, width))] * 8
        + [shape((count, width)), shape((1 + hidden // width, width), jnp.float32)]
        + [shape((count, width))],
        (bits, xm, part, other, g_own, g_other, vec, w_inner, w_outer),
        scratch=[
            pltpu.VMEM((count, hidden), jnp.bfloat16),
            pltpu.VMEM((count, width), jnp.bfloat16),
            pltpu.VMEM((count, hidden), jnp.bfloat16),
        ],
    )
    wf_a, wf_as, wf_b, wf_bs, wi_a, wi_as, wi_b, wi_bs, dh2, few_hidden, g = outs
    sum_f = Summing(order, bits, (wf_a, wf_b), (wf_as, wf_bs))
    sum_i = Summing(order, bits, (wi_a, wi_b), (wi_as, wi_bs))

    held = {}
    sum_f.exchange(0)
    dh2_other = flip(dh2, "tensor", 1)
    outs = order.call(
        attend_back_kernel,
        [shape((1, width // 2, 2 * local))] * 2
        + [shape((1, width // 2, local + width // 2))] * 2
        + [shape((count, width), jnp.float32), shape((count, local))]
        + [shape((total, local))] * 2
        + [shape((4, width), jnp.float32)],
        (bits, xm, part, other, g, dh2, dh2_other, vec, w_out, pos, allow)
        + (qm, om, hm, lse, h, k, v),
        scratch=[
            pltpu.VMEM((count, width), jnp.bfloat16),
            pltpu.VMEM((count, local), jnp.bfloat16),
        ],
    )
    da_a, da_as, da_b, da_bs, dx1, dq, dk, dv, few_attend = outs
    sum_a = Summing(order, bits, (da_a, da_b), (da_as, da_bs))

    def attend(at):
        keep, send = order.call(
            functools.partial(attend_kernel, at),
            [shape((run, local))] * 2,
            (bits, q, k, v, allow),
            scratch=[pltpu.VMEM((rows, local), jnp.bfloat16)],
        )
        held.setdefault("keep", []).append(keep)
        held.setdefault("send", []).append(send)

    def feed(base, pieces):
        span = slice(base, base + pieces)
        held["pair"][span] = order.call(
            functools.partial(feed_kernel, base, pieces),
            [shape((2, run, width))] * pieces,
            (bits, *own_rows[span], *held["keep"][span], held["mixed_other"], vec)
            + (held["bi"], w_out, held["wo"], w_inner, held["wi"], w_outer, held["wf"])
            + tuple(held["pair"][span]),
            scratch=[pltpu.VMEM((pieces * run, width), jnp.float32)],
            aliases={10 + 2 * pieces + i: i for i in range(pieces)},
        )

    small_steps = iter(stages_of(0)[::-1])
    sums = {"f": sum_f, "i": sum_i, "a": sum_a}

    def swap(value, kernels=2):
        other = flip(after(value, order.last), "tensor", 1)
        order.soon(other, kernels)
        return other

    def sum_step(of, step):
        one = sums[of]
        if step == "go":
            one.hold(order.last)
            one.exchange(0)
        elif step == "h1":
            one.halve_first()
            one.exchange(1)
        elif step == "h2":
            one.halve_second()
            held[of] = one.exchange_line(0)
        elif step == "l0":
            one.halve_line(0, held[of])
            held[of] = one.exchange_line(1)
        elif step == "l1":
            one.halve_line(1, held[of])
            held[of] = one.exchange_line(1)
        elif step == "d1":
            one.double_line(1, held[of])
            held[of] = one.exchange_line(0)
        elif step == "d0":
            one.double_line(0, held[of])
            one.exchange(1)
        elif step == "e2":
            one.double_second()
            one.exchange(0)
        elif of == "f":
            (held["grad_wf"],) = one.write(last_rows_kernel, [(hidden, width)])
        elif of == "i":
            (held["grad_wi"],) = one.write(last_columns_kernel, [(width, hidden)])
        else:
            held["grad_a"] = one.write(last_attend_kernel, [(width, local)] * 3 + [(local, width)])

    def input_grad():
        held["dh_own"], dh_send = order.call(
            input_kernel,
            [shape((total // 2, width))] * 2,
            (bits, pos, dq, dk, dv, w_query, w_key, w_value),
            scratch=[pltpu.VMEM((total, local), jnp.bfloat16)],
        )
        held["dh_other"] = flip(dh_send, "tensor", 1)

    def first_norm():
        *held["pair"], held["few"] = order.call(
            functools.partial(first_norm_kernel, windows),
            [shape((2, run, width))] * windows + [shape((2, width), jnp.float32)],
            (bits, pos_half, held["dh_own"], dx1, vec, *own_rows, held["dh_other"]),
            scratch=[pltpu.VMEM((total // 2, width), jnp.bfloat16)] * 2,
        )
        held["few_other"] = flip(held["few"], "tensor", 1)
        order.soon(held["few_other"])

    def small(step):
        if step == "0":
            (held["small"],) = order.call(
                gather_small_kernel,
                [shape((7 + hidden // width, width), jnp.float32)],
                (bits, held["few"], held["few_other"], few_attend, few_hidden),
            )
        else:
            (held["small"],) = order.call(
                add_small_kernel,
                [shape(held["small"].shape, jnp.float32)],
                (bits, held["small"], held["small_other"]),
            )
        if step != "4":
            held["small_other"] = flip(held["small"], *next(small_steps))

    def send_back(at):
        held["pair"][at] = flip(after(held["pair"][at], order.last), "seq", at)
        order.soon(held["pair"][at], 3)

    def swap_back(at):
        held.setdefault("over", {})[at] = swap(held["pair"][at])

    def interleave():
        over = [held["over"][at] for at in range(windows)]
        held["all"] = order.call(
            interleave_kernel,
            [shape((windows, rows, width))] * 2,
            (bits, *held["pair"], *over),
        )

    for step in STEPS:
        kind, what = step[0], step[2:]
        if kind in sums:
            sum_step(kind, what)
        elif kind == "A":
            attend(int(what))
        elif kind == "F":
            feed(int(what) * windows // 2, windows // 2)
        elif kind == "W":
            held[what] = swap({"wi": w_inner, "wf": w_outer, "wo": w_out, "bi": vec[7:]}[what])
        elif kind == "X":
            laid = order.call(lay_kernel, [shape((windows * run, local))], (bits, *held["send"]))
            held["mixed_other"] = swap(laid[0])
        elif kind == "S":
            small(what)
        elif kind == "R":
            send_back(int(what))
        elif kind == "Q":
            swap_back(int(what))
        elif kind == "L":
            interleave()
        elif kind == "I":
            input_grad()
        else:
            first_norm()
    grad_tokens, out = held["all"]
    grad_q, grad_k, grad_v, grad_o = held["grad_a"]
    grad_wf, grad_wi, small_all = held["grad_wf"], held["grad_wi"], held["small"]
    return (
        out,
        grad_tokens,
        small_all[0],
        small_all[1],
        grad_q,
        small_all[5, :local],
        grad_k,
        grad_v,
        small_all[5, local:],
        grad_o,
        small_all[4],
        small_all[2],
        small_all[3],
        grad_wi,
        small_all[7:].reshape(-1),
        grad_wf,
        small_all[6],
    )


def with_halo(block, sides, width):
    for axis, dim in sides:
        count = lax.axis_size(axis)
        forward = [(i, i + 1) for i in range(count - 1)]
        backward = [(target, source) for source, target in forward]
        low = lax.ppermute(
            lax.slice_in_dim(block, block.shape[dim] - width, None, axis=dim), axis, forward
        )
        high = lax.ppermute(lax.slice_in_dim(block, 0, width, axis=dim), axis, backward)
        block = jnp.concatenate([low, block, high], axis=dim)
    return block


def broadcast(value, axis, root):
    mine = lax.axis_index(axis) == root
    return lax.psum(jnp.where(mine, value, jnp.zeros_like(value)), axis)


def norm_forward(values, gain, shift):
    center = values - jnp.mean(values, axis=-1, keepdims=True)
    scaled = lax.rsqrt(jnp.mean(center * center, axis=-1, keepdims=True) + eps_norm)
    normed = center * scaled
    return (normed * gain + shift, normed, scaled)


def norm_backward(upstream, gain, normed, scaled):
    weighted = upstream * gain
    centered = weighted - jnp.mean(weighted, axis=-1, keepdims=True)
    return scaled * (centered - normed * jnp.mean(weighted * normed, axis=-1, keepdims=True))


def row_dot(left, right):
    return lax.dot_general(
        left, right, (((left.ndim - 1,), (0,)), ((), ())), preferred_element_type=jnp.float32
    )


def back_dot(left, right):
    return lax.dot_general(
        left, right, (((left.ndim - 1,), (1,)), ((), ())), preferred_element_type=jnp.float32
    )


def outer_sum(left, right):
    return lax.dot_general(
        left, right, (((0, 1), (0, 1)), ((), ())), preferred_element_type=jnp.float32
    )


def column_sum(values):
    return jnp.sum(values, axis=(0, 1), dtype=jnp.float32)


def list_masks(rand_local, first_block, block_count):
    window_count, local_count = (rand_local.shape[0], rand_local.shape[1])
    query_ids = first_block + jnp.arange(local_count, dtype=jnp.int32)
    slide_ok = jnp.stack(
        [query_ids - 1 >= 0, query_ids >= 0, query_ids + 1 <= block_count - 1], axis=1
    )
    end_ok = jnp.stack([jnp.abs(query_ids) > 1, jnp.abs(block_count - 1 - query_ids) > 1], axis=1)
    rand_ok = (
        (jnp.abs(rand_local - query_ids[None, :, None]) > 1)
        & (rand_local != 0)
        & (rand_local != block_count - 1)
    )
    fixed_ok = jnp.broadcast_to(
        jnp.concatenate([slide_ok, end_ok], axis=1)[None], (window_count, local_count, 5)
    )
    return jnp.concatenate([fixed_ok, rand_ok], axis=-1)


def build_routing(rand_batch, position, devices, local_count, capacity):
    window_count = rand_batch.shape[0]
    item_count = window_count * local_count * 3

    def arrange(grid_values):
        grid_values = grid_values.reshape(window_count, devices, local_count, 3)
        return jnp.transpose(grid_values, (1, 0, 2, 3)).reshape(devices, item_count)

    window_grid = jnp.broadcast_to(
        jnp.arange(window_count, dtype=jnp.int32)[:, None, None], rand_batch.shape
    )
    owner_table = arrange(rand_batch // local_count)
    source_table = arrange(window_grid * local_count + rand_batch % local_count)
    device_ids = jnp.arange(devices, dtype=jnp.int32)
    matches = (owner_table[:, :, None] == device_ids[None, None, :]).astype(jnp.int32)
    earlier = jnp.cumsum(matches, axis=1) - matches
    slot_table = jnp.sum(earlier * matches, axis=2)
    owned_here = (owner_table == position).astype(jnp.int32)
    slot_ids = jnp.arange(capacity, dtype=jnp.int32)
    slot_matches = (slot_table[:, :, None] == slot_ids[None, None, :]).astype(
        jnp.int32
    ) * owned_here[:, :, None]
    send_rows = jnp.sum(slot_matches * source_table[:, :, None], axis=1).reshape(devices * capacity)
    send_live = jnp.sum(slot_matches, axis=1).reshape(devices * capacity)
    my_owner = lax.dynamic_index_in_dim(owner_table, position, 0, keepdims=False)
    my_slot = lax.dynamic_index_in_dim(slot_table, position, 0, keepdims=False)
    take_rows = my_owner * capacity + my_slot
    return (send_rows, send_live, take_rows)


def fetch_blocks(packed, routing, block_rows):
    window_count, local_rows, kv_width = packed.shape
    local_count = local_rows // block_rows
    devices = lax.axis_size("seq")
    padded = with_halo(packed, (("seq", 1),), block_rows)
    padded = padded.reshape(window_count, local_count + 2, block_rows, kv_width)
    sliding = jnp.stack([padded[:, offset : offset + local_count] for offset in range(3)], axis=2)
    first_part = broadcast(packed[:, :block_rows], "seq", 0)
    last_part = broadcast(packed[:, local_rows - block_rows :], "seq", devices - 1)
    end_blocks = jnp.stack([first_part, last_part], axis=1)
    end_blocks = jnp.broadcast_to(
        end_blocks[:, None], (window_count, local_count, 2, block_rows, kv_width)
    )
    send_rows, send_live, take_rows = routing
    sources = packed.reshape(window_count * local_count, block_rows, kv_width)
    outgoing = jnp.take(sources, send_rows, axis=0).reshape(devices, -1, block_rows, kv_width)
    incoming = lax.all_to_all(outgoing, "seq", split_axis=0, concat_axis=0, tiled=True).reshape(
        -1, block_rows, kv_width
    )
    fetched = jnp.take(incoming, take_rows, axis=0).reshape(
        window_count, local_count, 3, block_rows, kv_width
    )
    return jnp.concatenate([sliding, end_blocks, fetched], axis=2)


def return_blocks(kv_grads, routing, block_rows):
    window_count, local_count = (kv_grads.shape[0], kv_grads.shape[1])
    kv_width = kv_grads.shape[-1]
    local_rows = local_count * block_rows
    devices = lax.axis_size("seq")
    position = lax.axis_index("seq")
    padded_grad = jnp.zeros((window_count, local_count + 2, block_rows, kv_width), jnp.float32)
    for offset in range(3):
        padded_grad = padded_grad.at[:, offset : offset + local_count].add(kv_grads[:, :, offset])
    rim_rows = jnp.concatenate([padded_grad[:, 0], padded_grad[:, local_count + 1]], axis=1)
    rim_back = with_halo(rim_rows.astype(jnp.bfloat16), (("seq", 1),), block_rows).astype(
        rim_rows.dtype
    )
    end_grads = lax.psum(jnp.sum(kv_grads[:, :, 3:5], axis=1).astype(jnp.bfloat16), "seq").astype(
        jnp.float32
    )
    zeros_block = jnp.zeros((window_count, block_rows, kv_width), jnp.float32)
    first_add = rim_back[:, :block_rows] + jnp.where(position == 0, end_grads[:, 0], zeros_block)
    last_add = rim_back[:, 3 * block_rows :] + jnp.where(
        position == devices - 1, end_grads[:, 1], zeros_block
    )
    send_rows, send_live, take_rows = routing
    rand_items = kv_grads[:, :, 5:8].reshape(-1, block_rows, kv_width)
    capacity_rows = send_rows.shape[0]
    outgoing = (
        jnp.zeros((capacity_rows, block_rows, kv_width), jnp.float32).at[take_rows].set(rand_items)
    )
    incoming = lax.all_to_all(
        outgoing.reshape(devices, -1, block_rows, kv_width).astype(jnp.bfloat16),
        "seq",
        split_axis=0,
        concat_axis=0,
        tiled=True,
    ).astype(jnp.float32)
    incoming = (
        incoming.reshape(capacity_rows, block_rows, kv_width)
        * send_live.astype(jnp.float32)[:, None, None]
    )
    from_owners = (
        jnp.zeros((window_count * local_count, block_rows, kv_width), jnp.float32)
        .at[send_rows]
        .add(incoming)
    )
    summed = padded_grad[:, 1 : local_count + 1].reshape(window_count, local_rows, kv_width)
    summed = summed + from_owners.reshape(window_count, local_rows, kv_width)
    summed = summed.at[:, :block_rows].add(first_add)
    summed = summed.at[:, local_rows - block_rows :].add(last_add)
    return summed


def split_scores(query_low, keyset, key_valid):
    window_count, local_rows, local_width = query_low.shape
    local_count = keyset.shape[1]
    head_count = local_width // HD
    key_rows = keyset.shape[2] * BS
    query_split = query_low.reshape(window_count, local_count, BS, head_count, HD)
    paired = keyset.reshape(window_count, local_count, key_rows, 2, head_count, HD)
    key_part = paired[:, :, :, 0]
    value_part = paired[:, :, :, 1]
    scores = jnp.einsum(
        "wbqhd,wbkhd->wbhqk", query_split, key_part, preferred_element_type=jnp.float32
    ) * HD ** (-0.5)
    allowed = jnp.repeat(key_valid, BS, axis=2)[:, :, None, None, :]
    scores = jnp.where(allowed, scores, -1e30)
    return (scores, query_split, key_part, value_part)


def attend_forward(query_low, keyset, key_valid):
    scores, query_split, key_part, value_part = split_scores(query_low, keyset, key_valid)
    top_score = jnp.max(scores, axis=-1, keepdims=True)
    log_total = top_score + jnp.log(jnp.sum(jnp.exp(scores - top_score), axis=-1, keepdims=True))
    weights = jnp.exp(scores - log_total).astype(jnp.bfloat16)
    mixed = jnp.einsum(
        "wbhqk,wbkhd->wbqhd", weights, value_part, preferred_element_type=jnp.float32
    )
    return (mixed.reshape(query_low.shape).astype(jnp.bfloat16), log_total)


def attend_backward(query_low, keyset, key_valid, log_total, grad_mixed):
    scores, query_split, key_part, value_part = split_scores(query_low, keyset, key_valid)
    window_count, local_count = (keyset.shape[0], keyset.shape[1])
    local_width = query_low.shape[2]
    weights = jnp.exp(scores - log_total)
    grad_split = grad_mixed.reshape(query_split.shape)
    grad_weights = jnp.einsum(
        "wbqhd,wbkhd->wbhqk", grad_split, value_part, preferred_element_type=jnp.float32
    )
    delta_sum = jnp.sum(weights * grad_weights, axis=-1, keepdims=True)
    grad_scores = (weights * (grad_weights - delta_sum)).astype(jnp.bfloat16)
    grad_query = jnp.einsum(
        "wbhqk,wbkhd->wbqhd", grad_scores, key_part, preferred_element_type=jnp.float32
    ) * HD ** (-0.5)
    grad_key = jnp.einsum(
        "wbhqk,wbqhd->wbkhd", grad_scores, query_split, preferred_element_type=jnp.float32
    ) * HD ** (-0.5)
    grad_value = jnp.einsum(
        "wbhqk,wbqhd->wbkhd",
        weights.astype(jnp.bfloat16),
        grad_split,
        preferred_element_type=jnp.float32,
    )
    list_shape = (window_count, local_count, keyset.shape[2], BS, local_width)
    kv_grads = jnp.concatenate(
        [grad_key.reshape(list_shape), grad_value.reshape(list_shape)], axis=-1
    )
    return (grad_query.reshape(query_low.shape), kv_grads)


def flatten_all(members):
    return jnp.concatenate([member.reshape(-1) for member in members])


def share_sum(vector):
    return lax.psum_scatter(vector, ("dp", "seq"), scatter_dimension=0, tiled=True)


def spread_body(
    tokens,
    cotangent,
    masked_pos,
    rand_blocks,
    ln1_gain,
    ln1_bias,
    w_query,
    b_query,
    w_key,
    w_value,
    b_value,
    w_out,
    b_out,
    ln2_gain,
    ln2_bias,
    w_inner,
    b_inner,
    w_outer,
    b_outer,
):
    local_rows = tokens.shape[1]
    devices = lax.axis_size("seq")
    position = lax.axis_index("seq")
    block_count = rand_blocks.shape[1]
    local_count = block_count // devices
    capacity = (3 * WIN_MB * local_count + devices - 1) // devices
    gain_one = ln1_gain.astype(jnp.float32)
    bias_one = ln1_bias.astype(jnp.float32)
    gain_two = ln2_gain.astype(jnp.float32)
    bias_two = ln2_bias.astype(jnp.float32)
    row_ids = position * local_rows + jnp.arange(local_rows, dtype=jnp.int32)
    first_block = position * local_count
    outputs = []
    input_grads = []
    totals = None
    for batch_index in range(MB):
        batch_start = batch_index * WIN_MB
        batch_stop = batch_start + WIN_MB
        tokens_now = tokens[batch_start:batch_stop].astype(jnp.float32)
        rand_now = rand_blocks[batch_start:batch_stop]
        routing = build_routing(rand_now, position, devices, local_count, capacity)
        rand_local = lax.dynamic_slice_in_dim(rand_now, first_block, local_count, 1)
        key_valid = list_masks(rand_local, first_block, block_count)
        hidden_one, normed_one, scaled_one = norm_forward(tokens_now, gain_one, bias_one)
        hidden_low = hidden_one.astype(jnp.bfloat16)
        query_low = (row_dot(hidden_low, w_query) + b_query.astype(jnp.float32)).astype(
            jnp.bfloat16
        )
        key_low = row_dot(hidden_low, w_key).astype(jnp.bfloat16)
        value_low = (row_dot(hidden_low, w_value) + b_value.astype(jnp.float32)).astype(
            jnp.bfloat16
        )
        packed = jnp.concatenate([key_low, value_low], axis=2)
        keyset = fetch_blocks(packed, routing, BS)
        mixed_low, log_total = attend_forward(query_low, keyset, key_valid)
        attn_out = lax.psum(row_dot(mixed_low, w_out).astype(jnp.bfloat16), "tensor").astype(
            jnp.float32
        ) + b_out.astype(jnp.float32)
        middle = tokens_now + attn_out
        hidden_two, normed_two, scaled_two = norm_forward(middle, gain_two, bias_two)
        hidden_two_low = hidden_two.astype(jnp.bfloat16)
        inner_pre = row_dot(hidden_two_low, w_inner) + b_inner.astype(jnp.float32)
        active = jax.nn.gelu(inner_pre, approximate=False).astype(jnp.bfloat16)
        ffn_out = lax.psum(row_dot(active, w_outer).astype(jnp.bfloat16), "tensor").astype(
            jnp.float32
        ) + b_outer.astype(jnp.float32)
        outputs.append((middle + ffn_out).astype(jnp.bfloat16))
        masked_now = masked_pos[batch_start:batch_stop]
        chosen = jnp.any(row_ids[None, :, None] == masked_now[:, None, :], axis=2)
        cot_now = cotangent[batch_start:batch_stop]
        grad_top = jnp.where(chosen[:, :, None], cot_now, jnp.zeros_like(cot_now))
        grad_active = back_dot(grad_top, w_outer)
        normal_cdf = 0.5 * (1.0 + lax.erf(inner_pre * inv_root_two))
        density = jnp.exp(-0.5 * inner_pre * inner_pre) * inv_root_two_pi
        grad_inner = (grad_active * (normal_cdf + inner_pre * density)).astype(jnp.bfloat16)
        grad_hidden_two = lax.psum(
            back_dot(grad_inner, w_inner).astype(jnp.bfloat16), "tensor"
        ).astype(jnp.float32)
        grad_middle = grad_top.astype(jnp.float32) + norm_backward(
            grad_hidden_two, gain_two, normed_two, scaled_two
        )
        grad_attn = grad_middle.astype(jnp.bfloat16)
        grad_mixed = back_dot(grad_attn, w_out).astype(jnp.bfloat16)
        keyset_back = fetch_blocks(packed, routing, BS)
        grad_query, kv_grads = attend_backward(
            query_low, keyset_back, key_valid, log_total, grad_mixed
        )
        grad_query = grad_query.astype(jnp.bfloat16)
        grad_packed = return_blocks(kv_grads, routing, BS)
        local_width = query_low.shape[2]
        grad_key = grad_packed[:, :, :local_width].astype(jnp.bfloat16)
        grad_value = grad_packed[:, :, local_width:].astype(jnp.bfloat16)
        grad_partial = (
            back_dot(grad_query, w_query)
            + back_dot(grad_key, w_key)
            + back_dot(grad_value, w_value)
        )
        grad_hidden_one = lax.psum(grad_partial.astype(jnp.bfloat16), "tensor").astype(jnp.float32)
        grad_tokens_now = grad_middle + norm_backward(
            grad_hidden_one, gain_one, normed_one, scaled_one
        )
        input_grads.append(grad_tokens_now.astype(jnp.bfloat16))
        batch_grads = (
            jnp.sum(grad_hidden_one * normed_one, axis=(0, 1)),
            jnp.sum(grad_hidden_one, axis=(0, 1)),
            outer_sum(hidden_low, grad_query),
            column_sum(grad_query),
            outer_sum(hidden_low, grad_key),
            outer_sum(hidden_low, grad_value),
            column_sum(grad_value),
            outer_sum(mixed_low, grad_attn),
            column_sum(grad_attn),
            jnp.sum(grad_hidden_two * normed_two, axis=(0, 1)),
            jnp.sum(grad_hidden_two, axis=(0, 1)),
            outer_sum(hidden_two_low, grad_inner),
            column_sum(grad_inner),
            outer_sum(active, grad_top),
            column_sum(grad_top),
        )
        totals = batch_grads if totals is None else jax.tree.map(jnp.add, totals, batch_grads)
    final_share = share_sum(flatten_all(totals))
    gathered = lax.all_gather(
        final_share.astype(jnp.bfloat16), ("dp", "seq"), axis=0, tiled=True
    ).astype(final_share.dtype)
    param_shapes = [
        member.shape
        for member in (
            ln1_gain,
            ln1_bias,
            w_query,
            b_query,
            w_key,
            w_value,
            b_value,
            w_out,
            b_out,
            ln2_gain,
            ln2_bias,
            w_inner,
            b_inner,
            w_outer,
            b_outer,
        )
    ]
    results = []
    cursor = 0
    for shape_now in param_shapes:
        length = 1
        for extent in shape_now:
            length = length * extent
        results.append(gathered[cursor : cursor + length].reshape(shape_now))
        cursor = cursor + length
    out_all = jnp.concatenate(outputs, axis=0)
    grad_all = jnp.concatenate(input_grads, axis=0)
    return (
        out_all,
        grad_all,
        results[0],
        results[1],
        results[2],
        results[3],
        results[4],
        results[5],
        results[6],
        results[7],
        results[8],
        results[9],
        results[10],
        results[11],
        results[12],
        results[13],
        results[14],
    )


def power_of_two(number):
    return number & (number - 1) == 0


def body(tokens, *rest):
    dp, seq, tensor = (lax.axis_size(axis) for axis in ("dp", "seq", "tensor"))
    fits = seq == tokens.shape[0] and tensor == 2 and dp == 4 and power_of_two(seq)
    return (window_body if fits else spread_body)(tokens, *rest)


def solution(mesh):
    in_specs = (
        P("dp", "seq", None),
        P("dp", "seq", None),
        P("dp", None),
        P("dp", None, None),
        P(),
        P(),
        P(None, "tensor"),
        P("tensor"),
        P(None, "tensor"),
        P(None, "tensor"),
        P("tensor"),
        P("tensor", None),
        P(),
        P(),
        P(),
        P(None, "tensor"),
        P("tensor"),
        P("tensor", None),
        P(),
    )
    out_specs = (
        P("dp", "seq", None),
        P("dp", "seq", None),
        P(),
        P(),
        P(None, "tensor"),
        P("tensor"),
        P(None, "tensor"),
        P(None, "tensor"),
        P("tensor"),
        P("tensor", None),
        P(),
        P(),
        P(),
        P(None, "tensor"),
        P("tensor"),
        P("tensor", None),
        P(),
    )
    return jax.shard_map(body, mesh=mesh, in_specs=in_specs, out_specs=out_specs, check_vma=False)
```

```python
import functools

import jax
import jax.numpy as jnp
from jax import lax
from jax.experimental import pallas as pl
from jax.experimental.pallas import tpu as pltpu
from jax.sharding import PartitionSpec as P

HD = 64
BS = 64
MB = 2
WIN_MB = 2


eps_norm = 1e-05
inv_root_two = 0.7071067811865476
inv_root_two_pi = 0.3989422804014327


LANES = 128
NEG = -1e30
VMEM_LIMIT = 16 * 1024 * 1024


def dot_nn(left, right):
    return lax.dot_general(left, right, (((1,), (0,)), ((), ())), preferred_element_type=jnp.float32)


def dot_nt(left, right):
    return lax.dot_general(left, right, (((1,), (1,)), ((), ())), preferred_element_type=jnp.float32)


def dot_tn(left, right):
    return lax.dot_general(left, right, (((0,), (0,)), ((), ())), preferred_element_type=jnp.float32)


def norm_parts(values):
    center = values - jnp.mean(values, axis=-1, keepdims=True)
    scaled = lax.rsqrt(jnp.mean(center * center, axis=-1, keepdims=True) + eps_norm)
    return center * scaled, scaled


def pick_rows(positions, total):
    ids = lax.broadcasted_iota(jnp.int32, (positions.shape[0], total), 1)
    return jnp.where(ids == positions, 1.0, 0.0).astype(jnp.bfloat16)


def row_lists(blocks, allow):
    ids = lax.broadcasted_iota(jnp.int32, (blocks.shape[0], allow.shape[0]), 1)
    return dot_nn(jnp.where(ids == blocks, 1.0, 0.0).astype(jnp.bfloat16), allow)


def head_half(half):
    lane = lax.broadcasted_iota(jnp.int32, (1, LANES), 1)
    return (lane < HD) if half == 0 else (lane >= HD)


def one_head(slab, half):
    return jnp.where(head_half(half), slab, jnp.zeros_like(slab))


class Order:
    def __init__(self):
        self.last = None
        self.needed = []
        self.later = []

    def soon(self, array, kernels=2):
        self.later.append([kernels, array])

    def need(self, *arrays):
        self.needed += arrays

    def call(self, kernel, outs, args, smem=1, scratch=(), aliases=None):
        first = args[0]
        for entry in self.later:
            entry[0] -= 1
        self.needed += [array for left, array in self.later if left == 0]
        self.later = [entry for entry in self.later if entry[0] > 0]
        if self.last is not None:
            first = after(first, self.last, *self.needed)
            self.needed = []
        spec = pl.BlockSpec(memory_space=pltpu.VMEM)
        found = pl.pallas_call(
            kernel,
            name=getattr(kernel, "func", kernel).__name__.removesuffix("_kernel"),
            out_shape=outs,
            in_specs=[pl.BlockSpec(memory_space=pltpu.SMEM)] * smem + [spec] * (len(args) - smem),
            out_specs=[spec] * len(outs),
            scratch_shapes=list(scratch),
            input_output_aliases=aliases or {},
            compiler_params=pltpu.CompilerParams(vmem_limit_bytes=VMEM_LIMIT),
            cost_estimate=pl.CostEstimate(flops=1, bytes_accessed=1, transcendentals=0),
        )(first, *args[1:])
        self.last = min(found, key=lambda a: a.size)
        return found


def after(value, *others):
    return lax.optimization_barrier((value, others))[0]


def shape(dims, dtype=jnp.bfloat16):
    return jax.ShapeDtypeStruct(dims, dtype)


def shard_kernel(at, bits, own, other, vec, wq, wk, wv, *rest):
    tok, h, q, k, v = rest[-5:]
    run = own.shape[0]
    local = wq.shape[1]

    def keep_rows(before, carry):
        rows = pl.ds(pl.multiple_of(before * 2 * run, 2 * run), 2 * run)
        for kept, out in zip(rest[:-5], rest[-5:]):
            out[rows, :] = kept[rows, :]
        return carry

    if at:
        lax.fori_loop(0, at, keep_rows, 0)

    def one_half(half, carry):
        rows = pl.ds(pl.multiple_of((2 * at + half) * run, run), run)
        low_rows = jnp.where(half == bits[2], own[...], other[...])
        tok[rows, :] = low_rows
        normed, _ = norm_parts(low_rows.astype(jnp.float32))
        low = (normed * vec[0:1, :] + vec[1:2, :]).astype(jnp.bfloat16)
        h[rows, :] = low
        q[rows, :] = (dot_nn(low, wq[...]) + vec[6:7, :local]).astype(jnp.bfloat16)
        k[rows, :] = dot_nn(low, wk[...]).astype(jnp.bfloat16)
        v[rows, :] = (dot_nn(low, wv[...]) + vec[6:7, local:]).astype(jnp.bfloat16)
        return carry

    lax.fori_loop(0, 2, one_half, 0)


def sum_rows_kernel(bits, *refs):
    total = None
    for piece in refs[:-1]:
        value = piece[...].astype(jnp.float32)
        total = value if total is None else total + value
    refs[-1][...] = total.astype(jnp.bfloat16)


def front_kernel(bits, pos, allow, wo, tok, h, q, k, v, xm, hm, qm, om, lse, part):
    total, local = q.shape
    pick = pick_rows(pos[...], total)
    xm[...] = dot_nn(pick, tok[...]).astype(jnp.bfloat16)
    hm[...] = dot_nn(pick, h[...]).astype(jnp.bfloat16)
    qm[...] = dot_nn(pick, q[...]).astype(jnp.bfloat16)
    listed = row_lists(pos[...] >> 6, allow[...]) > 0.5
    lane = lax.broadcasted_iota(jnp.int32, (pos.shape[0], LANES), 1)

    def one_slab(slab, sums):
        cols = pl.ds(pl.multiple_of(slab * LANES, LANES), LANES)
        query = (qm[:, cols].astype(jnp.float32) * HD ** (-0.5)).astype(jnp.bfloat16)
        mixed = None
        for half in range(2):
            scores = jnp.where(listed, dot_nt(one_head(query, half), k[:, cols]), NEG)
            top = jnp.max(scores, axis=-1, keepdims=True)
            weight = jnp.exp(scores - top)
            total_weight = jnp.sum(weight, axis=-1, keepdims=True)
            sums = jnp.where(lane == 2 * slab + half, top + jnp.log(total_weight), sums)
            found = dot_nn(weight.astype(jnp.bfloat16), v[:, cols]) * (1.0 / total_weight)
            mixed = found if half == 0 else jnp.where(head_half(0), mixed, found)
        om[:, cols] = mixed.astype(jnp.bfloat16)
        return sums

    none = jnp.zeros((pos.shape[0], LANES), jnp.float32)
    sums = lax.fori_loop(0, local // LANES, one_slab, none)
    lse[...] = sums
    part[...] = dot_nn(om[...], wo[...]).astype(jnp.bfloat16)


def gelu_parts(z):
    cdf = 0.5 * (1.0 + lax.erf(z * inv_root_two))
    return z * cdf, cdf + z * (jnp.exp(-0.5 * z * z) * inv_root_two_pi)


def middle_of(xm, part, other, vec):
    both = part[...].astype(jnp.float32) + other[...].astype(jnp.float32)
    return xm[...].astype(jnp.float32) + (both + vec[2:3, :])


def hidden_kernel(
    bits, xm, part, other, g_own, g_other, vec, wi, wf,
    wf_a, wf_as, wf_b, wf_bs, wi_a, wi_as, wi_b, wi_bs, dh2, few, g,
    u_all, h2_all, dz_all,
):
    width, hidden = wi.shape
    split = width // 2
    first = bits[2] == 0
    g[:, :split] = jnp.where(first, g_own[...], g_other[...])
    g[:, split:] = jnp.where(first, g_other[...], g_own[...])
    normed, _ = norm_parts(middle_of(xm, part, other, vec))
    h2_all[...] = (normed * vec[3:4, :] + vec[4:5, :]).astype(jnp.bfloat16)
    h2 = h2_all[...]
    for at in range(hidden // width):
        cols = pl.ds(at * width, width)
        z = dot_nn(h2, wi[:, cols]) + vec[7 + at : 8 + at, :]
        act, slope = gelu_parts(z)
        u_all[:, cols] = act.astype(jnp.bfloat16)
        dz = (dot_nt(g[...], wf[cols, :]) * slope).astype(jnp.bfloat16)
        dz_all[:, cols] = dz
        few[1 + at : 2 + at, :] = jnp.sum(dz.astype(jnp.float32), axis=0, keepdims=True)
    few[0:1, :] = jnp.sum(g[...].astype(jnp.float32), axis=0, keepdims=True)
    half = hidden // 2
    count = width // 2
    for order, keep, send in ((0, wf_a, wf_as), (1, wf_b, wf_bs)):
        for out, bit in ((keep, bits[order]), (send, 1 - bits[order])):
            at = pl.multiple_of(order * half + bit * count, LANES)
            out[0] = dot_tn(u_all[:, pl.ds(at, count)], g[...]).astype(jnp.bfloat16)
    for order, keep, send in ((0, wi_a, wi_as), (1, wi_b, wi_bs)):
        for out, bit in ((keep, bits[order]), (send, 1 - bits[order])):
            at = pl.multiple_of(bit * count, LANES)
            out[0] = dot_tn(
                h2_all[:, pl.ds(at, count)], dz_all[:, pl.ds(order * half, half)]
            ).astype(jnp.bfloat16)
    dh2[...] = dot_nt(dz_all[...], wi[...]).astype(jnp.bfloat16)


def attend_back_kernel(
    bits, xm, part, other, g, dh2, dh2_other, vec, wo, pos, allow, qm, om, hm, lse, h, k, v,
    da_a, da_as, da_b, da_bs, dx1, dq, dk, dv, few, da_all, do_all,
):
    width = g.shape[1]
    normed, scaled = norm_parts(middle_of(xm, part, other, vec))
    up = dh2[...].astype(jnp.float32) + dh2_other[...].astype(jnp.float32)
    few[0:1, :] = jnp.sum(up * normed, axis=0, keepdims=True)
    few[1:2, :] = jnp.sum(up, axis=0, keepdims=True)
    weighted = up * vec[3:4, :]
    centered = weighted - jnp.mean(weighted, axis=-1, keepdims=True)
    slope = jnp.mean(weighted * normed, axis=-1, keepdims=True)
    grad = g[...].astype(jnp.float32) + scaled * (centered - normed * slope)
    dx1[...] = grad
    low = grad.astype(jnp.bfloat16)
    da_all[...] = low
    few[2:3, :] = jnp.sum(low.astype(jnp.float32), axis=0, keepdims=True)
    do_all[...] = dot_nt(low, wo[...]).astype(jnp.bfloat16)
    listed = row_lists(pos[...] >> 6, allow[...]) > 0.5
    lane = lax.broadcasted_iota(jnp.int32, (1, LANES), 1)

    def one_slab(slab, carry):
        cols = pl.ds(pl.multiple_of(slab * LANES, LANES), LANES)
        query = (qm[:, cols].astype(jnp.float32) * HD ** (-0.5)).astype(jnp.bfloat16)
        grad_q, grad_k, grad_v = None, None, None
        for half in range(2):
            own = one_head(query, half)
            own_do = one_head(do_all[:, cols], half)
            scores = jnp.where(listed, dot_nt(own, k[:, cols]), NEG)
            total = jnp.where(lane == 2 * slab + half, lse[...], 0.0)
            prob = jnp.exp(scores - jnp.sum(total, axis=-1, keepdims=True))
            grad_p = dot_nt(own_do, v[:, cols])
            delta = jnp.sum(prob * grad_p, axis=-1, keepdims=True)
            ds = (prob * (grad_p - delta)).astype(jnp.bfloat16)
            found_q = dot_nn(ds, k[:, cols])
            found_k = dot_tn(ds, own)
            found_v = dot_tn(prob.astype(jnp.bfloat16), own_do)
            grad_q = found_q if half == 0 else jnp.where(head_half(0), grad_q, found_q)
            grad_k = found_k if half == 0 else grad_k + found_k
            grad_v = found_v if half == 0 else grad_v + found_v
        dq[:, cols] = (grad_q * HD ** (-0.5)).astype(jnp.bfloat16)
        dk[:, cols] = grad_k.astype(jnp.bfloat16)
        dv[:, cols] = grad_v.astype(jnp.bfloat16)
        return carry

    lax.fori_loop(0, qm.shape[1] // LANES, one_slab, 0)
    local = qm.shape[1]
    few[3:4, :local] = jnp.sum(dq[...].astype(jnp.float32), axis=0, keepdims=True)
    few[3:4, local:] = jnp.sum(dv[...].astype(jnp.float32), axis=0, keepdims=True)
    count = width // 2
    for keep, bit in ((da_a, bits[0]), (da_as, 1 - bits[0])):
        cols = pl.ds(pl.multiple_of(bit * count, LANES), count)
        keep[0, :, :local] = dot_tn(hm[:, cols], dq[...]).astype(jnp.bfloat16)
        keep[0, :, local:] = dot_tn(h[:, cols], dk[...]).astype(jnp.bfloat16)
    for keep, bit in ((da_b, bits[1]), (da_bs, 1 - bits[1])):
        cols = pl.ds(pl.multiple_of(bit * count, LANES), count)
        keep[0, :, :local] = dot_tn(h[:, cols], dv[...]).astype(jnp.bfloat16)
        keep[0, :, local:] = dot_tn(om[...], da_all[:, cols]).astype(jnp.bfloat16)


def input_kernel(bits, pos, dq, dk, dv, wq, wk, wv, keep, *rest):
    sends, dq_all = rest[:-1], rest[-1]
    total = dk.shape[0]
    dq_all[...] = dot_tn(pick_rows(pos[...], total), dq[...]).astype(jnp.bfloat16)
    run = BS * 2

    def one_piece(at, carry):
        here = pl.ds(pl.multiple_of(at * run, run), run)
        for out, bit in ((keep, bits[2]), (sends[0], 1 - bits[2])):
            rows = pl.ds(pl.multiple_of(at * 2 * run + bit * run, run), run)
            out[here, :] = (
                dot_nt(dq_all[rows, :], wq[...])
                + dot_nt(dk[rows, :], wk[...])
                + dot_nt(dv[rows, :], wv[...])
            ).astype(jnp.bfloat16)
        return carry

    lax.fori_loop(0, total // (2 * run), one_piece, 0)


def first_norm_kernel(count, bits, pos_half, own, dx1, vec, *rest):
    toks, others, grads = rest[:count], rest[count : -3 - count], rest[-3 - count : -3]
    few, tok, other = rest[-3:]
    run = others[0].shape[0]
    for at, piece in enumerate(others):
        other[pl.ds(at * run, run), :] = piece[...]
    run = toks[0].shape[0]
    for at, piece in enumerate(toks):
        tok[pl.ds(at * run, run), :] = piece[...]
    normed, scaled = norm_parts(tok[...].astype(jnp.float32))
    up = own[...].astype(jnp.float32) + other[...].astype(jnp.float32)
    few[0:1, :] = jnp.sum(up * normed, axis=0, keepdims=True)
    few[1:2, :] = jnp.sum(up, axis=0, keepdims=True)
    weighted = up * vec[0:1, :]
    centered = weighted - jnp.mean(weighted, axis=-1, keepdims=True)
    slope = jnp.mean(weighted * normed, axis=-1, keepdims=True)
    pick = pick_rows(pos_half[...], tok.shape[0])
    high = dx1[...].astype(jnp.bfloat16)
    rest = (dx1[...] - high.astype(jnp.float32)).astype(jnp.bfloat16)
    through = dot_tn(pick, high) + dot_tn(pick, rest)
    grad = (through + scaled * (centered - normed * slope)).astype(jnp.bfloat16)
    for at, piece in enumerate(grads):
        piece[0] = grad[at * run : (at + 1) * run, :]


def attend_kernel(at, bits, q, k, v, allow, keep, send, mixed_all):
    tile = mixed_all.shape[0]
    run = tile // 2
    rows = pl.ds(at * tile, tile)
    ids = lax.broadcasted_iota(jnp.int32, (tile, 1), 0)
    bias = (row_lists(at * (tile // BS) + (ids >> 6), allow[...]) - 1.0) * -NEG

    def one_slab(slab, carry):
        cols = pl.ds(pl.multiple_of(slab * LANES, LANES), LANES)
        query = (q[rows, cols].astype(jnp.float32) * HD ** (-0.5)).astype(jnp.bfloat16)
        mixed = None
        for half in range(2):
            scores = dot_nt(one_head(query, half), k[:, cols]) + bias
            weight = jnp.exp(scores - jnp.max(scores, axis=-1, keepdims=True))
            total_weight = jnp.sum(weight, axis=-1, keepdims=True)
            found = dot_nn(weight.astype(jnp.bfloat16), v[:, cols]) * (1.0 / total_weight)
            mixed = found if half == 0 else jnp.where(head_half(0), mixed, found)
        mixed_all[:, cols] = mixed.astype(jnp.bfloat16)
        return carry

    lax.fori_loop(0, q.shape[1] // LANES, one_slab, 0)
    for out, bit in ((keep, bits[2]), (send, 1 - bits[2])):
        out[...] = mixed_all[pl.ds(pl.multiple_of(bit * run, run), run), :]


def lay_kernel(bits, *refs):
    run = refs[0].shape[0]
    for at, piece in enumerate(refs[:-1]):
        refs[-1][pl.ds(at * run, run), :] = piece[...]


def feed_kernel(base, count, bits, *refs):
    toks, refs = refs[:count], refs[count:]
    own, refs = refs[:count], refs[count:]
    other, vec, bi_other, wo, wo_other, wi, wi_other, wf, wf_other = refs[:9]
    pairs, outs, mid_all = refs[9 : 9 + count], refs[-1 - count : -1], refs[-1]
    width, hidden = wi.shape
    run = toks[0].shape[0]
    for at in range(count):
        theirs = other[pl.ds((base + at) * run, run), :]
        mixed = dot_nn(own[at][...], wo[...]) + dot_nn(theirs, wo_other[...])
        mid_all[pl.ds(at * run, run), :] = toks[at][...].astype(jnp.float32) + (
            mixed + vec[2:3, :]
        )
    middle = mid_all[...]
    normed, _ = norm_parts(middle)
    h2 = (normed * vec[3:4, :] + vec[4:5, :]).astype(jnp.bfloat16)
    total = middle + vec[5:6, :]
    mid_all[...] = total
    for row, bias, inner, outer in ((7, vec, wi, wf), (0, bi_other, wi_other, wf_other)):

        def one_chunk(at, carry, row=row, bias=bias, inner=inner, outer=outer):
            cols = pl.ds(pl.multiple_of(at * width, LANES), width)
            z = dot_nn(h2, inner[:, cols]) + bias[pl.ds(row + at, 1), :]
            act = z * (0.5 * (1.0 + lax.erf(z * inv_root_two)))
            mid_all[...] += dot_nn(act.astype(jnp.bfloat16), outer[cols, :])
            return carry

        lax.fori_loop(0, hidden // width, one_chunk, 0)
    low = mid_all[...].astype(jnp.bfloat16)
    for at in range(count):
        outs[at][0] = pairs[at][0]
        outs[at][1] = low[at * run : (at + 1) * run, :]


def gather_small_kernel(bits, first, first_other, attend, hidden, out):
    out[0:2, :] = first[...] + first_other[...]
    out[2:6, :] = attend[...]
    out[6:, :] = hidden[...]


def add_small_kernel(bits, own, other, out):
    out[...] = own[...] + other[...]


def interleave_kernel(bits, *refs):
    count = (len(refs) - 2) // 2
    own, over, outs = refs[:count], refs[count : 2 * count], refs[2 * count :]
    run = own[0].shape[1]
    for at in range(count):
        window = bits[5] ^ at
        for which, out in enumerate(outs):
            for pieces, side in ((own, bits[2]), (over, 1 - bits[2])):
                rows = pl.ds(pl.multiple_of(side * run, run), run)
                out[window, rows, :] = pieces[at][which]


def add_low(left, right):
    return (left.astype(jnp.float32) + right.astype(jnp.float32)).astype(jnp.bfloat16)


def part_rows(bit, count):
    return pl.ds(pl.multiple_of(bit * count, 16), count)


def halve_plane_kernel(at, bits, ka, ra, kb, rb, keep_a, send_a, keep_b, send_b):
    count = keep_a.shape[1]
    groups = ((ka, ra, keep_a, send_a, bits[at[0]]), (kb, rb, keep_b, send_b, bits[at[1]]))
    for k, r, keep, send, bit in groups:
        for out, side in ((keep, bit), (send, 1 - bit)):
            rows = part_rows(side, count)
            out[...] = add_low(k[:, rows, :], r[:, rows, :])


def halve_join_kernel(at, bits, ka, ra, kb, rb, keep, send):
    group, count = ka.shape[0], keep.shape[1]
    for out, side in ((keep, bits[at]), (send, 1 - bits[at])):
        rows = part_rows(side, count)
        out[:group] = add_low(ka[:, rows, :], ra[:, rows, :])
        out[group:] = add_low(kb[:, rows, :], rb[:, rows, :])


def halve_line_kernel(at, bits, k, r, keep, send):
    count = keep.shape[1]
    for out, side in ((keep, bits[at]), (send, 1 - bits[at])):
        rows = part_rows(side, count)
        out[...] = add_low(k[:, rows, :], r[:, rows, :])


def last_line_kernel(bits, k, r, out):
    out[...] = add_low(k[...], r[...])


def double_line_kernel(at, bits, own, other, out):
    count = own.shape[1]
    out[:, part_rows(bits[at], count), :] = own[...]
    out[:, part_rows(1 - bits[at], count), :] = other[...]


def double_split_kernel(at, bits, own, other, out_a, out_b):
    count = own.shape[1]
    group = out_a.shape[0]
    for which, out in ((0, out_a), (1, out_b)):
        part = pl.ds(which * group, group)
        out[:, part_rows(bits[at], count), :] = own[part]
        out[:, part_rows(1 - bits[at], count), :] = other[part]


def double_plane_kernel(at, bits, own_a, other_a, own_b, other_b, out_a, out_b):
    groups = ((own_a, other_a, out_a, bits[at[0]]), (own_b, other_b, out_b, bits[at[1]]))
    for own, other, out, bit in groups:
        count = own.shape[1]
        out[:, part_rows(bit, count), :] = own[...]
        out[:, part_rows(1 - bit, count), :] = other[...]


def last_rows_kernel(at, bits, own_a, other_a, own_b, other_b, out):
    count = own_a.shape[1]
    groups = ((own_a, other_a, bits[at[0]]), (own_b, other_b, bits[at[1]]))
    for which, (own, other, bit) in enumerate(groups):
        for value, side in ((own, bit), (other, 1 - bit)):
            out[part_rows(2 * which + side, count), :] = value[0].astype(jnp.float32)


def last_columns_kernel(at, bits, own_a, other_a, own_b, other_b, out):
    count, width = own_a.shape[1:]
    groups = ((own_a, other_a, bits[at[0]]), (own_b, other_b, bits[at[1]]))
    for which, (own, other, bit) in enumerate(groups):
        for value, side in ((own, bit), (other, 1 - bit)):
            out[part_rows(side, count), pl.ds(which * width, width)] = value[0].astype(
                jnp.float32
            )


def last_attend_kernel(
    at, bits, own_a, other_a, own_b, other_b, grad_q, grad_k, grad_v, grad_o
):
    count = own_a.shape[1]
    local = grad_q.shape[1]
    for value, side in ((own_a, bits[at[0]]), (other_a, 1 - bits[at[0]])):
        grad_q[part_rows(side, count), :] = value[0, :, :local].astype(jnp.float32)
        grad_k[part_rows(side, count), :] = value[0, :, local:].astype(jnp.float32)
    for value, side in ((own_b, bits[at[1]]), (other_b, 1 - bits[at[1]])):
        grad_v[part_rows(side, count), :] = value[0, :, :local].astype(jnp.float32)
        cols = pl.ds(pl.multiple_of(side * count, LANES), count)
        grad_o[:, cols] = value[0, :, local:].astype(jnp.float32)


def joined_size(piece):
    group, rows, width = piece.shape
    return shape((group, 2 * rows, width))


def halved_size(piece):
    group, rows, width = piece.shape
    return shape((group, rows // 2, width))


def flip(value, axis, bit):
    return lax.ppermute(value, axis, [(i, i ^ bit) for i in range(lax.axis_size(axis))])


def bit_of(axis, bit):
    return jnp.where((lax.axis_index(axis) & bit) != 0, 1, 0).astype(jnp.int32)


def stages_of(order):
    dp_bits = [("dp", 1 << i) for i in range(lax.axis_size("dp").bit_length() - 1)]
    seq_bits = [("seq", 1 << i) for i in range(lax.axis_size("seq").bit_length() - 1)]
    return (dp_bits if order == 0 else dp_bits[::-1]) + seq_bits


class Summing:
    def __init__(self, order, bits, keep, send):
        self.order, self.bits = order, bits
        self.keep, self.send = list(keep), list(send)
        self.plane = [stages_of(which)[:2] for which in range(2)]
        self.line = stages_of(0)[2:]

    def hold(self, *others):
        self.send = [after(value, *others) for value in self.send]

    def exchange(self, at):
        self.got = [flip(s, *self.plane[which][at]) for which, s in enumerate(self.send)]
        return self.got

    def exchange_line(self, at):
        return flip(self.send, *self.line[at])

    def halve_first(self):
        other = self.got
        ka, sa, kb, sb = self.order.call(
            functools.partial(halve_plane_kernel, (1, 0)),
            [halved_size(self.keep[0])] * 4,
            (self.bits, self.keep[0], other[0], self.keep[1], other[1]),
        )
        self.keep, self.send = [ka, kb], [sa, sb]

    def halve_second(self):
        other = self.got
        group, rows, width = self.keep[0].shape
        self.keep, self.send = self.order.call(
            functools.partial(halve_join_kernel, 3),
            [shape((2 * group, rows // 2, width))] * 2,
            (self.bits, self.keep[0], other[0], self.keep[1], other[1]),
        )

    def halve_line(self, at, other):
        two, rows, width = self.keep.shape
        if at + 1 < len(self.line):
            self.keep, self.send = self.order.call(
                functools.partial(halve_line_kernel, 4 + at),
                [shape((two, rows // 2, width))] * 2,
                (self.bits, self.keep, other),
            )
        else:
            (self.send,) = self.order.call(
                last_line_kernel, [shape(self.keep.shape)], (self.bits, self.keep, other)
            )

    def double_line(self, at, other):
        two, rows, width = self.send.shape
        if at > 0:
            (self.send,) = self.order.call(
                functools.partial(double_line_kernel, 3 + at),
                [shape((two, 2 * rows, width))],
                (self.bits, self.send, other),
            )
        else:
            self.send = self.order.call(
                functools.partial(double_split_kernel, 3 + at),
                [shape((two // 2, 2 * rows, width))] * 2,
                (self.bits, self.send, other),
            )

    def double_second(self):
        other = self.got
        self.send = self.order.call(
            functools.partial(double_plane_kernel, (1, 0)),
            [joined_size(self.send[0])] * 2,
            (self.bits, self.send[0], other[0], self.send[1], other[1]),
        )

    def write(self, kernel, outs):
        return self.order.call(
            functools.partial(kernel, (0, 1)),
            [shape(dims, jnp.float32) for dims in outs],
            (self.bits, self.send[0], self.got[0], self.send[1], self.got[1]),
        )


STEPS = (
    "I.0", "W.wf", "f.h1", "i.go", "W.wi", "f.h2", "A.0", "f.l0", "i.h1", "a.go", "W.wo",
    "A.1", "i.h2", "A.2", "i.l0", "A.3", "f.l1", "i.l1", "W.bi", "a.h1", "X.0", "f.d1", "N.0",
    "a.h2", "f.d0", "F.0", "a.l0", "i.d1", "f.e2", "F.1", "i.d0", "a.l1", "S.0", "f.wr",
    "S.1", "a.d1", "i.e2", "a.d0", "S.2", "R.3", "i.wr", "S.3", "R.2", "S.4", "R.1", "Q.0",
    "Q.2", "a.e2", "Q.3", "Q.1", "a.wr", "L.all",
)


def window_body(
    tokens, cotangent, masked_pos, rand_blocks, ln1_gain, ln1_bias, w_query, b_query, w_key,
    w_value, b_value, w_out, b_out, ln2_gain, ln2_bias, w_inner, b_inner, w_outer, b_outer,
):
    windows, rows, width = tokens.shape
    local = w_query.shape[1]
    hidden = w_inner.shape[1]
    total = windows * rows
    blocks = total // BS
    run = rows // 2
    split = width // 2
    place = lax.axis_index("seq")
    core = lax.axis_index("tensor")
    plane, line = stages_of(0)[:2], stages_of(0)[2:]
    bits = jnp.stack(
        [bit_of(*step) for step in plane]
        + [core.astype(jnp.int32)]
        + [bit_of(*step) for step in line]
        + [place.astype(jnp.int32)]
    )

    cut = tokens.reshape(windows, 2, run, width)
    own_rows = []
    for at in range(windows):
        piece = lax.dynamic_slice(cut, (place ^ at, core, 0, 0), (1, 1, run, width))
        piece = piece.reshape(run, width)
        own_rows.append(piece if at == 0 else flip(piece, "seq", at))

    named = masked_pos.shape[1]
    count = -(-named // 16) * 16
    spots = jnp.concatenate(
        [masked_pos, jnp.full((windows, count - named), -1, jnp.int32)], axis=1
    )
    slot = jnp.arange(count, dtype=jnp.int32)
    again = jnp.any(
        (spots[:, :, None] == spots[:, None, :]) & (slot[None, :] < slot[:, None])[None], axis=2
    )
    spots = jnp.where(again, -1, spots)
    spot = lax.dynamic_index_in_dim(spots, place, 0, keepdims=True).reshape(count, 1)
    there, inside = (spot // rows) ^ place, spot % rows
    pos = jnp.where(spot >= 0, there * rows + inside, -1)
    mine = (spot >= 0) & (inside // run == core)
    pos_half = jnp.where(mine, there * run + inside % run, -1)

    here = spots - place * rows
    found = []
    for at in range(windows):
        named_rows = lax.dynamic_index_in_dim(here, place ^ at, 0, keepdims=False)
        pick = (named_rows[:, None] == jnp.arange(rows, dtype=jnp.int32)[None, :]).astype(
            jnp.bfloat16
        )
        shard = lax.dynamic_slice(
            cotangent, (place ^ at, 0, core * split), (1, rows, split)
        ).reshape(rows, split)
        found.append(dot_nn(pick, shard).astype(jnp.bfloat16))

    rand = lax.dynamic_index_in_dim(rand_blocks, place, 0, keepdims=False)
    numbers = jnp.arange(blocks, dtype=jnp.int32)
    shard_blocks = rows // BS
    ids = ((numbers // shard_blocks) ^ place) * shard_blocks + numbers % shard_blocks
    named_blocks = jnp.any(rand[:, :, None] == ids[None, None, :], axis=1)
    named_blocks = jnp.any(
        (ids[:, None] == numbers[None, :])[:, :, None] & named_blocks[None], axis=1
    )
    listed = (
        (jnp.abs(ids[:, None] - ids[None, :]) <= 1)
        | (ids == 0)[None, :]
        | (ids == blocks - 1)[None, :]
        | named_blocks
    )
    allow = jnp.repeat(listed.astype(jnp.bfloat16), BS, axis=1)

    rows_wide = [ln1_gain, ln1_bias, b_out, ln2_gain, ln2_bias, b_outer, b_query, b_value, b_inner]
    vec = jnp.concatenate([x.astype(jnp.float32) for x in rows_wide]).reshape(-1, width)

    order = Order()
    state = None
    for at in range(windows):
        if at == 1:
            order.need(pos, pos_half, allow, *own_rows[1:], *found)
        kept = () if state is None else tuple(state)
        over = own_rows[at] if at == 0 else after(own_rows[at], entry)
        state = order.call(
            functools.partial(shard_kernel, at),
            [shape((total, width))] * 2 + [shape((total, local))] * 3,
            (bits, own_rows[at], flip(over, "tensor", 1), vec, w_query, w_key, w_value) + kept,
            aliases={7 + i: i for i in range(len(kept))},
        )
        if at == 0:
            entry = order.last
    tok, h, q, k, v = state
    found = [found[0]] + [
        flip(after(found[i], *own_rows[1:]), "seq", i) for i in range(1, windows)
    ]
    xm, hm, qm, om, lse, part = order.call(
        front_kernel,
        [shape((count, width))] * 2
        + [shape((count, local))] * 2
        + [shape((count, LANES), jnp.float32), shape((count, width))],
        (bits, pos, allow, w_out, tok, h, q, k, v),
    )
    other = flip(part, "tensor", 1)
    (g_own,) = order.call(sum_rows_kernel, [shape((count, split))], (bits, *found))
    g_other = flip(g_own, "tensor", 1)
    outs = order.call(
        hidden_kernel,
        [shape((1, width // 2, width))] * 8
        + [shape((count, width)), shape((1 + hidden // width, width), jnp.float32)]
        + [shape((count, width))],
        (bits, xm, part, other, g_own, g_other, vec, w_inner, w_outer),
        scratch=[
            pltpu.VMEM((count, hidden), jnp.bfloat16),
            pltpu.VMEM((count, width), jnp.bfloat16),
            pltpu.VMEM((count, hidden), jnp.bfloat16),
        ],
    )
    wf_a, wf_as, wf_b, wf_bs, wi_a, wi_as, wi_b, wi_bs, dh2, few_hidden, g = outs
    sum_f = Summing(order, bits, (wf_a, wf_b), (wf_as, wf_bs))
    sum_i = Summing(order, bits, (wi_a, wi_b), (wi_as, wi_bs))

    held = {}
    sum_f.exchange(0)
    dh2_other = flip(dh2, "tensor", 1)
    outs = order.call(
        attend_back_kernel,
        [shape((1, width // 2, 2 * local))] * 2
        + [shape((1, width // 2, local + width // 2))] * 2
        + [shape((count, width), jnp.float32), shape((count, local))]
        + [shape((total, local))] * 2
        + [shape((4, width), jnp.float32)],
        (bits, xm, part, other, g, dh2, dh2_other, vec, w_out, pos, allow)
        + (qm, om, hm, lse, h, k, v),
        scratch=[
            pltpu.VMEM((count, width), jnp.bfloat16),
            pltpu.VMEM((count, local), jnp.bfloat16),
        ],
    )
    da_a, da_as, da_b, da_bs, dx1, dq, dk, dv, few_attend = outs
    sum_a = Summing(order, bits, (da_a, da_b), (da_as, da_bs))

    def attend(at):
        keep, send = order.call(
            functools.partial(attend_kernel, at),
            [shape((run, local))] * 2,
            (bits, q, k, v, allow),
            scratch=[pltpu.VMEM((rows, local), jnp.bfloat16)],
        )
        held.setdefault("keep", []).append(keep)
        held.setdefault("send", []).append(send)

    def feed(base, pieces):
        span = slice(base, base + pieces)
        held["pair"][span] = order.call(
            functools.partial(feed_kernel, base, pieces),
            [shape((2, run, width))] * pieces,
            (bits, *own_rows[span], *held["keep"][span], held["mixed_other"], vec)
            + (held["bi"], w_out, held["wo"], w_inner, held["wi"], w_outer, held["wf"])
            + tuple(held["pair"][span]),
            scratch=[pltpu.VMEM((pieces * run, width), jnp.float32)],
            aliases={10 + 2 * pieces + i: i for i in range(pieces)},
        )

    small_steps = iter(stages_of(0)[::-1])
    sums = {"f": sum_f, "i": sum_i, "a": sum_a}

    def swap(value, kernels=2):
        other = flip(after(value, order.last), "tensor", 1)
        order.soon(other, kernels)
        return other

    def sum_step(of, step):
        one = sums[of]
        if step == "go":
            one.hold(order.last)
            one.exchange(0)
        elif step == "h1":
            one.halve_first()
            one.exchange(1)
        elif step == "h2":
            one.halve_second()
            held[of] = one.exchange_line(0)
        elif step == "l0":
            one.halve_line(0, held[of])
            held[of] = one.exchange_line(1)
        elif step == "l1":
            one.halve_line(1, held[of])
            held[of] = one.exchange_line(1)
        elif step == "d1":
            one.double_line(1, held[of])
            held[of] = one.exchange_line(0)
        elif step == "d0":
            one.double_line(0, held[of])
            one.exchange(1)
        elif step == "e2":
            one.double_second()
            one.exchange(0)
        elif of == "f":
            (held["grad_wf"],) = one.write(last_rows_kernel, [(hidden, width)])
        elif of == "i":
            (held["grad_wi"],) = one.write(last_columns_kernel, [(width, hidden)])
        else:
            held["grad_a"] = one.write(last_attend_kernel, [(width, local)] * 3 + [(local, width)])

    def input_grad():
        held["dh_own"], dh_send = order.call(
            input_kernel,
            [shape((total // 2, width))] * 2,
            (bits, pos, dq, dk, dv, w_query, w_key, w_value),
            scratch=[pltpu.VMEM((total, local), jnp.bfloat16)],
        )
        held["dh_other"] = flip(dh_send, "tensor", 1)

    def first_norm():
        *held["pair"], held["few"] = order.call(
            functools.partial(first_norm_kernel, windows),
            [shape((2, run, width))] * windows + [shape((2, width), jnp.float32)],
            (bits, pos_half, held["dh_own"], dx1, vec, *own_rows, held["dh_other"]),
            scratch=[pltpu.VMEM((total // 2, width), jnp.bfloat16)] * 2,
        )
        held["few_other"] = flip(held["few"], "tensor", 1)
        order.soon(held["few_other"])

    def small(step):
        if step == "0":
            (held["small"],) = order.call(
                gather_small_kernel,
                [shape((7 + hidden // width, width), jnp.float32)],
                (bits, held["few"], held["few_other"], few_attend, few_hidden),
            )
        else:
            (held["small"],) = order.call(
                add_small_kernel,
                [shape(held["small"].shape, jnp.float32)],
                (bits, held["small"], held["small_other"]),
            )
        if step != "4":
            held["small_other"] = flip(held["small"], *next(small_steps))

    def send_back(at):
        held["pair"][at] = flip(after(held["pair"][at], order.last), "seq", at)
        order.soon(held["pair"][at], 3)

    def swap_back(at):
        held.setdefault("over", {})[at] = swap(held["pair"][at])

    def interleave():
        over = [held["over"][at] for at in range(windows)]
        held["all"] = order.call(
            interleave_kernel,
            [shape((windows, rows, width))] * 2,
            (bits, *held["pair"], *over),
        )

    for step in STEPS:
        kind, what = step[0], step[2:]
        if kind in sums:
            sum_step(kind, what)
        elif kind == "A":
            attend(int(what))
        elif kind == "F":
            feed(int(what) * windows // 2, windows // 2)
        elif kind == "W":
            held[what] = swap({"wi": w_inner, "wf": w_outer, "wo": w_out, "bi": vec[7:]}[what])
        elif kind == "X":
            laid = order.call(lay_kernel, [shape((windows * run, local))], (bits, *held["send"]))
            held["mixed_other"] = swap(laid[0])
        elif kind == "S":
            small(what)
        elif kind == "R":
            send_back(int(what))
        elif kind == "Q":
            swap_back(int(what))
        elif kind == "L":
            interleave()
        elif kind == "I":
            input_grad()
        else:
            first_norm()
    grad_tokens, out = held["all"]
    grad_q, grad_k, grad_v, grad_o = held["grad_a"]
    grad_wf, grad_wi, small_all = held["grad_wf"], held["grad_wi"], held["small"]
    return (
        out,
        grad_tokens,
        small_all[0],
        small_all[1],
        grad_q,
        small_all[5, :local],
        grad_k,
        grad_v,
        small_all[5, local:],
        grad_o,
        small_all[4],
        small_all[2],
        small_all[3],
        grad_wi,
        small_all[7:].reshape(-1),
        grad_wf,
        small_all[6],
    )


def with_halo(block, sides, width):
    for axis, dim in sides:
        count = lax.axis_size(axis)
        forward = [(i, i + 1) for i in range(count - 1)]
        backward = [(target, source) for source, target in forward]
        low = lax.ppermute(
            lax.slice_in_dim(block, block.shape[dim] - width, None, axis=dim), axis, forward
        )
        high = lax.ppermute(lax.slice_in_dim(block, 0, width, axis=dim), axis, backward)
        block = jnp.concatenate([low, block, high], axis=dim)
    return block


def broadcast(value, axis, root):
    mine = lax.axis_index(axis) == root
    return lax.psum(jnp.where(mine, value, jnp.zeros_like(value)), axis)


def norm_forward(values, gain, shift):
    center = values - jnp.mean(values, axis=-1, keepdims=True)
    scaled = lax.rsqrt(jnp.mean(center * center, axis=-1, keepdims=True) + eps_norm)
    normed = center * scaled
    return (normed * gain + shift, normed, scaled)


def norm_backward(upstream, gain, normed, scaled):
    weighted = upstream * gain
    centered = weighted - jnp.mean(weighted, axis=-1, keepdims=True)
    return scaled * (centered - normed * jnp.mean(weighted * normed, axis=-1, keepdims=True))


def row_dot(left, right):
    return lax.dot_general(
        left, right, (((left.ndim - 1,), (0,)), ((), ())), preferred_element_type=jnp.float32
    )


def back_dot(left, right):
    return lax.dot_general(
        left, right, (((left.ndim - 1,), (1,)), ((), ())), preferred_element_type=jnp.float32
    )


def outer_sum(left, right):
    return lax.dot_general(
        left, right, (((0, 1), (0, 1)), ((), ())), preferred_element_type=jnp.float32
    )


def column_sum(values):
    return jnp.sum(values, axis=(0, 1), dtype=jnp.float32)


def list_masks(rand_local, first_block, block_count):
    window_count, local_count = (rand_local.shape[0], rand_local.shape[1])
    query_ids = first_block + jnp.arange(local_count, dtype=jnp.int32)
    slide_ok = jnp.stack(
        [query_ids - 1 >= 0, query_ids >= 0, query_ids + 1 <= block_count - 1], axis=1
    )
    end_ok = jnp.stack([jnp.abs(query_ids) > 1, jnp.abs(block_count - 1 - query_ids) > 1], axis=1)
    rand_ok = (
        (jnp.abs(rand_local - query_ids[None, :, None]) > 1)
        & (rand_local != 0)
        & (rand_local != block_count - 1)
    )
    fixed_ok = jnp.broadcast_to(
        jnp.concatenate([slide_ok, end_ok], axis=1)[None], (window_count, local_count, 5)
    )
    return jnp.concatenate([fixed_ok, rand_ok], axis=-1)


def build_routing(rand_batch, position, devices, local_count, capacity):
    window_count = rand_batch.shape[0]
    item_count = window_count * local_count * 3

    def arrange(grid_values):
        grid_values = grid_values.reshape(window_count, devices, local_count, 3)
        return jnp.transpose(grid_values, (1, 0, 2, 3)).reshape(devices, item_count)

    window_grid = jnp.broadcast_to(
        jnp.arange(window_count, dtype=jnp.int32)[:, None, None], rand_batch.shape
    )
    owner_table = arrange(rand_batch // local_count)
    source_table = arrange(window_grid * local_count + rand_batch % local_count)
    device_ids = jnp.arange(devices, dtype=jnp.int32)
    matches = (owner_table[:, :, None] == device_ids[None, None, :]).astype(jnp.int32)
    earlier = jnp.cumsum(matches, axis=1) - matches
    slot_table = jnp.sum(earlier * matches, axis=2)
    owned_here = (owner_table == position).astype(jnp.int32)
    slot_ids = jnp.arange(capacity, dtype=jnp.int32)
    slot_matches = (slot_table[:, :, None] == slot_ids[None, None, :]).astype(
        jnp.int32
    ) * owned_here[:, :, None]
    send_rows = jnp.sum(slot_matches * source_table[:, :, None], axis=1).reshape(devices * capacity)
    send_live = jnp.sum(slot_matches, axis=1).reshape(devices * capacity)
    my_owner = lax.dynamic_index_in_dim(owner_table, position, 0, keepdims=False)
    my_slot = lax.dynamic_index_in_dim(slot_table, position, 0, keepdims=False)
    take_rows = my_owner * capacity + my_slot
    return (send_rows, send_live, take_rows)


def fetch_blocks(packed, routing, block_rows):
    window_count, local_rows, kv_width = packed.shape
    local_count = local_rows // block_rows
    devices = lax.axis_size("seq")
    padded = with_halo(packed, (("seq", 1),), block_rows)
    padded = padded.reshape(window_count, local_count + 2, block_rows, kv_width)
    sliding = jnp.stack([padded[:, offset : offset + local_count] for offset in range(3)], axis=2)
    first_part = broadcast(packed[:, :block_rows], "seq", 0)
    last_part = broadcast(packed[:, local_rows - block_rows :], "seq", devices - 1)
    end_blocks = jnp.stack([first_part, last_part], axis=1)
    end_blocks = jnp.broadcast_to(
        end_blocks[:, None], (window_count, local_count, 2, block_rows, kv_width)
    )
    send_rows, send_live, take_rows = routing
    sources = packed.reshape(window_count * local_count, block_rows, kv_width)
    outgoing = jnp.take(sources, send_rows, axis=0).reshape(devices, -1, block_rows, kv_width)
    incoming = lax.all_to_all(outgoing, "seq", split_axis=0, concat_axis=0, tiled=True).reshape(
        -1, block_rows, kv_width
    )
    fetched = jnp.take(incoming, take_rows, axis=0).reshape(
        window_count, local_count, 3, block_rows, kv_width
    )
    return jnp.concatenate([sliding, end_blocks, fetched], axis=2)


def return_blocks(kv_grads, routing, block_rows):
    window_count, local_count = (kv_grads.shape[0], kv_grads.shape[1])
    kv_width = kv_grads.shape[-1]
    local_rows = local_count * block_rows
    devices = lax.axis_size("seq")
    position = lax.axis_index("seq")
    padded_grad = jnp.zeros((window_count, local_count + 2, block_rows, kv_width), jnp.float32)
    for offset in range(3):
        padded_grad = padded_grad.at[:, offset : offset + local_count].add(kv_grads[:, :, offset])
    rim_rows = jnp.concatenate([padded_grad[:, 0], padded_grad[:, local_count + 1]], axis=1)
    rim_back = with_halo(rim_rows.astype(jnp.bfloat16), (("seq", 1),), block_rows).astype(
        rim_rows.dtype
    )
    end_grads = lax.psum(jnp.sum(kv_grads[:, :, 3:5], axis=1).astype(jnp.bfloat16), "seq").astype(
        jnp.float32
    )
    zeros_block = jnp.zeros((window_count, block_rows, kv_width), jnp.float32)
    first_add = rim_back[:, :block_rows] + jnp.where(position == 0, end_grads[:, 0], zeros_block)
    last_add = rim_back[:, 3 * block_rows :] + jnp.where(
        position == devices - 1, end_grads[:, 1], zeros_block
    )
    send_rows, send_live, take_rows = routing
    rand_items = kv_grads[:, :, 5:8].reshape(-1, block_rows, kv_width)
    capacity_rows = send_rows.shape[0]
    outgoing = (
        jnp.zeros((capacity_rows, block_rows, kv_width), jnp.float32).at[take_rows].set(rand_items)
    )
    incoming = lax.all_to_all(
        outgoing.reshape(devices, -1, block_rows, kv_width).astype(jnp.bfloat16),
        "seq",
        split_axis=0,
        concat_axis=0,
        tiled=True,
    ).astype(jnp.float32)
    incoming = (
        incoming.reshape(capacity_rows, block_rows, kv_width)
        * send_live.astype(jnp.float32)[:, None, None]
    )
    from_owners = (
        jnp.zeros((window_count * local_count, block_rows, kv_width), jnp.float32)
        .at[send_rows]
        .add(incoming)
    )
    summed = padded_grad[:, 1 : local_count + 1].reshape(window_count, local_rows, kv_width)
    summed = summed + from_owners.reshape(window_count, local_rows, kv_width)
    summed = summed.at[:, :block_rows].add(first_add)
    summed = summed.at[:, local_rows - block_rows :].add(last_add)
    return summed


def split_scores(query_low, keyset, key_valid):
    window_count, local_rows, local_width = query_low.shape
    local_count = keyset.shape[1]
    head_count = local_width // HD
    key_rows = keyset.shape[2] * BS
    query_split = query_low.reshape(window_count, local_count, BS, head_count, HD)
    paired = keyset.reshape(window_count, local_count, key_rows, 2, head_count, HD)
    key_part = paired[:, :, :, 0]
    value_part = paired[:, :, :, 1]
    scores = jnp.einsum(
        "wbqhd,wbkhd->wbhqk", query_split, key_part, preferred_element_type=jnp.float32
    ) * HD ** (-0.5)
    allowed = jnp.repeat(key_valid, BS, axis=2)[:, :, None, None, :]
    scores = jnp.where(allowed, scores, -1e30)
    return (scores, query_split, key_part, value_part)


def attend_forward(query_low, keyset, key_valid):
    scores, query_split, key_part, value_part = split_scores(query_low, keyset, key_valid)
    top_score = jnp.max(scores, axis=-1, keepdims=True)
    log_total = top_score + jnp.log(jnp.sum(jnp.exp(scores - top_score), axis=-1, keepdims=True))
    weights = jnp.exp(scores - log_total).astype(jnp.bfloat16)
    mixed = jnp.einsum(
        "wbhqk,wbkhd->wbqhd", weights, value_part, preferred_element_type=jnp.float32
    )
    return (mixed.reshape(query_low.shape).astype(jnp.bfloat16), log_total)


def attend_backward(query_low, keyset, key_valid, log_total, grad_mixed):
    scores, query_split, key_part, value_part = split_scores(query_low, keyset, key_valid)
    window_count, local_count = (keyset.shape[0], keyset.shape[1])
    local_width = query_low.shape[2]
    weights = jnp.exp(scores - log_total)
    grad_split = grad_mixed.reshape(query_split.shape)
    grad_weights = jnp.einsum(
        "wbqhd,wbkhd->wbhqk", grad_split, value_part, preferred_element_type=jnp.float32
    )
    delta_sum = jnp.sum(weights * grad_weights, axis=-1, keepdims=True)
    grad_scores = (weights * (grad_weights - delta_sum)).astype(jnp.bfloat16)
    grad_query = jnp.einsum(
        "wbhqk,wbkhd->wbqhd", grad_scores, key_part, preferred_element_type=jnp.float32
    ) * HD ** (-0.5)
    grad_key = jnp.einsum(
        "wbhqk,wbqhd->wbkhd", grad_scores, query_split, preferred_element_type=jnp.float32
    ) * HD ** (-0.5)
    grad_value = jnp.einsum(
        "wbhqk,wbqhd->wbkhd",
        weights.astype(jnp.bfloat16),
        grad_split,
        preferred_element_type=jnp.float32,
    )
    list_shape = (window_count, local_count, keyset.shape[2], BS, local_width)
    kv_grads = jnp.concatenate(
        [grad_key.reshape(list_shape), grad_value.reshape(list_shape)], axis=-1
    )
    return (grad_query.reshape(query_low.shape), kv_grads)


def flatten_all(members):
    return jnp.concatenate([member.reshape(-1) for member in members])


def share_sum(vector):
    return lax.psum_scatter(vector, ("dp", "seq"), scatter_dimension=0, tiled=True)


def spread_body(
    tokens,
    cotangent,
    masked_pos,
    rand_blocks,
    ln1_gain,
    ln1_bias,
    w_query,
    b_query,
    w_key,
    w_value,
    b_value,
    w_out,
    b_out,
    ln2_gain,
    ln2_bias,
    w_inner,
    b_inner,
    w_outer,
    b_outer,
):
    local_rows = tokens.shape[1]
    devices = lax.axis_size("seq")
    position = lax.axis_index("seq")
    block_count = rand_blocks.shape[1]
    local_count = block_count // devices
    capacity = (3 * WIN_MB * local_count + devices - 1) // devices
    gain_one = ln1_gain.astype(jnp.float32)
    bias_one = ln1_bias.astype(jnp.float32)
    gain_two = ln2_gain.astype(jnp.float32)
    bias_two = ln2_bias.astype(jnp.float32)
    row_ids = position * local_rows + jnp.arange(local_rows, dtype=jnp.int32)
    first_block = position * local_count
    outputs = []
    input_grads = []
    totals = None
    for batch_index in range(MB):
        batch_start = batch_index * WIN_MB
        batch_stop = batch_start + WIN_MB
        tokens_now = tokens[batch_start:batch_stop].astype(jnp.float32)
        rand_now = rand_blocks[batch_start:batch_stop]
        routing = build_routing(rand_now, position, devices, local_count, capacity)
        rand_local = lax.dynamic_slice_in_dim(rand_now, first_block, local_count, 1)
        key_valid = list_masks(rand_local, first_block, block_count)
        hidden_one, normed_one, scaled_one = norm_forward(tokens_now, gain_one, bias_one)
        hidden_low = hidden_one.astype(jnp.bfloat16)
        query_low = (row_dot(hidden_low, w_query) + b_query.astype(jnp.float32)).astype(
            jnp.bfloat16
        )
        key_low = row_dot(hidden_low, w_key).astype(jnp.bfloat16)
        value_low = (row_dot(hidden_low, w_value) + b_value.astype(jnp.float32)).astype(
            jnp.bfloat16
        )
        packed = jnp.concatenate([key_low, value_low], axis=2)
        keyset = fetch_blocks(packed, routing, BS)
        mixed_low, log_total = attend_forward(query_low, keyset, key_valid)
        attn_out = lax.psum(row_dot(mixed_low, w_out).astype(jnp.bfloat16), "tensor").astype(
            jnp.float32
        ) + b_out.astype(jnp.float32)
        middle = tokens_now + attn_out
        hidden_two, normed_two, scaled_two = norm_forward(middle, gain_two, bias_two)
        hidden_two_low = hidden_two.astype(jnp.bfloat16)
        inner_pre = row_dot(hidden_two_low, w_inner) + b_inner.astype(jnp.float32)
        active = jax.nn.gelu(inner_pre, approximate=False).astype(jnp.bfloat16)
        ffn_out = lax.psum(row_dot(active, w_outer).astype(jnp.bfloat16), "tensor").astype(
            jnp.float32
        ) + b_outer.astype(jnp.float32)
        outputs.append((middle + ffn_out).astype(jnp.bfloat16))
        masked_now = masked_pos[batch_start:batch_stop]
        chosen = jnp.any(row_ids[None, :, None] == masked_now[:, None, :], axis=2)
        cot_now = cotangent[batch_start:batch_stop]
        grad_top = jnp.where(chosen[:, :, None], cot_now, jnp.zeros_like(cot_now))
        grad_active = back_dot(grad_top, w_outer)
        normal_cdf = 0.5 * (1.0 + lax.erf(inner_pre * inv_root_two))
        density = jnp.exp(-0.5 * inner_pre * inner_pre) * inv_root_two_pi
        grad_inner = (grad_active * (normal_cdf + inner_pre * density)).astype(jnp.bfloat16)
        grad_hidden_two = lax.psum(
            back_dot(grad_inner, w_inner).astype(jnp.bfloat16), "tensor"
        ).astype(jnp.float32)
        grad_middle = grad_top.astype(jnp.float32) + norm_backward(
            grad_hidden_two, gain_two, normed_two, scaled_two
        )
        grad_attn = grad_middle.astype(jnp.bfloat16)
        grad_mixed = back_dot(grad_attn, w_out).astype(jnp.bfloat16)
        keyset_back = fetch_blocks(packed, routing, BS)
        grad_query, kv_grads = attend_backward(
            query_low, keyset_back, key_valid, log_total, grad_mixed
        )
        grad_query = grad_query.astype(jnp.bfloat16)
        grad_packed = return_blocks(kv_grads, routing, BS)
        local_width = query_low.shape[2]
        grad_key = grad_packed[:, :, :local_width].astype(jnp.bfloat16)
        grad_value = grad_packed[:, :, local_width:].astype(jnp.bfloat16)
        grad_partial = (
            back_dot(grad_query, w_query)
            + back_dot(grad_key, w_key)
            + back_dot(grad_value, w_value)
        )
        grad_hidden_one = lax.psum(grad_partial.astype(jnp.bfloat16), "tensor").astype(jnp.float32)
        grad_tokens_now = grad_middle + norm_backward(
            grad_hidden_one, gain_one, normed_one, scaled_one
        )
        input_grads.append(grad_tokens_now.astype(jnp.bfloat16))
        batch_grads = (
            jnp.sum(grad_hidden_one * normed_one, axis=(0, 1)),
            jnp.sum(grad_hidden_one, axis=(0, 1)),
            outer_sum(hidden_low, grad_query),
            column_sum(grad_query),
            outer_sum(hidden_low, grad_key),
            outer_sum(hidden_low, grad_value),
            column_sum(grad_value),
            outer_sum(mixed_low, grad_attn),
            column_sum(grad_attn),
            jnp.sum(grad_hidden_two * normed_two, axis=(0, 1)),
            jnp.sum(grad_hidden_two, axis=(0, 1)),
            outer_sum(hidden_two_low, grad_inner),
            column_sum(grad_inner),
            outer_sum(active, grad_top),
            column_sum(grad_top),
        )
        totals = batch_grads if totals is None else jax.tree.map(jnp.add, totals, batch_grads)
    final_share = share_sum(flatten_all(totals))
    gathered = lax.all_gather(
        final_share.astype(jnp.bfloat16), ("dp", "seq"), axis=0, tiled=True
    ).astype(final_share.dtype)
    param_shapes = [
        member.shape
        for member in (
            ln1_gain,
            ln1_bias,
            w_query,
            b_query,
            w_key,
            w_value,
            b_value,
            w_out,
            b_out,
            ln2_gain,
            ln2_bias,
            w_inner,
            b_inner,
            w_outer,
            b_outer,
        )
    ]
    results = []
    cursor = 0
    for shape_now in param_shapes:
        length = 1
        for extent in shape_now:
            length = length * extent
        results.append(gathered[cursor : cursor + length].reshape(shape_now))
        cursor = cursor + length
    out_all = jnp.concatenate(outputs, axis=0)
    grad_all = jnp.concatenate(input_grads, axis=0)
    return (
        out_all,
        grad_all,
        results[0],
        results[1],
        results[2],
        results[3],
        results[4],
        results[5],
        results[6],
        results[7],
        results[8],
        results[9],
        results[10],
        results[11],
        results[12],
        results[13],
        results[14],
    )


def power_of_two(number):
    return number & (number - 1) == 0


def body(tokens, *rest):
    dp, seq, tensor = (lax.axis_size(axis) for axis in ("dp", "seq", "tensor"))
    fits = seq == tokens.shape[0] and tensor == 2 and dp == 4 and power_of_two(seq)
    return (window_body if fits else spread_body)(tokens, *rest)


def solution(mesh):
    in_specs = (
        P("dp", "seq", None),
        P("dp", "seq", None),
        P("dp", None),
        P("dp", None, None),
        P(),
        P(),
        P(None, "tensor"),
        P("tensor"),
        P(None, "tensor"),
        P(None, "tensor"),
        P("tensor"),
        P("tensor", None),
        P(),
        P(),
        P(),
        P(None, "tensor"),
        P("tensor"),
        P("tensor", None),
        P(),
    )
    out_specs = (
        P("dp", "seq", None),
        P("dp", "seq", None),
        P(),
        P(),
        P(None, "tensor"),
        P("tensor"),
        P(None, "tensor"),
        P(None, "tensor"),
        P("tensor"),
        P("tensor", None),
        P(),
        P(),
        P(),
        P(None, "tensor"),
        P("tensor"),
        P("tensor", None),
        P(),
    )
    return jax.shard_map(body, mesh=mesh, in_specs=in_specs, out_specs=out_specs, check_vma=False)
```

```python
import functools

import jax
import jax.numpy as jnp
from jax import lax
from jax.experimental import pallas as pl
from jax.experimental.pallas import tpu as pltpu
from jax.sharding import PartitionSpec as P

HD = 64
BS = 64
MB = 2
WIN_MB = 2


eps_norm = 1e-05
inv_root_two = 0.7071067811865476
inv_root_two_pi = 0.3989422804014327


LANES = 128
NEG = -1e30
VMEM_LIMIT = 16 * 1024 * 1024


def dot_nn(left, right):
    return lax.dot_general(left, right, (((1,), (0,)), ((), ())), preferred_element_type=jnp.float32)


def dot_nt(left, right):
    return lax.dot_general(left, right, (((1,), (1,)), ((), ())), preferred_element_type=jnp.float32)


def dot_tn(left, right):
    return lax.dot_general(left, right, (((0,), (0,)), ((), ())), preferred_element_type=jnp.float32)


def norm_parts(values):
    center = values - jnp.mean(values, axis=-1, keepdims=True)
    scaled = lax.rsqrt(jnp.mean(center * center, axis=-1, keepdims=True) + eps_norm)
    return center * scaled, scaled


def pick_rows(positions, total):
    ids = lax.broadcasted_iota(jnp.int32, (positions.shape[0], total), 1)
    return jnp.where(ids == positions, 1.0, 0.0).astype(jnp.bfloat16)


def row_lists(blocks, allow):
    ids = lax.broadcasted_iota(jnp.int32, (blocks.shape[0], allow.shape[0]), 1)
    return dot_nn(jnp.where(ids == blocks, 1.0, 0.0).astype(jnp.bfloat16), allow)


def head_half(half):
    lane = lax.broadcasted_iota(jnp.int32, (1, LANES), 1)
    return (lane < HD) if half == 0 else (lane >= HD)


def one_head(slab, half):
    return jnp.where(head_half(half), slab, jnp.zeros_like(slab))


class Order:
    def __init__(self):
        self.last = None
        self.needed = []
        self.later = []

    def soon(self, array, kernels=2):
        self.later.append([kernels, array])

    def need(self, *arrays):
        self.needed += arrays

    def call(self, kernel, outs, args, smem=1, scratch=(), aliases=None):
        first = args[0]
        for entry in self.later:
            entry[0] -= 1
        self.needed += [array for left, array in self.later if left == 0]
        self.later = [entry for entry in self.later if entry[0] > 0]
        if self.last is not None:
            first = after(first, self.last, *self.needed)
            self.needed = []
        spec = pl.BlockSpec(memory_space=pltpu.VMEM)
        found = pl.pallas_call(
            kernel,
            name=getattr(kernel, "func", kernel).__name__.removesuffix("_kernel"),
            out_shape=outs,
            in_specs=[pl.BlockSpec(memory_space=pltpu.SMEM)] * smem + [spec] * (len(args) - smem),
            out_specs=[spec] * len(outs),
            scratch_shapes=list(scratch),
            input_output_aliases=aliases or {},
            compiler_params=pltpu.CompilerParams(vmem_limit_bytes=VMEM_LIMIT),
            cost_estimate=pl.CostEstimate(flops=1, bytes_accessed=1, transcendentals=0),
        )(first, *args[1:])
        self.last = min(found, key=lambda a: a.size)
        return found


def after(value, *others):
    return lax.optimization_barrier((value, others))[0]


def shape(dims, dtype=jnp.bfloat16):
    return jax.ShapeDtypeStruct(dims, dtype)


def shard_kernel(at, bits, own, other, vec, wq, wk, wv, *rest):
    tok, h, q, k, v = rest[-5:]
    run = own.shape[0]
    local = wq.shape[1]

    def keep_rows(before, carry):
        rows = pl.ds(pl.multiple_of(before * 2 * run, 2 * run), 2 * run)
        for kept, out in zip(rest[:-5], rest[-5:]):
            out[rows, :] = kept[rows, :]
        return carry

    if at:
        lax.fori_loop(0, at, keep_rows, 0)

    def one_half(half, carry):
        rows = pl.ds(pl.multiple_of((2 * at + half) * run, run), run)
        low_rows = jnp.where(half == bits[2], own[...], other[...])
        tok[rows, :] = low_rows
        normed, _ = norm_parts(low_rows.astype(jnp.float32))
        low = (normed * vec[0:1, :] + vec[1:2, :]).astype(jnp.bfloat16)
        h[rows, :] = low
        q[rows, :] = (dot_nn(low, wq[...]) + vec[6:7, :local]).astype(jnp.bfloat16)
        k[rows, :] = dot_nn(low, wk[...]).astype(jnp.bfloat16)
        v[rows, :] = (dot_nn(low, wv[...]) + vec[6:7, local:]).astype(jnp.bfloat16)
        return carry

    lax.fori_loop(0, 2, one_half, 0)


def sum_rows_kernel(bits, *refs):
    total = None
    for piece in refs[:-1]:
        value = piece[...].astype(jnp.float32)
        total = value if total is None else total + value
    refs[-1][...] = total.astype(jnp.bfloat16)


def front_kernel(bits, pos, allow, wo, tok, h, q, k, v, xm, hm, qm, om, lse, part):
    total, local = q.shape
    pick = pick_rows(pos[...], total)
    xm[...] = dot_nn(pick, tok[...]).astype(jnp.bfloat16)
    hm[...] = dot_nn(pick, h[...]).astype(jnp.bfloat16)
    qm[...] = dot_nn(pick, q[...]).astype(jnp.bfloat16)
    listed = row_lists(pos[...] >> 6, allow[...]) > 0.5
    lane = lax.broadcasted_iota(jnp.int32, (pos.shape[0], LANES), 1)

    def one_slab(slab, sums):
        cols = pl.ds(pl.multiple_of(slab * LANES, LANES), LANES)
        query = (qm[:, cols].astype(jnp.float32) * HD ** (-0.5)).astype(jnp.bfloat16)
        mixed = None
        for half in range(2):
            scores = jnp.where(listed, dot_nt(one_head(query, half), k[:, cols]), NEG)
            top = jnp.max(scores, axis=-1, keepdims=True)
            weight = jnp.exp(scores - top)
            total_weight = jnp.sum(weight, axis=-1, keepdims=True)
            sums = jnp.where(lane == 2 * slab + half, top + jnp.log(total_weight), sums)
            found = dot_nn(weight.astype(jnp.bfloat16), v[:, cols]) * (1.0 / total_weight)
            mixed = found if half == 0 else jnp.where(head_half(0), mixed, found)
        om[:, cols] = mixed.astype(jnp.bfloat16)
        return sums

    none = jnp.zeros((pos.shape[0], LANES), jnp.float32)
    sums = lax.fori_loop(0, local // LANES, one_slab, none)
    lse[...] = sums
    part[...] = dot_nn(om[...], wo[...]).astype(jnp.bfloat16)


def gelu_parts(z):
    cdf = 0.5 * (1.0 + lax.erf(z * inv_root_two))
    return z * cdf, cdf + z * (jnp.exp(-0.5 * z * z) * inv_root_two_pi)


def middle_of(xm, part, other, vec):
    both = part[...].astype(jnp.float32) + other[...].astype(jnp.float32)
    return xm[...].astype(jnp.float32) + (both + vec[2:3, :])


def hidden_kernel(
    bits, xm, part, other, g_own, g_other, vec, wi, wf,
    wf_a, wf_as, wf_b, wf_bs, wi_a, wi_as, wi_b, wi_bs, dh2, few, g,
    u_all, h2_all, dz_all,
):
    width, hidden = wi.shape
    split = width // 2
    first = bits[2] == 0
    g[:, :split] = jnp.where(first, g_own[...], g_other[...])
    g[:, split:] = jnp.where(first, g_other[...], g_own[...])
    normed, _ = norm_parts(middle_of(xm, part, other, vec))
    h2_all[...] = (normed * vec[3:4, :] + vec[4:5, :]).astype(jnp.bfloat16)
    h2 = h2_all[...]
    for at in range(hidden // width):
        cols = pl.ds(at * width, width)
        z = dot_nn(h2, wi[:, cols]) + vec[7 + at : 8 + at, :]
        act, slope = gelu_parts(z)
        u_all[:, cols] = act.astype(jnp.bfloat16)
        dz = (dot_nt(g[...], wf[cols, :]) * slope).astype(jnp.bfloat16)
        dz_all[:, cols] = dz
        few[1 + at : 2 + at, :] = jnp.sum(dz.astype(jnp.float32), axis=0, keepdims=True)
    few[0:1, :] = jnp.sum(g[...].astype(jnp.float32), axis=0, keepdims=True)
    half = hidden // 2
    count = width // 2
    for order, keep, send in ((0, wf_a, wf_as), (1, wf_b, wf_bs)):
        for out, bit in ((keep, bits[order]), (send, 1 - bits[order])):
            at = pl.multiple_of(order * half + bit * count, LANES)
            out[0] = dot_tn(u_all[:, pl.ds(at, count)], g[...]).astype(jnp.bfloat16)
    for order, keep, send in ((0, wi_a, wi_as), (1, wi_b, wi_bs)):
        for out, bit in ((keep, bits[order]), (send, 1 - bits[order])):
            at = pl.multiple_of(bit * count, LANES)
            out[0] = dot_tn(
                h2_all[:, pl.ds(at, count)], dz_all[:, pl.ds(order * half, half)]
            ).astype(jnp.bfloat16)
    dh2[...] = dot_nt(dz_all[...], wi[...]).astype(jnp.bfloat16)


def attend_back_kernel(
    bits, xm, part, other, g, dh2, dh2_other, vec, wo, pos, allow, qm, om, hm, lse, h, k, v,
    da_a, da_as, da_b, da_bs, dx1, dq, dk, dv, few, da_all, do_all,
):
    width = g.shape[1]
    normed, scaled = norm_parts(middle_of(xm, part, other, vec))
    up = dh2[...].astype(jnp.float32) + dh2_other[...].astype(jnp.float32)
    few[0:1, :] = jnp.sum(up * normed, axis=0, keepdims=True)
    few[1:2, :] = jnp.sum(up, axis=0, keepdims=True)
    weighted = up * vec[3:4, :]
    centered = weighted - jnp.mean(weighted, axis=-1, keepdims=True)
    slope = jnp.mean(weighted * normed, axis=-1, keepdims=True)
    grad = g[...].astype(jnp.float32) + scaled * (centered - normed * slope)
    dx1[...] = grad
    low = grad.astype(jnp.bfloat16)
    da_all[...] = low
    few[2:3, :] = jnp.sum(low.astype(jnp.float32), axis=0, keepdims=True)
    do_all[...] = dot_nt(low, wo[...]).astype(jnp.bfloat16)
    listed = row_lists(pos[...] >> 6, allow[...]) > 0.5
    lane = lax.broadcasted_iota(jnp.int32, (1, LANES), 1)

    def one_slab(slab, carry):
        cols = pl.ds(pl.multiple_of(slab * LANES, LANES), LANES)
        query = (qm[:, cols].astype(jnp.float32) * HD ** (-0.5)).astype(jnp.bfloat16)
        grad_q, grad_k, grad_v = None, None, None
        for half in range(2):
            own = one_head(query, half)
            own_do = one_head(do_all[:, cols], half)
            scores = jnp.where(listed, dot_nt(own, k[:, cols]), NEG)
            total = jnp.where(lane == 2 * slab + half, lse[...], 0.0)
            prob = jnp.exp(scores - jnp.sum(total, axis=-1, keepdims=True))
            grad_p = dot_nt(own_do, v[:, cols])
            delta = jnp.sum(prob * grad_p, axis=-1, keepdims=True)
            ds = (prob * (grad_p - delta)).astype(jnp.bfloat16)
            found_q = dot_nn(ds, k[:, cols])
            found_k = dot_tn(ds, own)
            found_v = dot_tn(prob.astype(jnp.bfloat16), own_do)
            grad_q = found_q if half == 0 else jnp.where(head_half(0), grad_q, found_q)
            grad_k = found_k if half == 0 else grad_k + found_k
            grad_v = found_v if half == 0 else grad_v + found_v
        dq[:, cols] = (grad_q * HD ** (-0.5)).astype(jnp.bfloat16)
        dk[:, cols] = grad_k.astype(jnp.bfloat16)
        dv[:, cols] = grad_v.astype(jnp.bfloat16)
        return carry

    lax.fori_loop(0, qm.shape[1] // LANES, one_slab, 0)
    local = qm.shape[1]
    few[3:4, :local] = jnp.sum(dq[...].astype(jnp.float32), axis=0, keepdims=True)
    few[3:4, local:] = jnp.sum(dv[...].astype(jnp.float32), axis=0, keepdims=True)
    count = width // 2
    for keep, bit in ((da_a, bits[0]), (da_as, 1 - bits[0])):
        cols = pl.ds(pl.multiple_of(bit * count, LANES), count)
        keep[0, :, :local] = dot_tn(hm[:, cols], dq[...]).astype(jnp.bfloat16)
        keep[0, :, local:] = dot_tn(h[:, cols], dk[...]).astype(jnp.bfloat16)
    for keep, bit in ((da_b, bits[1]), (da_bs, 1 - bits[1])):
        cols = pl.ds(pl.multiple_of(bit * count, LANES), count)
        keep[0, :, :local] = dot_tn(h[:, cols], dv[...]).astype(jnp.bfloat16)
        keep[0, :, local:] = dot_tn(om[...], da_all[:, cols]).astype(jnp.bfloat16)


def input_kernel(bits, pos, dq, dk, dv, wq, wk, wv, keep, *rest):
    sends, dq_all = rest[:-1], rest[-1]
    total = dk.shape[0]
    dq_all[...] = dot_tn(pick_rows(pos[...], total), dq[...]).astype(jnp.bfloat16)
    run = BS * 2

    def one_piece(at, carry):
        here = pl.ds(pl.multiple_of(at * run, run), run)
        for out, bit in ((keep, bits[2]), (sends[0], 1 - bits[2])):
            rows = pl.ds(pl.multiple_of(at * 2 * run + bit * run, run), run)
            out[here, :] = (
                dot_nt(dq_all[rows, :], wq[...])
                + dot_nt(dk[rows, :], wk[...])
                + dot_nt(dv[rows, :], wv[...])
            ).astype(jnp.bfloat16)
        return carry

    lax.fori_loop(0, total // (2 * run), one_piece, 0)


def first_norm_kernel(count, bits, pos_half, own, dx1, vec, *rest):
    toks, others, grads = rest[:count], rest[count : -3 - count], rest[-3 - count : -3]
    few, tok, other = rest[-3:]
    run = others[0].shape[0]
    for at, piece in enumerate(others):
        other[pl.ds(at * run, run), :] = piece[...]
    run = toks[0].shape[0]
    for at, piece in enumerate(toks):
        tok[pl.ds(at * run, run), :] = piece[...]
    normed, scaled = norm_parts(tok[...].astype(jnp.float32))
    up = own[...].astype(jnp.float32) + other[...].astype(jnp.float32)
    few[0:1, :] = jnp.sum(up * normed, axis=0, keepdims=True)
    few[1:2, :] = jnp.sum(up, axis=0, keepdims=True)
    weighted = up * vec[0:1, :]
    centered = weighted - jnp.mean(weighted, axis=-1, keepdims=True)
    slope = jnp.mean(weighted * normed, axis=-1, keepdims=True)
    pick = pick_rows(pos_half[...], tok.shape[0])
    high = dx1[...].astype(jnp.bfloat16)
    rest = (dx1[...] - high.astype(jnp.float32)).astype(jnp.bfloat16)
    through = dot_tn(pick, high) + dot_tn(pick, rest)
    grad = (through + scaled * (centered - normed * slope)).astype(jnp.bfloat16)
    for at, piece in enumerate(grads):
        piece[0] = grad[at * run : (at + 1) * run, :]


def attend_kernel(at, bits, q, k, v, allow, keep, send, mixed_all):
    tile = mixed_all.shape[0]
    run = tile // 2
    rows = pl.ds(at * tile, tile)
    ids = lax.broadcasted_iota(jnp.int32, (tile, 1), 0)
    bias = (row_lists(at * (tile // BS) + (ids >> 6), allow[...]) - 1.0) * -NEG

    def one_slab(slab, carry):
        cols = pl.ds(pl.multiple_of(slab * LANES, LANES), LANES)
        query = (q[rows, cols].astype(jnp.float32) * HD ** (-0.5)).astype(jnp.bfloat16)
        mixed = None
        for half in range(2):
            scores = dot_nt(one_head(query, half), k[:, cols]) + bias
            weight = jnp.exp(scores - jnp.max(scores, axis=-1, keepdims=True))
            total_weight = jnp.sum(weight, axis=-1, keepdims=True)
            found = dot_nn(weight.astype(jnp.bfloat16), v[:, cols]) * (1.0 / total_weight)
            mixed = found if half == 0 else jnp.where(head_half(0), mixed, found)
        mixed_all[:, cols] = mixed.astype(jnp.bfloat16)
        return carry

    lax.fori_loop(0, q.shape[1] // LANES, one_slab, 0)
    for out, bit in ((keep, bits[2]), (send, 1 - bits[2])):
        out[...] = mixed_all[pl.ds(pl.multiple_of(bit * run, run), run), :]


def lay_kernel(bits, *refs):
    run = refs[0].shape[0]
    for at, piece in enumerate(refs[:-1]):
        refs[-1][pl.ds(at * run, run), :] = piece[...]


def feed_kernel(base, count, bits, *refs):
    toks, refs = refs[:count], refs[count:]
    own, refs = refs[:count], refs[count:]
    other, vec, bi_other, wo, wo_other, wi, wi_other, wf, wf_other = refs[:9]
    pairs, outs, mid_all = refs[9 : 9 + count], refs[-1 - count : -1], refs[-1]
    width, hidden = wi.shape
    run = toks[0].shape[0]
    for at in range(count):
        theirs = other[pl.ds((base + at) * run, run), :]
        mixed = dot_nn(own[at][...], wo[...]) + dot_nn(theirs, wo_other[...])
        mid_all[pl.ds(at * run, run), :] = toks[at][...].astype(jnp.float32) + (
            mixed + vec[2:3, :]
        )
    middle = mid_all[...]
    normed, _ = norm_parts(middle)
    h2 = (normed * vec[3:4, :] + vec[4:5, :]).astype(jnp.bfloat16)
    total = middle + vec[5:6, :]
    mid_all[...] = total
    for row, bias, inner, outer in ((7, vec, wi, wf), (0, bi_other, wi_other, wf_other)):

        def one_chunk(at, carry, row=row, bias=bias, inner=inner, outer=outer):
            cols = pl.ds(pl.multiple_of(at * width, LANES), width)
            z = dot_nn(h2, inner[:, cols]) + bias[pl.ds(row + at, 1), :]
            act = z * (0.5 * (1.0 + lax.erf(z * inv_root_two)))
            mid_all[...] += dot_nn(act.astype(jnp.bfloat16), outer[cols, :])
            return carry

        lax.fori_loop(0, hidden // width, one_chunk, 0)
    low = mid_all[...].astype(jnp.bfloat16)
    for at in range(count):
        outs[at][0] = pairs[at][0]
        outs[at][1] = low[at * run : (at + 1) * run, :]


def gather_small_kernel(bits, first, first_other, attend, hidden, out):
    out[0:2, :] = first[...] + first_other[...]
    out[2:6, :] = attend[...]
    out[6:, :] = hidden[...]


def add_small_kernel(bits, own, other, out):
    out[...] = own[...] + other[...]


def interleave_kernel(bits, *refs):
    count = (len(refs) - 2) // 2
    own, over, outs = refs[:count], refs[count : 2 * count], refs[2 * count :]
    run = own[0].shape[1]
    for at in range(count):
        window = bits[5] ^ at
        for which, out in enumerate(outs):
            for pieces, side in ((own, bits[2]), (over, 1 - bits[2])):
                rows = pl.ds(pl.multiple_of(side * run, run), run)
                out[window, rows, :] = pieces[at][which]


def add_low(left, right):
    return (left.astype(jnp.float32) + right.astype(jnp.float32)).astype(jnp.bfloat16)


def part_rows(bit, count):
    return pl.ds(pl.multiple_of(bit * count, 16), count)


def halve_plane_kernel(at, bits, ka, ra, kb, rb, keep_a, send_a, keep_b, send_b):
    count = keep_a.shape[1]
    groups = ((ka, ra, keep_a, send_a, bits[at[0]]), (kb, rb, keep_b, send_b, bits[at[1]]))
    for k, r, keep, send, bit in groups:
        for out, side in ((keep, bit), (send, 1 - bit)):
            rows = part_rows(side, count)
            out[...] = add_low(k[:, rows, :], r[:, rows, :])


def halve_join_kernel(at, bits, ka, ra, kb, rb, keep, send):
    group, count = ka.shape[0], keep.shape[1]
    for out, side in ((keep, bits[at]), (send, 1 - bits[at])):
        rows = part_rows(side, count)
        out[:group] = add_low(ka[:, rows, :], ra[:, rows, :])
        out[group:] = add_low(kb[:, rows, :], rb[:, rows, :])


def halve_line_kernel(at, bits, k, r, keep, send):
    count = keep.shape[1]
    for out, side in ((keep, bits[at]), (send, 1 - bits[at])):
        rows = part_rows(side, count)
        out[...] = add_low(k[:, rows, :], r[:, rows, :])


def last_line_kernel(bits, k, r, out):
    out[...] = add_low(k[...], r[...])


def double_line_kernel(at, bits, own, other, out):
    count = own.shape[1]
    out[:, part_rows(bits[at], count), :] = own[...]
    out[:, part_rows(1 - bits[at], count), :] = other[...]


def double_split_kernel(at, bits, own, other, out_a, out_b):
    count = own.shape[1]
    group = out_a.shape[0]
    for which, out in ((0, out_a), (1, out_b)):
        part = pl.ds(which * group, group)
        out[:, part_rows(bits[at], count), :] = own[part]
        out[:, part_rows(1 - bits[at], count), :] = other[part]


def double_plane_kernel(at, bits, own_a, other_a, own_b, other_b, out_a, out_b):
    groups = ((own_a, other_a, out_a, bits[at[0]]), (own_b, other_b, out_b, bits[at[1]]))
    for own, other, out, bit in groups:
        count = own.shape[1]
        out[:, part_rows(bit, count), :] = own[...]
        out[:, part_rows(1 - bit, count), :] = other[...]


def last_rows_kernel(at, bits, own_a, other_a, own_b, other_b, out):
    count = own_a.shape[1]
    groups = ((own_a, other_a, bits[at[0]]), (own_b, other_b, bits[at[1]]))
    for which, (own, other, bit) in enumerate(groups):
        for value, side in ((own, bit), (other, 1 - bit)):
            out[part_rows(2 * which + side, count), :] = value[0].astype(jnp.float32)


def last_columns_kernel(at, bits, own_a, other_a, own_b, other_b, out):
    count, width = own_a.shape[1:]
    groups = ((own_a, other_a, bits[at[0]]), (own_b, other_b, bits[at[1]]))
    for which, (own, other, bit) in enumerate(groups):
        for value, side in ((own, bit), (other, 1 - bit)):
            out[part_rows(side, count), pl.ds(which * width, width)] = value[0].astype(
                jnp.float32
            )


def last_attend_kernel(
    at, bits, own_a, other_a, own_b, other_b, grad_q, grad_k, grad_v, grad_o
):
    count = own_a.shape[1]
    local = grad_q.shape[1]
    for value, side in ((own_a, bits[at[0]]), (other_a, 1 - bits[at[0]])):
        grad_q[part_rows(side, count), :] = value[0, :, :local].astype(jnp.float32)
        grad_k[part_rows(side, count), :] = value[0, :, local:].astype(jnp.float32)
    for value, side in ((own_b, bits[at[1]]), (other_b, 1 - bits[at[1]])):
        grad_v[part_rows(side, count), :] = value[0, :, :local].astype(jnp.float32)
        cols = pl.ds(pl.multiple_of(side * count, LANES), count)
        grad_o[:, cols] = value[0, :, local:].astype(jnp.float32)


def joined_size(piece):
    group, rows, width = piece.shape
    return shape((group, 2 * rows, width))


def halved_size(piece):
    group, rows, width = piece.shape
    return shape((group, rows // 2, width))


def flip(value, axis, bit):
    return lax.ppermute(value, axis, [(i, i ^ bit) for i in range(lax.axis_size(axis))])


def bit_of(axis, bit):
    return jnp.where((lax.axis_index(axis) & bit) != 0, 1, 0).astype(jnp.int32)


def stages_of(order):
    dp_bits = [("dp", 1 << i) for i in range(lax.axis_size("dp").bit_length() - 1)]
    seq_bits = [("seq", 1 << i) for i in range(lax.axis_size("seq").bit_length() - 1)]
    return (dp_bits if order == 0 else dp_bits[::-1]) + seq_bits


class Summing:
    def __init__(self, order, bits, keep, send):
        self.order, self.bits = order, bits
        self.keep, self.send = list(keep), list(send)
        self.plane = [stages_of(which)[:2] for which in range(2)]
        self.line = stages_of(0)[2:]

    def hold(self, *others):
        self.send = [after(value, *others) for value in self.send]

    def exchange(self, at):
        self.got = [flip(s, *self.plane[which][at]) for which, s in enumerate(self.send)]
        return self.got

    def exchange_line(self, at):
        return flip(self.send, *self.line[at])

    def halve_first(self):
        other = self.got
        ka, sa, kb, sb = self.order.call(
            functools.partial(halve_plane_kernel, (1, 0)),
            [halved_size(self.keep[0])] * 4,
            (self.bits, self.keep[0], other[0], self.keep[1], other[1]),
        )
        self.keep, self.send = [ka, kb], [sa, sb]

    def halve_second(self):
        other = self.got
        group, rows, width = self.keep[0].shape
        self.keep, self.send = self.order.call(
            functools.partial(halve_join_kernel, 3),
            [shape((2 * group, rows // 2, width))] * 2,
            (self.bits, self.keep[0], other[0], self.keep[1], other[1]),
        )

    def halve_line(self, at, other):
        two, rows, width = self.keep.shape
        if at + 1 < len(self.line):
            self.keep, self.send = self.order.call(
                functools.partial(halve_line_kernel, 4 + at),
                [shape((two, rows // 2, width))] * 2,
                (self.bits, self.keep, other),
            )
        else:
            (self.send,) = self.order.call(
                last_line_kernel, [shape(self.keep.shape)], (self.bits, self.keep, other)
            )

    def double_line(self, at, other):
        two, rows, width = self.send.shape
        if at > 0:
            (self.send,) = self.order.call(
                functools.partial(double_line_kernel, 3 + at),
                [shape((two, 2 * rows, width))],
                (self.bits, self.send, other),
            )
        else:
            self.send = self.order.call(
                functools.partial(double_split_kernel, 3 + at),
                [shape((two // 2, 2 * rows, width))] * 2,
                (self.bits, self.send, other),
            )

    def double_second(self):
        other = self.got
        self.send = self.order.call(
            functools.partial(double_plane_kernel, (1, 0)),
            [joined_size(self.send[0])] * 2,
            (self.bits, self.send[0], other[0], self.send[1], other[1]),
        )

    def write(self, kernel, outs):
        return self.order.call(
            functools.partial(kernel, (0, 1)),
            [shape(dims, jnp.float32) for dims in outs],
            (self.bits, self.send[0], self.got[0], self.send[1], self.got[1]),
        )


STEPS = (
    "I.0", "W.wf", "f.h1", "i.go", "W.wi", "f.h2", "A.0", "f.l0", "i.h1", "a.go", "W.wo",
    "A.1", "i.h2", "A.2", "i.l0", "A.3", "f.l1", "i.l1", "W.bi", "a.h1", "X.0", "f.d1", "N.0",
    "a.h2", "f.d0", "F.0", "a.l0", "i.d1", "f.e2", "F.1", "i.d0", "a.l1", "S.0", "f.wr",
    "S.1", "a.d1", "i.e2", "a.d0", "S.2", "R.3", "i.wr", "S.3", "R.1", "S.4", "R.2", "Q.0",
    "Q.1", "a.e2", "Q.3", "Q.2", "a.wr", "L.all",
)


def window_body(
    tokens, cotangent, masked_pos, rand_blocks, ln1_gain, ln1_bias, w_query, b_query, w_key,
    w_value, b_value, w_out, b_out, ln2_gain, ln2_bias, w_inner, b_inner, w_outer, b_outer,
):
    windows, rows, width = tokens.shape
    local = w_query.shape[1]
    hidden = w_inner.shape[1]
    total = windows * rows
    blocks = total // BS
    run = rows // 2
    split = width // 2
    place = lax.axis_index("seq")
    core = lax.axis_index("tensor")
    plane, line = stages_of(0)[:2], stages_of(0)[2:]
    bits = jnp.stack(
        [bit_of(*step) for step in plane]
        + [core.astype(jnp.int32)]
        + [bit_of(*step) for step in line]
        + [place.astype(jnp.int32)]
    )

    cut = tokens.reshape(windows, 2, run, width)
    own_rows = []
    for at in range(windows):
        piece = lax.dynamic_slice(cut, (place ^ at, core, 0, 0), (1, 1, run, width))
        piece = piece.reshape(run, width)
        own_rows.append(piece if at == 0 else flip(piece, "seq", at))

    named = masked_pos.shape[1]
    count = -(-named // 16) * 16
    spots = jnp.concatenate(
        [masked_pos, jnp.full((windows, count - named), -1, jnp.int32)], axis=1
    )
    slot = jnp.arange(count, dtype=jnp.int32)
    again = jnp.any(
        (spots[:, :, None] == spots[:, None, :]) & (slot[None, :] < slot[:, None])[None], axis=2
    )
    spots = jnp.where(again, -1, spots)
    spot = lax.dynamic_index_in_dim(spots, place, 0, keepdims=True).reshape(count, 1)
    there, inside = (spot // rows) ^ place, spot % rows
    pos = jnp.where(spot >= 0, there * rows + inside, -1)
    mine = (spot >= 0) & (inside // run == core)
    pos_half = jnp.where(mine, there * run + inside % run, -1)

    here = spots - place * rows
    found = []
    for at in range(windows):
        named_rows = lax.dynamic_index_in_dim(here, place ^ at, 0, keepdims=False)
        pick = (named_rows[:, None] == jnp.arange(rows, dtype=jnp.int32)[None, :]).astype(
            jnp.bfloat16
        )
        shard = lax.dynamic_slice(
            cotangent, (place ^ at, 0, core * split), (1, rows, split)
        ).reshape(rows, split)
        found.append(dot_nn(pick, shard).astype(jnp.bfloat16))

    rand = lax.dynamic_index_in_dim(rand_blocks, place, 0, keepdims=False)
    numbers = jnp.arange(blocks, dtype=jnp.int32)
    shard_blocks = rows // BS
    ids = ((numbers // shard_blocks) ^ place) * shard_blocks + numbers % shard_blocks
    named_blocks = jnp.any(rand[:, :, None] == ids[None, None, :], axis=1)
    named_blocks = jnp.any(
        (ids[:, None] == numbers[None, :])[:, :, None] & named_blocks[None], axis=1
    )
    listed = (
        (jnp.abs(ids[:, None] - ids[None, :]) <= 1)
        | (ids == 0)[None, :]
        | (ids == blocks - 1)[None, :]
        | named_blocks
    )
    allow = jnp.repeat(listed.astype(jnp.bfloat16), BS, axis=1)

    rows_wide = [ln1_gain, ln1_bias, b_out, ln2_gain, ln2_bias, b_outer, b_query, b_value, b_inner]
    vec = jnp.concatenate([x.astype(jnp.float32) for x in rows_wide]).reshape(-1, width)

    order = Order()
    state = None
    for at in range(windows):
        if at == 1:
            order.need(pos, pos_half, allow, *own_rows[1:], *found)
        kept = () if state is None else tuple(state)
        over = own_rows[at] if at == 0 else after(own_rows[at], entry)
        state = order.call(
            functools.partial(shard_kernel, at),
            [shape((total, width))] * 2 + [shape((total, local))] * 3,
            (bits, own_rows[at], flip(over, "tensor", 1), vec, w_query, w_key, w_value) + kept,
            aliases={7 + i: i for i in range(len(kept))},
        )
        if at == 0:
            entry = order.last
    tok, h, q, k, v = state
    found = [found[0]] + [
        flip(after(found[i], *own_rows[1:]), "seq", i) for i in range(1, windows)
    ]
    xm, hm, qm, om, lse, part = order.call(
        front_kernel,
        [shape((count, width))] * 2
        + [shape((count, local))] * 2
        + [shape((count, LANES), jnp.float32), shape((count, width))],
        (bits, pos, allow, w_out, tok, h, q, k, v),
    )
    other = flip(part, "tensor", 1)
    (g_own,) = order.call(sum_rows_kernel, [shape((count, split))], (bits, *found))
    g_other = flip(g_own, "tensor", 1)
    outs = order.call(
        hidden_kernel,
        [shape((1, width // 2, width))] * 8
        + [shape((count, width)), shape((1 + hidden // width, width), jnp.float32)]
        + [shape((count, width))],
        (bits, xm, part, other, g_own, g_other, vec, w_inner, w_outer),
        scratch=[
            pltpu.VMEM((count, hidden), jnp.bfloat16),
            pltpu.VMEM((count, width), jnp.bfloat16),
            pltpu.VMEM((count, hidden), jnp.bfloat16),
        ],
    )
    wf_a, wf_as, wf_b, wf_bs, wi_a, wi_as, wi_b, wi_bs, dh2, few_hidden, g = outs
    sum_f = Summing(order, bits, (wf_a, wf_b), (wf_as, wf_bs))
    sum_i = Summing(order, bits, (wi_a, wi_b), (wi_as, wi_bs))

    held = {}
    sum_f.exchange(0)
    dh2_other = flip(dh2, "tensor", 1)
    outs = order.call(
        attend_back_kernel,
        [shape((1, width // 2, 2 * local))] * 2
        + [shape((1, width // 2, local + width // 2))] * 2
        + [shape((count, width), jnp.float32), shape((count, local))]
        + [shape((total, local))] * 2
        + [shape((4, width), jnp.float32)],
        (bits, xm, part, other, g, dh2, dh2_other, vec, w_out, pos, allow)
        + (qm, om, hm, lse, h, k, v),
        scratch=[
            pltpu.VMEM((count, width), jnp.bfloat16),
            pltpu.VMEM((count, local), jnp.bfloat16),
        ],
    )
    da_a, da_as, da_b, da_bs, dx1, dq, dk, dv, few_attend = outs
    sum_a = Summing(order, bits, (da_a, da_b), (da_as, da_bs))

    def attend(at):
        keep, send = order.call(
            functools.partial(attend_kernel, at),
            [shape((run, local))] * 2,
            (bits, q, k, v, allow),
            scratch=[pltpu.VMEM((rows, local), jnp.bfloat16)],
        )
        held.setdefault("keep", []).append(keep)
        held.setdefault("send", []).append(send)

    def feed(base, pieces):
        span = slice(base, base + pieces)
        held["pair"][span] = order.call(
            functools.partial(feed_kernel, base, pieces),
            [shape((2, run, width))] * pieces,
            (bits, *own_rows[span], *held["keep"][span], held["mixed_other"], vec)
            + (held["bi"], w_out, held["wo"], w_inner, held["wi"], w_outer, held["wf"])
            + tuple(held["pair"][span]),
            scratch=[pltpu.VMEM((pieces * run, width), jnp.float32)],
            aliases={10 + 2 * pieces + i: i for i in range(pieces)},
        )

    small_steps = iter(stages_of(0)[::-1])
    sums = {"f": sum_f, "i": sum_i, "a": sum_a}

    def swap(value, kernels=2):
        other = flip(after(value, order.last), "tensor", 1)
        order.soon(other, kernels)
        return other

    def sum_step(of, step):
        one = sums[of]
        if step == "go":
            one.hold(order.last)
            one.exchange(0)
        elif step == "h1":
            one.halve_first()
            one.exchange(1)
        elif step == "h2":
            one.halve_second()
            held[of] = one.exchange_line(0)
        elif step == "l0":
            one.halve_line(0, held[of])
            held[of] = one.exchange_line(1)
        elif step == "l1":
            one.halve_line(1, held[of])
            held[of] = one.exchange_line(1)
        elif step == "d1":
            one.double_line(1, held[of])
            held[of] = one.exchange_line(0)
        elif step == "d0":
            one.double_line(0, held[of])
            one.exchange(1)
        elif step == "e2":
            one.double_second()
            one.exchange(0)
        elif of == "f":
            (held["grad_wf"],) = one.write(last_rows_kernel, [(hidden, width)])
        elif of == "i":
            (held["grad_wi"],) = one.write(last_columns_kernel, [(width, hidden)])
        else:
            held["grad_a"] = one.write(last_attend_kernel, [(width, local)] * 3 + [(local, width)])

    def input_grad():
        held["dh_own"], dh_send = order.call(
            input_kernel,
            [shape((total // 2, width))] * 2,
            (bits, pos, dq, dk, dv, w_query, w_key, w_value),
            scratch=[pltpu.VMEM((total, local), jnp.bfloat16)],
        )
        held["dh_other"] = flip(dh_send, "tensor", 1)

    def first_norm():
        *held["pair"], held["few"] = order.call(
            functools.partial(first_norm_kernel, windows),
            [shape((2, run, width))] * windows + [shape((2, width), jnp.float32)],
            (bits, pos_half, held["dh_own"], dx1, vec, *own_rows, held["dh_other"]),
            scratch=[pltpu.VMEM((total // 2, width), jnp.bfloat16)] * 2,
        )
        held["few_other"] = flip(held["few"], "tensor", 1)
        order.soon(held["few_other"])

    def small(step):
        if step == "0":
            (held["small"],) = order.call(
                gather_small_kernel,
                [shape((7 + hidden // width, width), jnp.float32)],
                (bits, held["few"], held["few_other"], few_attend, few_hidden),
            )
        else:
            (held["small"],) = order.call(
                add_small_kernel,
                [shape(held["small"].shape, jnp.float32)],
                (bits, held["small"], held["small_other"]),
            )
        if step != "4":
            held["small_other"] = flip(held["small"], *next(small_steps))

    def send_back(at):
        held["pair"][at] = flip(after(held["pair"][at], order.last), "seq", at)
        order.soon(held["pair"][at], 3)

    def swap_back(at):
        held.setdefault("over", {})[at] = swap(held["pair"][at])

    def interleave():
        over = [held["over"][at] for at in range(windows)]
        held["all"] = order.call(
            interleave_kernel,
            [shape((windows, rows, width))] * 2,
            (bits, *held["pair"], *over),
        )

    for step in STEPS:
        kind, what = step[0], step[2:]
        if kind in sums:
            sum_step(kind, what)
        elif kind == "A":
            attend(int(what))
        elif kind == "F":
            feed(int(what) * windows // 2, windows // 2)
        elif kind == "W":
            held[what] = swap({"wi": w_inner, "wf": w_outer, "wo": w_out, "bi": vec[7:]}[what])
        elif kind == "X":
            laid = order.call(lay_kernel, [shape((windows * run, local))], (bits, *held["send"]))
            held["mixed_other"] = swap(laid[0])
        elif kind == "S":
            small(what)
        elif kind == "R":
            send_back(int(what))
        elif kind == "Q":
            swap_back(int(what))
        elif kind == "L":
            interleave()
        elif kind == "I":
            input_grad()
        else:
            first_norm()
    grad_tokens, out = held["all"]
    grad_q, grad_k, grad_v, grad_o = held["grad_a"]
    grad_wf, grad_wi, small_all = held["grad_wf"], held["grad_wi"], held["small"]
    return (
        out,
        grad_tokens,
        small_all[0],
        small_all[1],
        grad_q,
        small_all[5, :local],
        grad_k,
        grad_v,
        small_all[5, local:],
        grad_o,
        small_all[4],
        small_all[2],
        small_all[3],
        grad_wi,
        small_all[7:].reshape(-1),
        grad_wf,
        small_all[6],
    )


def with_halo(block, sides, width):
    for axis, dim in sides:
        count = lax.axis_size(axis)
        forward = [(i, i + 1) for i in range(count - 1)]
        backward = [(target, source) for source, target in forward]
        low = lax.ppermute(
            lax.slice_in_dim(block, block.shape[dim] - width, None, axis=dim), axis, forward
        )
        high = lax.ppermute(lax.slice_in_dim(block, 0, width, axis=dim), axis, backward)
        block = jnp.concatenate([low, block, high], axis=dim)
    return block


def broadcast(value, axis, root):
    mine = lax.axis_index(axis) == root
    return lax.psum(jnp.where(mine, value, jnp.zeros_like(value)), axis)


def norm_forward(values, gain, shift):
    center = values - jnp.mean(values, axis=-1, keepdims=True)
    scaled = lax.rsqrt(jnp.mean(center * center, axis=-1, keepdims=True) + eps_norm)
    normed = center * scaled
    return (normed * gain + shift, normed, scaled)


def norm_backward(upstream, gain, normed, scaled):
    weighted = upstream * gain
    centered = weighted - jnp.mean(weighted, axis=-1, keepdims=True)
    return scaled * (centered - normed * jnp.mean(weighted * normed, axis=-1, keepdims=True))


def row_dot(left, right):
    return lax.dot_general(
        left, right, (((left.ndim - 1,), (0,)), ((), ())), preferred_element_type=jnp.float32
    )


def back_dot(left, right):
    return lax.dot_general(
        left, right, (((left.ndim - 1,), (1,)), ((), ())), preferred_element_type=jnp.float32
    )


def outer_sum(left, right):
    return lax.dot_general(
        left, right, (((0, 1), (0, 1)), ((), ())), preferred_element_type=jnp.float32
    )


def column_sum(values):
    return jnp.sum(values, axis=(0, 1), dtype=jnp.float32)


def list_masks(rand_local, first_block, block_count):
    window_count, local_count = (rand_local.shape[0], rand_local.shape[1])
    query_ids = first_block + jnp.arange(local_count, dtype=jnp.int32)
    slide_ok = jnp.stack(
        [query_ids - 1 >= 0, query_ids >= 0, query_ids + 1 <= block_count - 1], axis=1
    )
    end_ok = jnp.stack([jnp.abs(query_ids) > 1, jnp.abs(block_count - 1 - query_ids) > 1], axis=1)
    rand_ok = (
        (jnp.abs(rand_local - query_ids[None, :, None]) > 1)
        & (rand_local != 0)
        & (rand_local != block_count - 1)
    )
    fixed_ok = jnp.broadcast_to(
        jnp.concatenate([slide_ok, end_ok], axis=1)[None], (window_count, local_count, 5)
    )
    return jnp.concatenate([fixed_ok, rand_ok], axis=-1)


def build_routing(rand_batch, position, devices, local_count, capacity):
    window_count = rand_batch.shape[0]
    item_count = window_count * local_count * 3

    def arrange(grid_values):
        grid_values = grid_values.reshape(window_count, devices, local_count, 3)
        return jnp.transpose(grid_values, (1, 0, 2, 3)).reshape(devices, item_count)

    window_grid = jnp.broadcast_to(
        jnp.arange(window_count, dtype=jnp.int32)[:, None, None], rand_batch.shape
    )
    owner_table = arrange(rand_batch // local_count)
    source_table = arrange(window_grid * local_count + rand_batch % local_count)
    device_ids = jnp.arange(devices, dtype=jnp.int32)
    matches = (owner_table[:, :, None] == device_ids[None, None, :]).astype(jnp.int32)
    earlier = jnp.cumsum(matches, axis=1) - matches
    slot_table = jnp.sum(earlier * matches, axis=2)
    owned_here = (owner_table == position).astype(jnp.int32)
    slot_ids = jnp.arange(capacity, dtype=jnp.int32)
    slot_matches = (slot_table[:, :, None] == slot_ids[None, None, :]).astype(
        jnp.int32
    ) * owned_here[:, :, None]
    send_rows = jnp.sum(slot_matches * source_table[:, :, None], axis=1).reshape(devices * capacity)
    send_live = jnp.sum(slot_matches, axis=1).reshape(devices * capacity)
    my_owner = lax.dynamic_index_in_dim(owner_table, position, 0, keepdims=False)
    my_slot = lax.dynamic_index_in_dim(slot_table, position, 0, keepdims=False)
    take_rows = my_owner * capacity + my_slot
    return (send_rows, send_live, take_rows)


def fetch_blocks(packed, routing, block_rows):
    window_count, local_rows, kv_width = packed.shape
    local_count = local_rows // block_rows
    devices = lax.axis_size("seq")
    padded = with_halo(packed, (("seq", 1),), block_rows)
    padded = padded.reshape(window_count, local_count + 2, block_rows, kv_width)
    sliding = jnp.stack([padded[:, offset : offset + local_count] for offset in range(3)], axis=2)
    first_part = broadcast(packed[:, :block_rows], "seq", 0)
    last_part = broadcast(packed[:, local_rows - block_rows :], "seq", devices - 1)
    end_blocks = jnp.stack([first_part, last_part], axis=1)
    end_blocks = jnp.broadcast_to(
        end_blocks[:, None], (window_count, local_count, 2, block_rows, kv_width)
    )
    send_rows, send_live, take_rows = routing
    sources = packed.reshape(window_count * local_count, block_rows, kv_width)
    outgoing = jnp.take(sources, send_rows, axis=0).reshape(devices, -1, block_rows, kv_width)
    incoming = lax.all_to_all(outgoing, "seq", split_axis=0, concat_axis=0, tiled=True).reshape(
        -1, block_rows, kv_width
    )
    fetched = jnp.take(incoming, take_rows, axis=0).reshape(
        window_count, local_count, 3, block_rows, kv_width
    )
    return jnp.concatenate([sliding, end_blocks, fetched], axis=2)


def return_blocks(kv_grads, routing, block_rows):
    window_count, local_count = (kv_grads.shape[0], kv_grads.shape[1])
    kv_width = kv_grads.shape[-1]
    local_rows = local_count * block_rows
    devices = lax.axis_size("seq")
    position = lax.axis_index("seq")
    padded_grad = jnp.zeros((window_count, local_count + 2, block_rows, kv_width), jnp.float32)
    for offset in range(3):
        padded_grad = padded_grad.at[:, offset : offset + local_count].add(kv_grads[:, :, offset])
    rim_rows = jnp.concatenate([padded_grad[:, 0], padded_grad[:, local_count + 1]], axis=1)
    rim_back = with_halo(rim_rows.astype(jnp.bfloat16), (("seq", 1),), block_rows).astype(
        rim_rows.dtype
    )
    end_grads = lax.psum(jnp.sum(kv_grads[:, :, 3:5], axis=1).astype(jnp.bfloat16), "seq").astype(
        jnp.float32
    )
    zeros_block = jnp.zeros((window_count, block_rows, kv_width), jnp.float32)
    first_add = rim_back[:, :block_rows] + jnp.where(position == 0, end_grads[:, 0], zeros_block)
    last_add = rim_back[:, 3 * block_rows :] + jnp.where(
        position == devices - 1, end_grads[:, 1], zeros_block
    )
    send_rows, send_live, take_rows = routing
    rand_items = kv_grads[:, :, 5:8].reshape(-1, block_rows, kv_width)
    capacity_rows = send_rows.shape[0]
    outgoing = (
        jnp.zeros((capacity_rows, block_rows, kv_width), jnp.float32).at[take_rows].set(rand_items)
    )
    incoming = lax.all_to_all(
        outgoing.reshape(devices, -1, block_rows, kv_width).astype(jnp.bfloat16),
        "seq",
        split_axis=0,
        concat_axis=0,
        tiled=True,
    ).astype(jnp.float32)
    incoming = (
        incoming.reshape(capacity_rows, block_rows, kv_width)
        * send_live.astype(jnp.float32)[:, None, None]
    )
    from_owners = (
        jnp.zeros((window_count * local_count, block_rows, kv_width), jnp.float32)
        .at[send_rows]
        .add(incoming)
    )
    summed = padded_grad[:, 1 : local_count + 1].reshape(window_count, local_rows, kv_width)
    summed = summed + from_owners.reshape(window_count, local_rows, kv_width)
    summed = summed.at[:, :block_rows].add(first_add)
    summed = summed.at[:, local_rows - block_rows :].add(last_add)
    return summed


def split_scores(query_low, keyset, key_valid):
    window_count, local_rows, local_width = query_low.shape
    local_count = keyset.shape[1]
    head_count = local_width // HD
    key_rows = keyset.shape[2] * BS
    query_split = query_low.reshape(window_count, local_count, BS, head_count, HD)
    paired = keyset.reshape(window_count, local_count, key_rows, 2, head_count, HD)
    key_part = paired[:, :, :, 0]
    value_part = paired[:, :, :, 1]
    scores = jnp.einsum(
        "wbqhd,wbkhd->wbhqk", query_split, key_part, preferred_element_type=jnp.float32
    ) * HD ** (-0.5)
    allowed = jnp.repeat(key_valid, BS, axis=2)[:, :, None, None, :]
    scores = jnp.where(allowed, scores, -1e30)
    return (scores, query_split, key_part, value_part)


def attend_forward(query_low, keyset, key_valid):
    scores, query_split, key_part, value_part = split_scores(query_low, keyset, key_valid)
    top_score = jnp.max(scores, axis=-1, keepdims=True)
    log_total = top_score + jnp.log(jnp.sum(jnp.exp(scores - top_score), axis=-1, keepdims=True))
    weights = jnp.exp(scores - log_total).astype(jnp.bfloat16)
    mixed = jnp.einsum(
        "wbhqk,wbkhd->wbqhd", weights, value_part, preferred_element_type=jnp.float32
    )
    return (mixed.reshape(query_low.shape).astype(jnp.bfloat16), log_total)


def attend_backward(query_low, keyset, key_valid, log_total, grad_mixed):
    scores, query_split, key_part, value_part = split_scores(query_low, keyset, key_valid)
    window_count, local_count = (keyset.shape[0], keyset.shape[1])
    local_width = query_low.shape[2]
    weights = jnp.exp(scores - log_total)
    grad_split = grad_mixed.reshape(query_split.shape)
    grad_weights = jnp.einsum(
        "wbqhd,wbkhd->wbhqk", grad_split, value_part, preferred_element_type=jnp.float32
    )
    delta_sum = jnp.sum(weights * grad_weights, axis=-1, keepdims=True)
    grad_scores = (weights * (grad_weights - delta_sum)).astype(jnp.bfloat16)
    grad_query = jnp.einsum(
        "wbhqk,wbkhd->wbqhd", grad_scores, key_part, preferred_element_type=jnp.float32
    ) * HD ** (-0.5)
    grad_key = jnp.einsum(
        "wbhqk,wbqhd->wbkhd", grad_scores, query_split, preferred_element_type=jnp.float32
    ) * HD ** (-0.5)
    grad_value = jnp.einsum(
        "wbhqk,wbqhd->wbkhd",
        weights.astype(jnp.bfloat16),
        grad_split,
        preferred_element_type=jnp.float32,
    )
    list_shape = (window_count, local_count, keyset.shape[2], BS, local_width)
    kv_grads = jnp.concatenate(
        [grad_key.reshape(list_shape), grad_value.reshape(list_shape)], axis=-1
    )
    return (grad_query.reshape(query_low.shape), kv_grads)


def flatten_all(members):
    return jnp.concatenate([member.reshape(-1) for member in members])


def share_sum(vector):
    return lax.psum_scatter(vector, ("dp", "seq"), scatter_dimension=0, tiled=True)


def spread_body(
    tokens,
    cotangent,
    masked_pos,
    rand_blocks,
    ln1_gain,
    ln1_bias,
    w_query,
    b_query,
    w_key,
    w_value,
    b_value,
    w_out,
    b_out,
    ln2_gain,
    ln2_bias,
    w_inner,
    b_inner,
    w_outer,
    b_outer,
):
    local_rows = tokens.shape[1]
    devices = lax.axis_size("seq")
    position = lax.axis_index("seq")
    block_count = rand_blocks.shape[1]
    local_count = block_count // devices
    capacity = (3 * WIN_MB * local_count + devices - 1) // devices
    gain_one = ln1_gain.astype(jnp.float32)
    bias_one = ln1_bias.astype(jnp.float32)
    gain_two = ln2_gain.astype(jnp.float32)
    bias_two = ln2_bias.astype(jnp.float32)
    row_ids = position * local_rows + jnp.arange(local_rows, dtype=jnp.int32)
    first_block = position * local_count
    outputs = []
    input_grads = []
    totals = None
    for batch_index in range(MB):
        batch_start = batch_index * WIN_MB
        batch_stop = batch_start + WIN_MB
        tokens_now = tokens[batch_start:batch_stop].astype(jnp.float32)
        rand_now = rand_blocks[batch_start:batch_stop]
        routing = build_routing(rand_now, position, devices, local_count, capacity)
        rand_local = lax.dynamic_slice_in_dim(rand_now, first_block, local_count, 1)
        key_valid = list_masks(rand_local, first_block, block_count)
        hidden_one, normed_one, scaled_one = norm_forward(tokens_now, gain_one, bias_one)
        hidden_low = hidden_one.astype(jnp.bfloat16)
        query_low = (row_dot(hidden_low, w_query) + b_query.astype(jnp.float32)).astype(
            jnp.bfloat16
        )
        key_low = row_dot(hidden_low, w_key).astype(jnp.bfloat16)
        value_low = (row_dot(hidden_low, w_value) + b_value.astype(jnp.float32)).astype(
            jnp.bfloat16
        )
        packed = jnp.concatenate([key_low, value_low], axis=2)
        keyset = fetch_blocks(packed, routing, BS)
        mixed_low, log_total = attend_forward(query_low, keyset, key_valid)
        attn_out = lax.psum(row_dot(mixed_low, w_out).astype(jnp.bfloat16), "tensor").astype(
            jnp.float32
        ) + b_out.astype(jnp.float32)
        middle = tokens_now + attn_out
        hidden_two, normed_two, scaled_two = norm_forward(middle, gain_two, bias_two)
        hidden_two_low = hidden_two.astype(jnp.bfloat16)
        inner_pre = row_dot(hidden_two_low, w_inner) + b_inner.astype(jnp.float32)
        active = jax.nn.gelu(inner_pre, approximate=False).astype(jnp.bfloat16)
        ffn_out = lax.psum(row_dot(active, w_outer).astype(jnp.bfloat16), "tensor").astype(
            jnp.float32
        ) + b_outer.astype(jnp.float32)
        outputs.append((middle + ffn_out).astype(jnp.bfloat16))
        masked_now = masked_pos[batch_start:batch_stop]
        chosen = jnp.any(row_ids[None, :, None] == masked_now[:, None, :], axis=2)
        cot_now = cotangent[batch_start:batch_stop]
        grad_top = jnp.where(chosen[:, :, None], cot_now, jnp.zeros_like(cot_now))
        grad_active = back_dot(grad_top, w_outer)
        normal_cdf = 0.5 * (1.0 + lax.erf(inner_pre * inv_root_two))
        density = jnp.exp(-0.5 * inner_pre * inner_pre) * inv_root_two_pi
        grad_inner = (grad_active * (normal_cdf + inner_pre * density)).astype(jnp.bfloat16)
        grad_hidden_two = lax.psum(
            back_dot(grad_inner, w_inner).astype(jnp.bfloat16), "tensor"
        ).astype(jnp.float32)
        grad_middle = grad_top.astype(jnp.float32) + norm_backward(
            grad_hidden_two, gain_two, normed_two, scaled_two
        )
        grad_attn = grad_middle.astype(jnp.bfloat16)
        grad_mixed = back_dot(grad_attn, w_out).astype(jnp.bfloat16)
        keyset_back = fetch_blocks(packed, routing, BS)
        grad_query, kv_grads = attend_backward(
            query_low, keyset_back, key_valid, log_total, grad_mixed
        )
        grad_query = grad_query.astype(jnp.bfloat16)
        grad_packed = return_blocks(kv_grads, routing, BS)
        local_width = query_low.shape[2]
        grad_key = grad_packed[:, :, :local_width].astype(jnp.bfloat16)
        grad_value = grad_packed[:, :, local_width:].astype(jnp.bfloat16)
        grad_partial = (
            back_dot(grad_query, w_query)
            + back_dot(grad_key, w_key)
            + back_dot(grad_value, w_value)
        )
        grad_hidden_one = lax.psum(grad_partial.astype(jnp.bfloat16), "tensor").astype(jnp.float32)
        grad_tokens_now = grad_middle + norm_backward(
            grad_hidden_one, gain_one, normed_one, scaled_one
        )
        input_grads.append(grad_tokens_now.astype(jnp.bfloat16))
        batch_grads = (
            jnp.sum(grad_hidden_one * normed_one, axis=(0, 1)),
            jnp.sum(grad_hidden_one, axis=(0, 1)),
            outer_sum(hidden_low, grad_query),
            column_sum(grad_query),
            outer_sum(hidden_low, grad_key),
            outer_sum(hidden_low, grad_value),
            column_sum(grad_value),
            outer_sum(mixed_low, grad_attn),
            column_sum(grad_attn),
            jnp.sum(grad_hidden_two * normed_two, axis=(0, 1)),
            jnp.sum(grad_hidden_two, axis=(0, 1)),
            outer_sum(hidden_two_low, grad_inner),
            column_sum(grad_inner),
            outer_sum(active, grad_top),
            column_sum(grad_top),
        )
        totals = batch_grads if totals is None else jax.tree.map(jnp.add, totals, batch_grads)
    final_share = share_sum(flatten_all(totals))
    gathered = lax.all_gather(
        final_share.astype(jnp.bfloat16), ("dp", "seq"), axis=0, tiled=True
    ).astype(final_share.dtype)
    param_shapes = [
        member.shape
        for member in (
            ln1_gain,
            ln1_bias,
            w_query,
            b_query,
            w_key,
            w_value,
            b_value,
            w_out,
            b_out,
            ln2_gain,
            ln2_bias,
            w_inner,
            b_inner,
            w_outer,
            b_outer,
        )
    ]
    results = []
    cursor = 0
    for shape_now in param_shapes:
        length = 1
        for extent in shape_now:
            length = length * extent
        results.append(gathered[cursor : cursor + length].reshape(shape_now))
        cursor = cursor + length
    out_all = jnp.concatenate(outputs, axis=0)
    grad_all = jnp.concatenate(input_grads, axis=0)
    return (
        out_all,
        grad_all,
        results[0],
        results[1],
        results[2],
        results[3],
        results[4],
        results[5],
        results[6],
        results[7],
        results[8],
        results[9],
        results[10],
        results[11],
        results[12],
        results[13],
        results[14],
    )


def power_of_two(number):
    return number & (number - 1) == 0


def body(tokens, *rest):
    dp, seq, tensor = (lax.axis_size(axis) for axis in ("dp", "seq", "tensor"))
    fits = seq == tokens.shape[0] and tensor == 2 and dp == 4 and power_of_two(seq)
    return (window_body if fits else spread_body)(tokens, *rest)


def solution(mesh):
    in_specs = (
        P("dp", "seq", None),
        P("dp", "seq", None),
        P("dp", None),
        P("dp", None, None),
        P(),
        P(),
        P(None, "tensor"),
        P("tensor"),
        P(None, "tensor"),
        P(None, "tensor"),
        P("tensor"),
        P("tensor", None),
        P(),
        P(),
        P(),
        P(None, "tensor"),
        P("tensor"),
        P("tensor", None),
        P(),
    )
    out_specs = (
        P("dp", "seq", None),
        P("dp", "seq", None),
        P(),
        P(),
        P(None, "tensor"),
        P("tensor"),
        P(None, "tensor"),
        P(None, "tensor"),
        P("tensor"),
        P("tensor", None),
        P(),
        P(),
        P(),
        P(None, "tensor"),
        P("tensor"),
        P("tensor", None),
        P(),
    )
    return jax.shard_map(body, mesh=mesh, in_specs=in_specs, out_specs=out_specs, check_vma=False)
```
